256 devices in a mesh: layer: 8 (over z_lo, core), row: 32 (over x, y, z_hi).
Axes of the slice: x: 4, y: 4, z: 8 (z_hi: 2, z_lo: 4; z = z_hi * 4 + z_lo), core: 2. Of those that a mesh axis runs over, the one named last changes fastest.
Arguments:
- residual: float32 [2, 2, 64, 2048, 192], P(None, None, 'layer', 'row'), may hold values from -6 to 6
- wavenumber: float32 [64, 2048, 192], P('layer', 'row'), may hold values from 0.25 to 1.5
- inverse: bfloat16 [2, 8, 6144, 6144], P(None, 'layer', 'row'), may hold values from -3 to 3
Outputs:
- preconditioned: float32 [2, 2, 64, 2048, 192], P(None, None, 'layer', 'row')
The draws below stay inside these ranges and needn't reach their ends.
All inputs are finite; a program needn't handle non-finite values.
Results may differ from the reference program's by a relative error of at most 0.003.
Values may be sent and summed in bfloat16 or wider, within the bound.
No kernel may reach another device: no remote copies, remote signals or barrier semaphores. Data moves between devices by JAX's collectives and lax.ppermute only.
A program may use at most 64 MiB of HBM per device.

```python
import math
import jax
import jax.numpy as jnp
from jax import lax

SHOTS = 2
CZ = 8
NX = 192
QY = 16
PX = 4
SWEEPS = 4
LAYERS = 8
NZ = 64
NY = 2048
ORDER = 6144
N_LAYER = 8


def draw_inverse(key, part):
    diagonal_key, spread_key = jax.random.split(jax.random.fold_in(key, 17))
    spread = jax.random.normal(spread_key, (2, LAYERS, ORDER, ORDER), jnp.float32) * (0.35 / math.sqrt(ORDER))
    diagonal = jnp.exp(jax.random.uniform(diagonal_key, (LAYERS, ORDER), jnp.float32, math.log(1.5), math.log(2.5)))
    identity = jnp.eye(ORDER, dtype=jnp.float32)
    real_part = spread[0] + diagonal[:, :, None] * identity[None]
    return jnp.stack([real_part, spread[1]]).astype(jnp.bfloat16)


def levels(rng, extent, pieces, least, top_value):
    factor_of, own = 1.0, jax.random.fold_in(rng, 6)
    for axis_at, blocks in pieces:
        heights = jnp.exp(jax.random.uniform(jax.random.fold_in(own, axis_at), (blocks,), jnp.float32, least / len(pieces), top_value / len(pieces)))
        factor_of = factor_of * jnp.repeat(heights, extent[axis_at] // blocks).reshape([-1 if axis == axis_at else 1 for axis in range(len(extent))])
    return factor_of


def centred(key, shape, scale, most, cuts=(), kind=jnp.bfloat16):
    entries = jax.random.normal(key, shape, jnp.float32) * scale
    if len(cuts) > 0:
        entries = levels(key, shape, cuts, -0.22, 0.18) * entries
    return jnp.clip(entries, min=-most, max=most).astype(kind)


def setup_inputs(seed: int = 0) -> dict:
    seeds = jax.random.split(jax.random.key(seed), 4)
    return {
        "residual": centred(seeds[0], (SHOTS, 2, NZ, NY, NX), 1.0, 6.0, ((2, 8), (3, 32)), jnp.float32),
        "wavenumber": jnp.clip(jnp.exp(math.log(1.5) - 1.7917595 * jax.random.uniform(seeds[1], (NZ, NY, NX), jnp.float32) ** levels(seeds[1], (NZ, NY, NX), ((0, 8), (1, 32)), -0.2, 0.2)), 0.25, 1.5),
        "inverse": draw_inverse(jax.random.fold_in(seeds[3], 71), 0),
    }


damping = 0.8
absorb = 0.5
coupling = 0.45


def diagonal_parts(wavenumber):
    real_part = 6.0 - wavenumber
    imag_part = -absorb * wavenumber
    modulus = real_part * real_part + imag_part * imag_part
    return real_part, imag_part, real_part / modulus, -imag_part / modulus


def first_sweep(source, reciprocal_re, reciprocal_im):
    update_re = reciprocal_re * source[:, 0] - reciprocal_im * source[:, 1]
    update_im = reciprocal_re * source[:, 1] + reciprocal_im * source[:, 0]
    return damping * jnp.stack([update_re, update_im], axis=1)


def relax(extended, source, diagonal_re, diagonal_im, reciprocal_re, reciprocal_im):
    centre = extended[:, :, 1:-1, 1:-1, :]
    beside = extended[:, :, 2:, 1:-1, :] + extended[:, :, :-2, 1:-1, :]
    beside = beside + extended[:, :, 1:-1, 2:, :] + extended[:, :, 1:-1, :-2, :]
    padded = jnp.pad(centre, ((0, 0), (0, 0), (0, 0), (0, 0), (1, 1)))
    beside = beside + padded[..., 2:] + padded[..., :-2]
    applied_re = diagonal_re * centre[:, 0] - diagonal_im * centre[:, 1] - beside[:, 0]
    applied_im = diagonal_re * centre[:, 1] + diagonal_im * centre[:, 0] - beside[:, 1]
    remain_re = source[:, 0] - applied_re
    remain_im = source[:, 1] - applied_im
    update_re = reciprocal_re * remain_re - reciprocal_im * remain_im
    update_im = reciprocal_re * remain_im + reciprocal_im * remain_re
    return centre + damping * jnp.stack([update_re, update_im], axis=1)


def reference(residual, wavenumber, inverse):
    diagonal_re, diagonal_im, reciprocal_re, reciprocal_im = diagonal_parts(wavenumber)
    coarse_rhs = residual.reshape(SHOTS, 2, N_LAYER, CZ, NY // QY, QY, NX // PX, PX).mean(axis=(3, 5, 7))
    coarse_rhs = coarse_rhs.reshape(SHOTS, 2, N_LAYER, ORDER).transpose(2, 1, 0, 3)

    def layer_step(previous, item):
        matrices, right_side = item
        vector = (right_side + coupling * previous).astype(jnp.bfloat16)
        columns = vector.reshape(2 * SHOTS, ORDER).T
        product_re = jnp.dot(matrices[0], columns, preferred_element_type=jnp.float32).T.reshape(2, SHOTS, ORDER)
        product_im = jnp.dot(matrices[1], columns, preferred_element_type=jnp.float32).T.reshape(2, SHOTS, ORDER)
        solved = jnp.stack([product_re[0] - product_im[1], product_re[1] + product_im[0]])
        return solved, solved

    start_state = jnp.zeros((2, SHOTS, ORDER), jnp.float32)
    _, coarse_all = lax.scan(layer_step, start_state, (jnp.moveaxis(inverse, 1, 0), coarse_rhs))
    coarse_shots = coarse_all.reshape(N_LAYER, 2, SHOTS, NY // QY, NX // PX).transpose(2, 1, 0, 3, 4)

    def smooth_one(pair):
        shot_field, shot_coarse = pair
        source = shot_field[None]
        iterate = first_sweep(source, reciprocal_re, reciprocal_im)
        for counter in range(SWEEPS - 1):
            extended = jnp.pad(iterate, ((0, 0), (0, 0), (1, 1), (1, 1), (0, 0)))
            iterate = relax(extended, source, diagonal_re, diagonal_im, reciprocal_re, reciprocal_im)
        lifted = jnp.broadcast_to(shot_coarse[:, :, None, :, None, :, None], (2, N_LAYER, CZ, NY // QY, QY, NX // PX, PX))
        lifted = lifted.reshape(2, N_LAYER * CZ, NY, NX)
        return iterate[0] + lifted

    return lax.map(smooth_one, (residual, coarse_shots))
```

```python
import functools

import jax
import jax.numpy as jnp
from jax import lax
from jax.experimental import pallas as pl
from jax.experimental.pallas import tpu as pltpu
from jax.sharding import PartitionSpec as P

QY = 16
PX = 4
SWEEPS = 4
HALO = SWEEPS - 1
ROWS = 8
LANES = 256

damping = 0.8
absorb = 0.5
coupling = 0.45

VMEM = pltpu.VMEM
f32 = jnp.float32
bf16 = jnp.bfloat16


def limit(mebibytes):
    return pltpu.CompilerParams(vmem_limit_bytes=mebibytes << 20)


def membership(fine, coarse):
    row = lax.broadcasted_iota(jnp.int32, (fine, coarse), 0)
    col = lax.broadcasted_iota(jnp.int32, (fine, coarse), 1)
    return jnp.where((row >= col * PX) & (row < col * PX + PX), 1.0, 0.0).astype(bf16)


def exact_dot(values, selection, contract):
    first = values.astype(bf16)
    rest = values - first.astype(f32)
    second = rest.astype(bf16)
    third = (rest - second.astype(f32)).astype(bf16)
    total = None
    for piece in (third, second, first):
        part = lax.dot_general(piece, selection, (((1,), (contract,)), ((), ())), preferred_element_type=f32)
        total = part if total is None else total + part
    return total


def restrict_kernel(residual, rhs, spread):
    shots, _, depth, height, width = residual.shape
    strips, across = height // QY, width // PX
    sums = []
    for strip in range(strips):
        for part in range(2):
            for shot in range(shots):
                total = residual[shot, part, 0, strip * QY : (strip + 1) * QY, :]
                for plane in range(1, depth):
                    total = total + residual[shot, part, plane, strip * QY : (strip + 1) * QY, :]
                sums.append(jnp.sum(total, axis=0, keepdims=True))
    means = exact_dot(jnp.concatenate(sums, axis=0), membership(width, across), 0) * (1.0 / (depth * QY * PX))
    lines = 2 * shots
    for strip in range(strips):
        rhs[:, strip * across : (strip + 1) * across] = means[strip * lines : (strip + 1) * lines, :]
    vector = rhs[...].astype(bf16)
    for device in range(spread.shape[0]):
        spread[device] = vector


def restrict(residual, devices):
    shots, _, _, height, width = residual.shape
    cells = (height // QY) * (width // PX)
    return pl.pallas_call(
        restrict_kernel,
        out_shape=(
            jax.ShapeDtypeStruct((2 * shots, cells), f32),
            jax.ShapeDtypeStruct((devices, 2 * shots, cells), bf16),
        ),
        compiler_params=limit(8),
        name="restrict",
    )(residual)


def layer_kernel(step, here, matrix, gathered, next_rhs, kept_before, kept, spread, held, vector, arrived):
    devices, lines, cells = gathered.shape
    shots = lines // 2
    pieces = arrived.shape[0]
    across = matrix.shape[2] // pieces
    columns = [slice(piece * across, (piece + 1) * across) for piece in range(pieces)]
    copies = [
        pltpu.make_async_copy(matrix.at[:, :, columns[piece]], held.at[:, :, columns[piece]], arrived.at[piece])
        for piece in range(pieces)
    ]
    for copy in copies:
        copy.start()
    for device in range(devices):
        vector[:, device * cells : (device + 1) * cells] = gathered[device]
    by_re = by_im = None
    for piece in range(pieces):
        part = vector[:, columns[piece]]
        copies[piece].wait()
        products = [
            lax.dot_general(part, held[side, :, columns[piece]], (((1,), (1,)), ((), ())), preferred_element_type=f32)
            for side in range(2)
        ]
        by_re = products[0] if by_re is None else by_re + products[0]
        by_im = products[1] if by_im is None else by_im + products[1]
    solved = jnp.concatenate([by_re[:shots] - by_im[shots:], by_re[shots:] + by_im[:shots]], axis=0)
    kept[...] = jnp.where(here[0] == step, solved, kept_before[...])
    out = (next_rhs[...] + coupling * solved).astype(bf16)
    for device in range(devices):
        spread[device] = out


def solve_layer(step, here, matrix, gathered, next_rhs, kept):
    devices, lines, cells = gathered.shape
    pieces = 6
    return pl.pallas_call(
        functools.partial(layer_kernel, step),
        out_shape=(
            jax.ShapeDtypeStruct((lines, cells), f32),
            jax.ShapeDtypeStruct((devices, lines, cells), bf16),
        ),
        in_specs=[pl.BlockSpec(memory_space=pltpu.SMEM), pl.BlockSpec(memory_space=pltpu.HBM)]
        + [pl.BlockSpec(memory_space=VMEM)] * 3,
        scratch_shapes=[
            pltpu.VMEM(matrix.shape, bf16),
            pltpu.VMEM((lines, devices * cells), bf16),
            pltpu.SemaphoreType.DMA((pieces,)),
        ],
        compiler_params=limit(8),
        cost_estimate=pl.CostEstimate(flops=4 * matrix.size, bytes_accessed=2 * matrix.size, transcendentals=0),
        name="solve_layer",
    )(here, matrix, gathered, next_rhs, kept)


def smooth_kernel(inside, residual, wavenumber, row_low, row_high, deep_low, deep_high, smoothed, gain, source, first, second):
    shots, _, depth, height, width = residual.shape
    top = ROWS
    start = top + ROWS
    total = height + 2 * ROWS
    planes = depth + 2 * HALO
    rest = LANES - width
    sides = (
        (0, HALO, deep_low, inside[0]),
        (HALO + depth, HALO, deep_high, inside[1]),
    )

    def gains(values, factor):
        real_part = 6.0 - values
        imag_part = -absorb * values
        scale = damping * factor / (real_part * real_part + imag_part * imag_part)
        return real_part * scale, -imag_part * scale

    def put_gain(plane, row, values, factor):
        real_part, imag_part = gains(values, factor)
        rows = values.shape[0]
        gain[0, plane, pl.ds(row, rows), 0:width] = real_part
        gain[1, plane, pl.ds(row, rows), 0:width] = imag_part

    blank = jnp.zeros((total, rest), f32)

    def clear(plane, _):
        for part in range(2):
            gain[part, plane, top : top + total, width:LANES] = blank
            source[part, plane, top : top + total, width:LANES] = blank
        return _

    lax.fori_loop(0, planes, clear, 0)

    def own_gain(plane, _):
        for row in range(0, height, 16):
            put_gain(HALO + plane, start + row, wavenumber[plane, row : row + 16, :], 1.0)
        put_gain(HALO + plane, top, row_low[2 * shots, plane].astype(f32), inside[2])
        put_gain(HALO + plane, start + height, row_high[2 * shots, plane].astype(f32), inside[3])
        return _

    lax.fori_loop(0, depth, own_gain, 0)
    for base, count, ghost, factor in sides:
        for plane in range(count):
            for row in range(0, total, 16):
                values = ghost[2 * shots, plane, row : row + 16, :].astype(f32)
                put_gain(base + plane, top + row, values, factor)
    for base, count, _, _ in sides:
        for plane in range(count):
            for part in range(2):
                low = gain[part, base + plane, top:start, :]
                gain[part, base + plane, top:start, :] = low * inside[2]
                high = gain[part, base + plane, start + height : start + height + ROWS, :]
                gain[part, base + plane, start + height : start + height + ROWS, :] = high * inside[3]

    def sweep(old, new, plane, row, rows, store):
        here = pl.ds(row, rows)
        terms = []
        for part in range(2):
            centre = old[part, plane, here, :]
            beside = old[part, plane - 1, here, :] + old[part, plane + 1, here, :]
            beside = beside + old[part, plane, pl.ds(row - 1, rows), :] + old[part, plane, pl.ds(row + 1, rows), :]
            beside = beside + pltpu.roll(centre, 1, 1) + pltpu.roll(centre, LANES - 1, 1)
            terms.append((centre, source[part, plane, here, :] + beside))
        (centre_re, sum_re), (centre_im, sum_im) = terms
        gain_re, gain_im = gain[0, plane, here, :], gain[1, plane, here, :]
        store(0, (1.0 - damping) * centre_re + (gain_re * sum_re - gain_im * sum_im))
        store(1, (1.0 - damping) * centre_im + (gain_re * sum_im + gain_im * sum_re))

    for shot in range(shots):

        def own_source(plane, _):
            for part in range(2):
                source[part, HALO + plane, start : start + height, 0:width] = residual[shot, part, plane]
                source[part, HALO + plane, top:start, 0:width] = row_low[2 * shot + part, plane].astype(f32)
                source[part, HALO + plane, start + height : start + height + ROWS, 0:width] = row_high[
                    2 * shot + part, plane
                ].astype(f32)
            return _

        lax.fori_loop(0, depth, own_source, 0)
        for base, count, ghost, _ in sides:
            for plane in range(count):
                for part in range(2):
                    source[part, base + plane, top : top + total, 0:width] = ghost[2 * shot + part, plane].astype(f32)

        def begin(plane, _):
            for row in range(top, top + total, 16):
                here = pl.ds(row, 16)
                gain_re, gain_im = gain[0, plane, here, :], gain[1, plane, here, :]
                source_re, source_im = source[0, plane, here, :], source[1, plane, here, :]
                first[0, plane, here, :] = gain_re * source_re - gain_im * source_im
                first[1, plane, here, :] = gain_re * source_im + gain_im * source_re
            return _

        lax.fori_loop(0, planes, begin, 0)
        old, new = first, second
        for counter in range(1, SWEEPS):
            last = counter == SWEEPS - 1

            def one_plane(plane, _, old=old, new=new, last=last, shot=shot):
                low, high = (start, start + height) if last else (top, top + total)
                for row in range(low, high, 16):

                    def store(part, value, row=row):
                        if last:
                            smoothed[shot, part, plane - HALO, row - start : row - start + 16, :] = value[:, :width]
                        else:
                            new[part, plane, pl.ds(row, 16), :] = value

                    sweep(old, new, plane, row, 16, store)
                return _

            lax.fori_loop(counter, planes - counter, one_plane, 0)
            old, new = new, old


def smooth(inside, residual, wavenumber, row_low, row_high, deep_low, deep_high):
    shots, _, depth, height, width = residual.shape
    scratch = pltpu.VMEM((2, depth + 2 * HALO, height + 4 * ROWS, LANES), f32)
    return pl.pallas_call(
        smooth_kernel,
        out_shape=jax.ShapeDtypeStruct(residual.shape, f32),
        in_specs=[pl.BlockSpec(memory_space=pltpu.SMEM)] + [pl.BlockSpec(memory_space=VMEM)] * 6,
        scratch_shapes=[scratch] * 4,
        cost_estimate=pl.CostEstimate(flops=300 * residual.size, bytes_accessed=12 * residual.size, transcendentals=0),
        compiler_params=limit(28),
        name="smooth",
    )(inside, residual, wavenumber, row_low, row_high, deep_low, deep_high)


def lift_kernel(smoothed, coarse, out):
    shots, _, depth, height, width = smoothed.shape
    strips, across = height // QY, width // PX
    pick = membership(width, across)
    lines = [coarse[:, strip * across : (strip + 1) * across] for strip in range(strips)]
    wide = exact_dot(jnp.concatenate(lines, axis=0), pick, 1)
    for part in range(2):
        for shot in range(shots):
            for strip in range(strips):
                at = strip * 2 * shots + part * shots + shot
                value = jnp.broadcast_to(wide[at : at + 1, :], (QY, width))
                rows = slice(strip * QY, (strip + 1) * QY)
                for plane in range(depth):
                    out[shot, part, plane, rows, :] = smoothed[shot, part, plane, rows, :] + value


def lift(smoothed, coarse):
    return pl.pallas_call(
        lift_kernel,
        out_shape=jax.ShapeDtypeStruct(smoothed.shape, f32),
        compiler_params=limit(8),
        name="lift",
    )(smoothed, coarse)


def both_ways(low_block, high_block, axis):
    size = lax.axis_size(axis)
    up = [(i, i + 1) for i in range(size - 1)]
    return lax.ppermute(high_block, axis, up), lax.ppermute(low_block, axis, [(b, a) for a, b in up])


def on_device(residual, wavenumber, inverse):
    shots, _, depth, height, width = residual.shape
    layers, devices = lax.axis_size("layer"), lax.axis_size("row")
    layer, row = lax.axis_index("layer"), lax.axis_index("row")
    here = jnp.reshape(layer, (1,)).astype(jnp.int32)
    inside = jnp.stack([layer > 0, layer < layers - 1, row > 0, row < devices - 1]).astype(f32)

    with jax.named_scope("restrict"):
        rhs, spread = restrict(residual, devices)
    matrix = pltpu.with_memory_space_constraint(inverse[:, 0], pltpu.HBM)

    with jax.named_scope("halo"):
        fields = jnp.concatenate([residual.reshape(2 * shots, depth, height, width), wavenumber[None]]).astype(bf16)
        row_low, row_high = both_ways(fields[:, :, :ROWS], fields[:, :, height - ROWS :], "row")

        def with_rows(planes):
            return jnp.concatenate([row_low[:, planes], fields[:, planes], row_high[:, planes]], axis=2)

        deep_low, deep_high = both_ways(
            with_rows(slice(0, HALO)), with_rows(slice(depth - HALO, depth)), "layer"
        )
        next_rhs = lax.ppermute(rhs, "layer", [(i + 1, i) for i in range(layers - 1)])
    with jax.named_scope("smooth"):
        smoothed = smooth(inside, residual, wavenumber, row_low, row_high, deep_low, deep_high)

    kept = rhs
    for step in range(layers):
        with jax.named_scope(f"chain_{step}"):
            gathered = lax.all_to_all(spread, "row", 0, 0, tiled=True)
            if step:
                gathered = lax.ppermute(gathered, "layer", hop(step - 1, layers))
            kept, spread = solve_layer(step, here, matrix, gathered, next_rhs, kept)
    with jax.named_scope("lift"):
        return lift(smoothed, kept)


def hop(source, layers):
    if source % 2 == 0:
        return [(i, i ^ 1) for i in range(layers)]
    pairs = [(i, i + 1) for i in range(1, layers - 1, 2)]
    return pairs + [(b, a) for a, b in pairs] + [(0, 0), (layers - 1, layers - 1)]


def solution(mesh):
    return jax.shard_map(
        on_device,
        mesh=mesh,
        in_specs=(
            P(None, None, "layer", "row", None),
            P("layer", "row", None),
            P(None, "layer", "row", None),
        ),
        out_specs=P(None, None, "layer", "row", None),
        check_vma=False,
    )
```

```python
import functools

import jax
import jax.numpy as jnp
from jax import lax
from jax.experimental import pallas as pl
from jax.experimental.pallas import tpu as pltpu
from jax.sharding import PartitionSpec as P


QY = 16
PX = 4
SWEEPS = 4
HALO = SWEEPS - 1
ROWS = 8
LANES = 256

damping = 0.8
absorb = 0.5
coupling = 0.45

VMEM = pltpu.VMEM
f32 = jnp.float32
bf16 = jnp.bfloat16


def limit(mebibytes):
    return pltpu.CompilerParams(vmem_limit_bytes=mebibytes << 20)


def membership(fine, coarse):
    row = lax.broadcasted_iota(jnp.int32, (fine, coarse), 0)
    col = lax.broadcasted_iota(jnp.int32, (fine, coarse), 1)
    return jnp.where((row >= col * PX) & (row < col * PX + PX), 1.0, 0.0).astype(bf16)


def exact_dot(values, selection, contract):
    first = values.astype(bf16)
    rest = values - first.astype(f32)
    second = rest.astype(bf16)
    third = (rest - second.astype(f32)).astype(bf16)
    total = None
    for piece in (third, second, first):
        part = lax.dot_general(piece, selection, (((1,), (contract,)), ((), ())), preferred_element_type=f32)
        total = part if total is None else total + part
    return total


def restrict_kernel(residual, rhs, spread):
    shots, _, depth, height, width = residual.shape
    strips, across = height // QY, width // PX
    sums = []
    for strip in range(strips):
        for part in range(2):
            for shot in range(shots):
                total = residual[shot, part, 0, strip * QY : (strip + 1) * QY, :]
                for plane in range(1, depth):
                    total = total + residual[shot, part, plane, strip * QY : (strip + 1) * QY, :]
                sums.append(jnp.sum(total, axis=0, keepdims=True))
    means = exact_dot(jnp.concatenate(sums, axis=0), membership(width, across), 0) * (1.0 / (depth * QY * PX))
    lines = 2 * shots
    for strip in range(strips):
        rhs[:, strip * across : (strip + 1) * across] = means[strip * lines : (strip + 1) * lines, :]
    vector = rhs[...].astype(bf16)
    for device in range(spread.shape[0]):
        spread[device] = vector


def restrict(residual, devices):
    shots, _, _, height, width = residual.shape
    cells = (height // QY) * (width // PX)
    return pl.pallas_call(
        restrict_kernel,
        out_shape=(
            jax.ShapeDtypeStruct((2 * shots, cells), f32),
            jax.ShapeDtypeStruct((devices, 2 * shots, cells), bf16),
        ),
        compiler_params=limit(8),
        name="restrict",
    )(residual)


def ordered(vector, same, other, first_end):
    columns, _, cells = same.shape
    for column in range(columns):
        own, far = same[column], other[column]
        at = 2 * column * cells
        vector[:, at : at + cells] = jnp.where(first_end, own, far)
        vector[:, at + cells : at + 2 * cells] = jnp.where(first_end, far, own)


def hand_on(step, place, by_re, by_im, next_rhs, kept_before, kept, spread):
    shots = by_re.shape[0] // 2
    solved = jnp.concatenate([by_re[:shots] - by_im[shots:], by_re[shots:] + by_im[:shots]], axis=0)
    kept[...] = jnp.where(place[0] == step, solved, kept_before[...])
    out = (next_rhs[...] + coupling * solved).astype(bf16)
    for column in range(spread.shape[0]):
        spread[column] = out


def times(part, rows):
    return lax.dot_general(part, rows, (((1,), (1,)), ((), ())), preferred_element_type=f32)


def first_kernel(place, matrix, gathered, next_rhs, kept_before, kept, spread, held, vector, arrived):
    devices, _, cells = gathered.shape
    pieces = arrived.shape[0]
    across = matrix.shape[2] // pieces
    columns = [slice(piece * across, (piece + 1) * across) for piece in range(pieces)]
    copies = [
        pltpu.make_async_copy(matrix.at[:, :, columns[piece]], held.at[:, :, columns[piece]], arrived.at[piece])
        for piece in range(pieces)
    ]
    for copy in copies:
        copy.start()
    for device in range(devices):
        vector[:, device * cells : (device + 1) * cells] = gathered[device]
    by = [None, None]
    for piece in range(pieces):
        part = vector[:, columns[piece]]
        copies[piece].wait()
        for side in range(2):
            product = times(part, held[side, :, columns[piece]])
            by[side] = product if by[side] is None else by[side] + product
    hand_on(0, place, by[0], by[1], next_rhs, kept_before, kept, spread)


def solve_first(place, matrix, gathered, next_rhs, kept):
    devices, lines, cells = gathered.shape
    pieces = 6
    return pl.pallas_call(
        first_kernel,
        out_shape=(
            jax.ShapeDtypeStruct((lines, cells), f32),
            jax.ShapeDtypeStruct((devices // 2, lines, cells), bf16),
            pltpu.VMEM(matrix.shape, bf16),
        ),
        in_specs=[pl.BlockSpec(memory_space=pltpu.SMEM), pl.BlockSpec(memory_space=pltpu.HBM)]
        + [pl.BlockSpec(memory_space=VMEM)] * 3,
        out_specs=[pl.BlockSpec(memory_space=VMEM)] * 3,
        scratch_shapes=[pltpu.VMEM((lines, devices * cells), bf16), pltpu.SemaphoreType.DMA((pieces,))],
        compiler_params=limit(3),
        cost_estimate=pl.CostEstimate(flops=4 * matrix.size, bytes_accessed=2 * matrix.size, transcendentals=0),
        name="solve_first",
    )(place, matrix, gathered, next_rhs, kept)


def layer_kernel(step, place, matrix, same, other, next_rhs, kept_before, kept, spread, vector):
    ordered(vector, same, other, place[1] == 0)
    full = vector[...]
    hand_on(step, place, times(full, matrix[0]), times(full, matrix[1]), next_rhs, kept_before, kept, spread)


def solve_layer(step, place, matrix, same, other, next_rhs, kept):
    columns, lines, cells = same.shape
    return pl.pallas_call(
        functools.partial(layer_kernel, step),
        out_shape=(
            jax.ShapeDtypeStruct((lines, cells), f32),
            jax.ShapeDtypeStruct((columns, lines, cells), bf16),
        ),
        in_specs=[pl.BlockSpec(memory_space=pltpu.SMEM)] + [pl.BlockSpec(memory_space=VMEM)] * 5,
        scratch_shapes=[pltpu.VMEM((lines, 2 * columns * cells), bf16)],
        compiler_params=limit(3),
        cost_estimate=pl.CostEstimate(flops=4 * matrix.size, bytes_accessed=2 * matrix.size, transcendentals=0),
        name="solve_layer",
    )(place, matrix, same, other, next_rhs, kept)


def smooth_kernel(inside, residual, wavenumber, row_low, row_high, deep_low, deep_high, smoothed, gain, source, first, second):
    shots, _, depth, height, width = residual.shape
    top = ROWS
    start = top + ROWS
    total = height + 2 * ROWS
    planes = depth + 2 * HALO
    rest = LANES - width
    sides = (
        (0, HALO, deep_low, inside[0]),
        (HALO + depth, HALO, deep_high, inside[1]),
    )

    def gains(values, factor):
        real_part = 6.0 - values
        imag_part = -absorb * values
        scale = damping * factor / (real_part * real_part + imag_part * imag_part)
        return real_part * scale, -imag_part * scale

    def put_gain(plane, row, values, factor):
        real_part, imag_part = gains(values, factor)
        rows = values.shape[0]
        gain[0, plane, pl.ds(row, rows), 0:width] = real_part
        gain[1, plane, pl.ds(row, rows), 0:width] = imag_part

    blank = jnp.zeros((total, rest), f32)

    def clear(plane, _):
        for part in range(2):
            gain[part, plane, top : top + total, width:LANES] = blank
            source[part, plane, top : top + total, width:LANES] = blank
        return _

    lax.fori_loop(0, planes, clear, 0)

    def own_gain(plane, _):
        for row in range(0, height, 16):
            put_gain(HALO + plane, start + row, wavenumber[plane, row : row + 16, :], 1.0)
        return _

    lax.fori_loop(0, depth, own_gain, 0)
    for base, count, ghost, factor in sides:
        for plane in range(count):
            for row in range(0, height, 16):
                put_gain(base + plane, start + row, ghost[2 * shots, plane, row : row + 16, :].astype(f32), factor)
    for base, count, factor in ((0, HALO, inside[0]), (HALO, depth, 1.0), (HALO + depth, HALO, inside[1])):

        def row_gain(plane, _, factor=factor):
            put_gain(plane, top, row_low[2 * shots, plane].astype(f32), factor * inside[2])
            put_gain(plane, start + height, row_high[2 * shots, plane].astype(f32), factor * inside[3])
            return _

        lax.fori_loop(base, base + count, row_gain, 0)

    def sweep(old, plane, row, rows, store):
        here = pl.ds(row, rows)
        terms = []
        for part in range(2):
            centre = old[part, plane, here, :]
            beside = old[part, plane - 1, here, :] + old[part, plane + 1, here, :]
            beside = beside + old[part, plane, pl.ds(row - 1, rows), :] + old[part, plane, pl.ds(row + 1, rows), :]
            beside = beside + pltpu.roll(centre, 1, 1) + pltpu.roll(centre, LANES - 1, 1)
            terms.append((centre, source[part, plane, here, :] + beside))
        (centre_re, sum_re), (centre_im, sum_im) = terms
        gain_re, gain_im = gain[0, plane, here, :], gain[1, plane, here, :]
        store(0, (1.0 - damping) * centre_re + (gain_re * sum_re - gain_im * sum_im))
        store(1, (1.0 - damping) * centre_im + (gain_re * sum_im + gain_im * sum_re))

    for shot in range(shots):

        def own_source(plane, _):
            for part in range(2):
                source[part, HALO + plane, start : start + height, 0:width] = residual[shot, part, plane]
            return _

        def row_source(plane, _):
            for part in range(2):
                source[part, plane, top:start, 0:width] = row_low[2 * shot + part, plane].astype(f32)
                source[part, plane, start + height : start + height + ROWS, 0:width] = row_high[
                    2 * shot + part, plane
                ].astype(f32)
            return _

        lax.fori_loop(0, depth, own_source, 0)
        lax.fori_loop(0, planes, row_source, 0)
        for base, count, ghost, _ in sides:
            for plane in range(count):
                for part in range(2):
                    source[part, base + plane, start : start + height, 0:width] = ghost[2 * shot + part, plane].astype(f32)

        def begin(plane, _):
            for row in range(top, top + total, 16):
                here = pl.ds(row, 16)
                gain_re, gain_im = gain[0, plane, here, :], gain[1, plane, here, :]
                source_re, source_im = source[0, plane, here, :], source[1, plane, here, :]
                first[0, plane, here, :] = gain_re * source_re - gain_im * source_im
                first[1, plane, here, :] = gain_re * source_im + gain_im * source_re
            return _

        lax.fori_loop(0, planes, begin, 0)
        old, new = first, second
        for counter in range(1, SWEEPS):
            last = counter == SWEEPS - 1

            def one_plane(plane, _, old=old, new=new, last=last, shot=shot):
                low, high = (start, start + height) if last else (top, top + total)
                for row in range(low, high, 16):

                    def store(part, value, row=row):
                        if last:
                            smoothed[shot, part, plane - HALO, row - start : row - start + 16, :] = value[:, :width]
                        else:
                            new[part, plane, pl.ds(row, 16), :] = value

                    sweep(old, plane, row, 16, store)
                return _

            lax.fori_loop(counter, planes - counter, one_plane, 0)
            old, new = new, old


def smooth(inside, residual, wavenumber, row_low, row_high, deep_low, deep_high):
    shots, _, depth, height, width = residual.shape
    scratch = pltpu.VMEM((2, depth + 2 * HALO, height + 4 * ROWS, LANES), f32)
    return pl.pallas_call(
        smooth_kernel,
        out_shape=jax.ShapeDtypeStruct(residual.shape, f32),
        in_specs=[pl.BlockSpec(memory_space=pltpu.SMEM)] + [pl.BlockSpec(memory_space=VMEM)] * 6,
        scratch_shapes=[scratch] * 4,
        cost_estimate=pl.CostEstimate(flops=300 * residual.size, bytes_accessed=12 * residual.size, transcendentals=0),
        compiler_params=limit(28),
        name="smooth",
    )(inside, residual, wavenumber, row_low, row_high, deep_low, deep_high)


def lift_kernel(smoothed, coarse, out):
    shots, _, depth, height, width = smoothed.shape
    strips, across = height // QY, width // PX
    pick = membership(width, across)
    lines = [coarse[:, strip * across : (strip + 1) * across] for strip in range(strips)]
    wide = exact_dot(jnp.concatenate(lines, axis=0), pick, 1)
    for part in range(2):
        for shot in range(shots):
            for strip in range(strips):
                at = strip * 2 * shots + part * shots + shot
                value = jnp.broadcast_to(wide[at : at + 1, :], (QY, width))
                rows = slice(strip * QY, (strip + 1) * QY)
                for plane in range(depth):
                    out[shot, part, plane, rows, :] = smoothed[shot, part, plane, rows, :] + value


def lift(smoothed, coarse):
    return pl.pallas_call(
        lift_kernel,
        out_shape=jax.ShapeDtypeStruct(smoothed.shape, f32),
        compiler_params=limit(8),
        name="lift",
    )(smoothed, coarse)


def pack_planes_kernel(residual, wavenumber, first, last):
    shots, _, depth, height, width = residual.shape
    for out, base in ((first, 0), (last, depth - HALO)):
        for plane in range(HALO):
            for shot in range(shots):
                for part in range(2):
                    out[2 * shot + part, plane] = residual[shot, part, base + plane].astype(bf16)
            out[2 * shots, plane] = wavenumber[base + plane].astype(bf16)


def pack_planes(residual, wavenumber):
    shots, _, _, height, width = residual.shape
    shape = jax.ShapeDtypeStruct((2 * shots + 1, HALO, height, width), bf16)
    return pl.pallas_call(
        pack_planes_kernel, out_shape=(shape, shape), compiler_params=limit(10), name="pack_planes"
    )(residual, wavenumber)


def pack_rows_kernel(residual, wavenumber, below, above, first, last):
    shots, _, depth, height, width = residual.shape
    for out, base in ((first, 0), (last, height - ROWS)):
        rows = slice(base, base + ROWS)
        for field in range(2 * shots + 1):
            for plane in range(HALO):
                out[field, plane] = below[field, plane, rows, :]
                out[field, HALO + depth + plane] = above[field, plane, rows, :]
            for plane in range(depth):
                own = wavenumber[plane, rows, :] if field == 2 * shots else residual[field // 2, field % 2, plane, rows, :]
                out[field, HALO + plane] = own.astype(bf16)


def pack_rows(residual, wavenumber, below, above):
    shots, _, depth, _, width = residual.shape
    shape = jax.ShapeDtypeStruct((2 * shots + 1, depth + 2 * HALO, ROWS, width), bf16)
    return pl.pallas_call(
        pack_rows_kernel, out_shape=(shape, shape), compiler_params=limit(10), name="pack_rows"
    )(residual, wavenumber, below, above)


def both_ways(low_block, high_block, axis):
    size = lax.axis_size(axis)
    up = [(i, i + 1) for i in range(size - 1)]
    return lax.ppermute(high_block, axis, up), lax.ppermute(low_block, axis, [(b, a) for a, b in up])


def every_layer(residual, wavenumber, inverse):
    layers, devices = lax.axis_size("layer"), lax.axis_size("row")
    layer, row = lax.axis_index("layer"), lax.axis_index("row")
    place = jnp.stack([layer, row & 1]).astype(jnp.int32)
    inside = jnp.stack([layer > 0, layer < layers - 1, row > 0, row < devices - 1]).astype(f32)

    rhs, spread = restrict(residual, devices)
    next_rhs = lax.ppermute(rhs, "layer", [(i + 1, i) for i in range(layers - 1)])
    matrix = pltpu.with_memory_space_constraint(inverse[:, 0], pltpu.HBM)
    gathered = lax.all_to_all(spread, "row", 0, 0, tiled=True)
    kept, spread, matrix = solve_first(place, matrix, gathered, next_rhs, rhs)

    ends = [[2 * column + end for column in range(devices // 2)] for end in range(2)]
    for step in range(1, layers):
        half = lax.all_to_all(spread, "row", 0, 0, axis_index_groups=ends, tiled=True)
        ways = [
            [((step - 1) * devices + i, step * devices + (i ^ flip)) for i in range(devices)] for flip in range(2)
        ]
        other = lax.ppermute(half, ("layer", "row"), ways[1])
        same = lax.ppermute(half, ("layer", "row"), ways[0])
        kept, spread = solve_layer(step, place, matrix, same, other, next_rhs, kept)

    first, last = pack_planes(residual, wavenumber)
    below, above = both_ways(first, last, "layer")
    first, last = pack_rows(residual, wavenumber, below, above)
    row_low, row_high = both_ways(first, last, "row")
    smoothed = smooth(inside, residual, wavenumber, row_low, row_high, below, above)
    return lift(smoothed, kept)


def solution(mesh):
    return jax.shard_map(
        every_layer,
        mesh=mesh,
        in_specs=(
            P(None, None, "layer", "row", None),
            P("layer", "row", None),
            P(None, "layer", "row", None),
        ),
        out_specs=P(None, None, "layer", "row", None),
        check_vma=False,
    )
```

```python
import functools

import jax
import jax.numpy as jnp
from jax import lax
from jax.experimental import pallas as pl
from jax.experimental.pallas import tpu as pltpu
from jax.sharding import PartitionSpec as P


QY = 16
PX = 4
SWEEPS = 4
HALO = SWEEPS - 1
ROWS = 8
LANES = 256

damping = 0.8
absorb = 0.5
coupling = 0.45

VMEM = pltpu.VMEM
f32 = jnp.float32
bf16 = jnp.bfloat16


def limit(mebibytes):
    return pltpu.CompilerParams(vmem_limit_bytes=mebibytes << 20)


def membership(fine, coarse):
    row = lax.broadcasted_iota(jnp.int32, (fine, coarse), 0)
    col = lax.broadcasted_iota(jnp.int32, (fine, coarse), 1)
    return jnp.where((row >= col * PX) & (row < col * PX + PX), 1.0, 0.0).astype(bf16)


def exact_dot(values, selection, contract):
    first = values.astype(bf16)
    rest = values - first.astype(f32)
    second = rest.astype(bf16)
    third = (rest - second.astype(f32)).astype(bf16)
    total = None
    for piece in (third, second, first):
        part = lax.dot_general(piece, selection, (((1,), (contract,)), ((), ())), preferred_element_type=f32)
        total = part if total is None else total + part
    return total


def restrict_kernel(residual, rhs, spread):
    shots, _, depth, height, width = residual.shape
    strips, across = height // QY, width // PX
    sums = []
    for strip in range(strips):
        for part in range(2):
            for shot in range(shots):
                total = residual[shot, part, 0, strip * QY : (strip + 1) * QY, :]
                for plane in range(1, depth):
                    total = total + residual[shot, part, plane, strip * QY : (strip + 1) * QY, :]
                sums.append(jnp.sum(total, axis=0, keepdims=True))
    means = exact_dot(jnp.concatenate(sums, axis=0), membership(width, across), 0) * (1.0 / (depth * QY * PX))
    lines = 2 * shots
    for strip in range(strips):
        rhs[:, strip * across : (strip + 1) * across] = means[strip * lines : (strip + 1) * lines, :]
    vector = rhs[...].astype(bf16)
    for device in range(spread.shape[0]):
        spread[device] = vector


def restrict(residual, devices):
    shots, _, _, height, width = residual.shape
    cells = (height // QY) * (width // PX)
    return pl.pallas_call(
        restrict_kernel,
        out_shape=(
            jax.ShapeDtypeStruct((2 * shots, cells), f32),
            jax.ShapeDtypeStruct((devices, 2 * shots, cells), bf16),
        ),
        compiler_params=limit(8),
        name="restrict",
    )(residual)


def hold_kernel(step, place, matrix, held, arrived):
    @pl.when(place[0] == step)
    def _():
        copy = pltpu.make_async_copy(matrix, held, arrived)
        copy.start()
        copy.wait()


def hold(step, place, matrix):
    return pl.pallas_call(
        functools.partial(hold_kernel, step),
        out_shape=pltpu.VMEM(matrix.shape, matrix.dtype),
        in_specs=[pl.BlockSpec(memory_space=pltpu.SMEM), pl.BlockSpec(memory_space=pltpu.HBM)],
        out_specs=pl.BlockSpec(memory_space=VMEM),
        scratch_shapes=[pltpu.SemaphoreType.DMA],
        compiler_params=limit(1),
        name="hold",
    )(place, matrix)


def ordered(vector, same, other, first_end):
    columns, _, cells = same.shape
    for column in range(columns):
        own, far = same[column], other[column]
        at = 2 * column * cells
        vector[:, at : at + cells] = jnp.where(first_end, own, far)
        vector[:, at + cells : at + 2 * cells] = jnp.where(first_end, far, own)


def hand_on(by_re, by_im, next_rhs, kept, spread):
    shots = by_re.shape[0] // 2
    solved = jnp.concatenate([by_re[:shots] - by_im[shots:], by_re[shots:] + by_im[:shots]], axis=0)
    kept[...] = solved
    out = (next_rhs[...] + coupling * solved).astype(bf16)
    for column in range(spread.shape[0]):
        spread[column] = out


def times(part, rows):
    return lax.dot_general(part, rows, (((1,), (1,)), ((), ())), preferred_element_type=f32)


def first_kernel(matrix, gathered, next_rhs, kept, spread, held, vector, arrived):
    devices, _, cells = gathered.shape
    pieces = arrived.shape[0]
    across = matrix.shape[2] // pieces
    columns = [slice(piece * across, (piece + 1) * across) for piece in range(pieces)]
    copies = [
        pltpu.make_async_copy(matrix.at[:, :, columns[piece]], held.at[:, :, columns[piece]], arrived.at[piece])
        for piece in range(pieces)
    ]
    for copy in copies:
        copy.start()
    for device in range(devices):
        vector[:, device * cells : (device + 1) * cells] = gathered[device]
    by = [None, None]
    for piece in range(pieces):
        part = vector[:, columns[piece]]
        copies[piece].wait()
        for side in range(2):
            product = times(part, held[side, :, columns[piece]])
            by[side] = product if by[side] is None else by[side] + product
    hand_on(by[0], by[1], next_rhs, kept, spread)


def solve_first(matrix, gathered, next_rhs):
    devices, lines, cells = gathered.shape
    pieces = 6
    return pl.pallas_call(
        first_kernel,
        out_shape=(
            jax.ShapeDtypeStruct((lines, cells), f32),
            jax.ShapeDtypeStruct((devices // 2, lines, cells), bf16),
        ),
        in_specs=[pl.BlockSpec(memory_space=pltpu.HBM)] + [pl.BlockSpec(memory_space=VMEM)] * 2,
        scratch_shapes=[
            pltpu.VMEM(matrix.shape, bf16),
            pltpu.VMEM((lines, devices * cells), bf16),
            pltpu.SemaphoreType.DMA((pieces,)),
        ],
        compiler_params=limit(8),
        cost_estimate=pl.CostEstimate(flops=4 * matrix.size, bytes_accessed=2 * matrix.size, transcendentals=0),
        name="solve_first",
    )(matrix, gathered, next_rhs)


def layer_kernel(step, place, matrix, same, other, next_rhs, kept_before, kept, spread, vector):
    @pl.when(place[0] == step)
    def _():
        ordered(vector, same, other, place[1] == 0)
        full = vector[...]
        hand_on(times(full, matrix[0]), times(full, matrix[1]), next_rhs, kept, spread)

    @pl.when(place[0] != step)
    def _():
        kept[...] = kept_before[...]


def solve_layer(step, place, matrix, same, other, next_rhs, kept):
    columns, lines, cells = same.shape
    return pl.pallas_call(
        functools.partial(layer_kernel, step),
        out_shape=(
            jax.ShapeDtypeStruct((lines, cells), f32),
            jax.ShapeDtypeStruct((columns, lines, cells), bf16),
        ),
        in_specs=[pl.BlockSpec(memory_space=pltpu.SMEM)] + [pl.BlockSpec(memory_space=VMEM)] * 5,
        scratch_shapes=[pltpu.VMEM((lines, 2 * columns * cells), bf16)],
        compiler_params=limit(3),
        cost_estimate=pl.CostEstimate(flops=4 * matrix.size, bytes_accessed=2 * matrix.size, transcendentals=0),
        name="solve_layer",
    )(place, matrix, same, other, next_rhs, kept)


def smooth_kernel(inside, residual, wavenumber, row_low, row_high, deep_low, deep_high, smoothed, gain, source, first, second):
    shots, _, depth, height, width = residual.shape
    top = ROWS
    start = top + ROWS
    total = height + 2 * ROWS
    planes = depth + 2 * HALO
    rest = LANES - width
    sides = (
        (0, HALO, deep_low, inside[0]),
        (HALO + depth, HALO, deep_high, inside[1]),
    )

    def gains(values, factor):
        real_part = 6.0 - values
        imag_part = -absorb * values
        scale = damping * factor / (real_part * real_part + imag_part * imag_part)
        return real_part * scale, -imag_part * scale

    def put_gain(plane, row, values, factor):
        real_part, imag_part = gains(values, factor)
        rows = values.shape[0]
        gain[0, plane, pl.ds(row, rows), 0:width] = real_part
        gain[1, plane, pl.ds(row, rows), 0:width] = imag_part

    blank = jnp.zeros((total, rest), f32)

    def clear(plane, _):
        for part in range(2):
            gain[part, plane, top : top + total, width:LANES] = blank
            source[part, plane, top : top + total, width:LANES] = blank
        return _

    lax.fori_loop(0, planes, clear, 0)

    def own_gain(plane, _):
        for row in range(0, height, 16):
            put_gain(HALO + plane, start + row, wavenumber[plane, row : row + 16, :], 1.0)
        return _

    lax.fori_loop(0, depth, own_gain, 0)
    for base, count, ghost, factor in sides:
        for plane in range(count):
            for row in range(0, height, 16):
                put_gain(base + plane, start + row, ghost[2 * shots, plane, row : row + 16, :].astype(f32), factor)
    for base, count, factor in ((0, HALO, inside[0]), (HALO, depth, 1.0), (HALO + depth, HALO, inside[1])):

        def row_gain(plane, _, factor=factor):
            put_gain(plane, top, row_low[2 * shots, plane].astype(f32), factor * inside[2])
            put_gain(plane, start + height, row_high[2 * shots, plane].astype(f32), factor * inside[3])
            return _

        lax.fori_loop(base, base + count, row_gain, 0)

    def sweep(old, plane, row, rows, store):
        here = pl.ds(row, rows)
        terms = []
        for part in range(2):
            centre = old[part, plane, here, :]
            beside = old[part, plane - 1, here, :] + old[part, plane + 1, here, :]
            beside = beside + old[part, plane, pl.ds(row - 1, rows), :] + old[part, plane, pl.ds(row + 1, rows), :]
            beside = beside + pltpu.roll(centre, 1, 1) + pltpu.roll(centre, LANES - 1, 1)
            terms.append((centre, source[part, plane, here, :] + beside))
        (centre_re, sum_re), (centre_im, sum_im) = terms
        gain_re, gain_im = gain[0, plane, here, :], gain[1, plane, here, :]
        store(0, (1.0 - damping) * centre_re + (gain_re * sum_re - gain_im * sum_im))
        store(1, (1.0 - damping) * centre_im + (gain_re * sum_im + gain_im * sum_re))

    for shot in range(shots):

        def own_source(plane, _):
            for part in range(2):
                source[part, HALO + plane, start : start + height, 0:width] = residual[shot, part, plane]
            return _

        def row_source(plane, _):
            for part in range(2):
                source[part, plane, top:start, 0:width] = row_low[2 * shot + part, plane].astype(f32)
                source[part, plane, start + height : start + height + ROWS, 0:width] = row_high[
                    2 * shot + part, plane
                ].astype(f32)
            return _

        lax.fori_loop(0, depth, own_source, 0)
        lax.fori_loop(0, planes, row_source, 0)
        for base, count, ghost, _ in sides:
            for plane in range(count):
                for part in range(2):
                    source[part, base + plane, start : start + height, 0:width] = ghost[2 * shot + part, plane].astype(f32)

        def begin(plane, _):
            for row in range(top, top + total, 16):
                here = pl.ds(row, 16)
                gain_re, gain_im = gain[0, plane, here, :], gain[1, plane, here, :]
                source_re, source_im = source[0, plane, here, :], source[1, plane, here, :]
                first[0, plane, here, :] = gain_re * source_re - gain_im * source_im
                first[1, plane, here, :] = gain_re * source_im + gain_im * source_re
            return _

        lax.fori_loop(0, planes, begin, 0)
        old, new = first, second
        for counter in range(1, SWEEPS):
            last = counter == SWEEPS - 1

            def one_plane(plane, _, old=old, new=new, last=last, shot=shot):
                low, high = (start, start + height) if last else (top, top + total)
                for row in range(low, high, 16):

                    def store(part, value, row=row):
                        if last:
                            smoothed[shot, part, plane - HALO, row - start : row - start + 16, :] = value[:, :width]
                        else:
                            new[part, plane, pl.ds(row, 16), :] = value

                    sweep(old, plane, row, 16, store)
                return _

            lax.fori_loop(counter, planes - counter, one_plane, 0)
            old, new = new, old


def smooth(inside, residual, wavenumber, row_low, row_high, deep_low, deep_high):
    shots, _, depth, height, width = residual.shape
    scratch = pltpu.VMEM((2, depth + 2 * HALO, height + 4 * ROWS, LANES), f32)
    return pl.pallas_call(
        smooth_kernel,
        out_shape=jax.ShapeDtypeStruct(residual.shape, f32),
        in_specs=[pl.BlockSpec(memory_space=pltpu.SMEM)] + [pl.BlockSpec(memory_space=VMEM)] * 6,
        scratch_shapes=[scratch] * 4,
        cost_estimate=pl.CostEstimate(flops=300 * residual.size, bytes_accessed=12 * residual.size, transcendentals=0),
        compiler_params=limit(28),
        name="smooth",
    )(inside, residual, wavenumber, row_low, row_high, deep_low, deep_high)


def lift_kernel(smoothed, coarse, out):
    shots, _, depth, height, width = smoothed.shape
    strips, across = height // QY, width // PX
    pick = membership(width, across)
    lines = [coarse[:, strip * across : (strip + 1) * across] for strip in range(strips)]
    wide = exact_dot(jnp.concatenate(lines, axis=0), pick, 1)
    for part in range(2):
        for shot in range(shots):
            for strip in range(strips):
                at = strip * 2 * shots + part * shots + shot
                value = jnp.broadcast_to(wide[at : at + 1, :], (QY, width))
                rows = slice(strip * QY, (strip + 1) * QY)
                for plane in range(depth):
                    out[shot, part, plane, rows, :] = smoothed[shot, part, plane, rows, :] + value


def lift(smoothed, coarse):
    return pl.pallas_call(
        lift_kernel,
        out_shape=jax.ShapeDtypeStruct(smoothed.shape, f32),
        compiler_params=limit(8),
        name="lift",
    )(smoothed, coarse)


def pack_planes_kernel(residual, wavenumber, first, last):
    shots, _, depth, height, width = residual.shape
    for out, base in ((first, 0), (last, depth - HALO)):
        for plane in range(HALO):
            for shot in range(shots):
                for part in range(2):
                    out[2 * shot + part, plane] = residual[shot, part, base + plane].astype(bf16)
            out[2 * shots, plane] = wavenumber[base + plane].astype(bf16)


def pack_planes(residual, wavenumber):
    shots, _, _, height, width = residual.shape
    shape = jax.ShapeDtypeStruct((2 * shots + 1, HALO, height, width), bf16)
    return pl.pallas_call(
        pack_planes_kernel, out_shape=(shape, shape), compiler_params=limit(10), name="pack_planes"
    )(residual, wavenumber)


def pack_rows_kernel(residual, wavenumber, below, above, first, last):
    shots, _, depth, height, width = residual.shape
    for out, base in ((first, 0), (last, height - ROWS)):
        rows = slice(base, base + ROWS)
        for field in range(2 * shots + 1):
            for plane in range(HALO):
                out[field, plane] = below[field, plane, rows, :]
                out[field, HALO + depth + plane] = above[field, plane, rows, :]
            for plane in range(depth):
                own = wavenumber[plane, rows, :] if field == 2 * shots else residual[field // 2, field % 2, plane, rows, :]
                out[field, HALO + plane] = own.astype(bf16)


def pack_rows(residual, wavenumber, below, above):
    shots, _, depth, _, width = residual.shape
    shape = jax.ShapeDtypeStruct((2 * shots + 1, depth + 2 * HALO, ROWS, width), bf16)
    return pl.pallas_call(
        pack_rows_kernel, out_shape=(shape, shape), compiler_params=limit(10), name="pack_rows"
    )(residual, wavenumber, below, above)


def both_ways(low_block, high_block, axis):
    size = lax.axis_size(axis)
    up = [(i, i + 1) for i in range(size - 1)]
    return lax.ppermute(high_block, axis, up), lax.ppermute(low_block, axis, [(b, a) for a, b in up])


def every_layer(residual, wavenumber, inverse):
    layers, devices = lax.axis_size("layer"), lax.axis_size("row")
    layer, row = lax.axis_index("layer"), lax.axis_index("row")
    place = jnp.stack([layer, row & 1]).astype(jnp.int32)
    inside = jnp.stack([layer > 0, layer < layers - 1, row > 0, row < devices - 1]).astype(f32)

    rhs, spread = restrict(residual, devices)
    next_rhs = lax.ppermute(rhs, "layer", [(i + 1, i) for i in range(layers - 1)])
    matrix = pltpu.with_memory_space_constraint(inverse[:, 0], pltpu.HBM)
    gathered = lax.all_to_all(spread, "row", 0, 0, tiled=True)
    kept, spread = solve_first(matrix, gathered, next_rhs)

    ends = [[2 * column + end for column in range(devices // 2)] for end in range(2)]
    for step in range(1, layers):
        half = lax.cond(
            layer == step - 1,
            lambda blocks: lax.all_to_all(blocks, "row", 0, 0, axis_index_groups=ends, tiled=True),
            lambda blocks: blocks,
            spread,
        )
        ways = [
            [((step - 1) * devices + i, step * devices + (i ^ flip)) for i in range(devices)] for flip in range(2)
        ]
        other = lax.ppermute(half, ("layer", "row"), ways[1])
        same = lax.ppermute(half, ("layer", "row"), ways[0])
        held = hold(step, place, matrix)
        kept, spread = solve_layer(step, place, held, same, other, next_rhs, kept)

    first, last = pack_planes(residual, wavenumber)
    below, above = both_ways(first, last, "layer")
    first, last = pack_rows(residual, wavenumber, below, above)
    row_low, row_high = both_ways(first, last, "row")
    smoothed = smooth(inside, residual, wavenumber, row_low, row_high, below, above)
    return lift(smoothed, kept)


def solution(mesh):
    return jax.shard_map(
        every_layer,
        mesh=mesh,
        in_specs=(
            P(None, None, "layer", "row", None),
            P("layer", "row", None),
            P(None, "layer", "row", None),
        ),
        out_specs=P(None, None, "layer", "row", None),
        check_vma=False,
    )
```

```python
import functools

import jax
import jax.numpy as jnp
from jax import lax
from jax.experimental import pallas as pl
from jax.experimental.pallas import tpu as pltpu
from jax.sharding import PartitionSpec as P


QY = 16
PX = 4
SWEEPS = 4
HALO = SWEEPS - 1
ROWS = 8
LANES = 256

damping = 0.8
absorb = 0.5
coupling = 0.45

VMEM = pltpu.VMEM
f32 = jnp.float32
bf16 = jnp.bfloat16


def limit(mebibytes):
    return pltpu.CompilerParams(vmem_limit_bytes=mebibytes << 20)


def membership(fine, coarse):
    row = lax.broadcasted_iota(jnp.int32, (fine, coarse), 0)
    col = lax.broadcasted_iota(jnp.int32, (fine, coarse), 1)
    return jnp.where((row >= col * PX) & (row < col * PX + PX), 1.0, 0.0).astype(bf16)


def exact_dot(values, selection, contract):
    first = values.astype(bf16)
    rest = values - first.astype(f32)
    second = rest.astype(bf16)
    third = (rest - second.astype(f32)).astype(bf16)
    total = None
    for piece in (third, second, first):
        part = lax.dot_general(piece, selection, (((1,), (contract,)), ((), ())), preferred_element_type=f32)
        total = part if total is None else total + part
    return total


def restrict_kernel(residual, rhs, spread):
    shots, _, depth, height, width = residual.shape
    strips, across = height // QY, width // PX
    sums = []
    for strip in range(strips):
        for part in range(2):
            for shot in range(shots):
                total = residual[shot, part, 0, strip * QY : (strip + 1) * QY, :]
                for plane in range(1, depth):
                    total = total + residual[shot, part, plane, strip * QY : (strip + 1) * QY, :]
                sums.append(jnp.sum(total, axis=0, keepdims=True))
    means = exact_dot(jnp.concatenate(sums, axis=0), membership(width, across), 0) * (1.0 / (depth * QY * PX))
    lines = 2 * shots
    for strip in range(strips):
        rhs[:, strip * across : (strip + 1) * across] = means[strip * lines : (strip + 1) * lines, :]
    vector = rhs[...].astype(bf16)
    for device in range(spread.shape[0]):
        spread[device] = vector


def restrict(residual, devices):
    shots, _, _, height, width = residual.shape
    cells = (height // QY) * (width // PX)
    return pl.pallas_call(
        restrict_kernel,
        out_shape=(
            jax.ShapeDtypeStruct((2 * shots, cells), f32),
            jax.ShapeDtypeStruct((devices, 2 * shots, cells), bf16),
        ),
        compiler_params=limit(8),
        name="restrict",
    )(residual)


def hold_kernel(matrix, held, arrived):
    copy = pltpu.make_async_copy(matrix, held, arrived)
    copy.start()
    copy.wait()


def hold(matrix):
    return pl.pallas_call(
        hold_kernel,
        out_shape=pltpu.VMEM(matrix.shape, matrix.dtype),
        in_specs=[pl.BlockSpec(memory_space=pltpu.HBM)],
        out_specs=pl.BlockSpec(memory_space=VMEM),
        scratch_shapes=[pltpu.SemaphoreType.DMA],
        compiler_params=limit(1),
        name="hold",
    )(matrix)


def ordered(vector, same, other, first_end):
    columns, _, cells = same.shape
    for column in range(columns):
        own, far = same[column], other[column]
        at = 2 * column * cells
        vector[:, at : at + cells] = jnp.where(first_end, own, far)
        vector[:, at + cells : at + 2 * cells] = jnp.where(first_end, far, own)


def combined(by_re, by_im):
    shots = by_re.shape[0] // 2
    return jnp.concatenate([by_re[:shots] - by_im[shots:], by_re[shots:] + by_im[:shots]], axis=0)


def hand_on(solved, next_rhs, spread):
    out = (next_rhs[...] + coupling * solved).astype(bf16)
    for column in range(spread.shape[0]):
        spread[column] = out


def times(part, rows):
    return lax.dot_general(part, rows, (((1,), (1,)), ((), ())), preferred_element_type=f32)


def first_kernel(matrix, gathered, next_rhs, kept, spread, held, vector, arrived):
    devices, _, cells = gathered.shape
    pieces = arrived.shape[0]
    across = matrix.shape[2] // pieces
    columns = [slice(piece * across, (piece + 1) * across) for piece in range(pieces)]
    copies = [
        pltpu.make_async_copy(matrix.at[:, :, columns[piece]], held.at[:, :, columns[piece]], arrived.at[piece])
        for piece in range(pieces)
    ]
    for copy in copies:
        copy.start()
    for device in range(devices):
        vector[:, device * cells : (device + 1) * cells] = gathered[device]
    by = [None, None]
    for piece in range(pieces):
        part = vector[:, columns[piece]]
        copies[piece].wait()
        for side in range(2):
            product = times(part, held[side, :, columns[piece]])
            by[side] = product if by[side] is None else by[side] + product
    solved = combined(by[0], by[1])
    kept[...] = solved
    hand_on(solved, next_rhs, spread)


def solve_first(matrix, gathered, next_rhs):
    devices, lines, cells = gathered.shape
    pieces = 6
    return pl.pallas_call(
        first_kernel,
        out_shape=(
            jax.ShapeDtypeStruct((lines, cells), f32),
            jax.ShapeDtypeStruct((devices // 2, lines, cells), bf16),
        ),
        in_specs=[pl.BlockSpec(memory_space=pltpu.HBM)] + [pl.BlockSpec(memory_space=VMEM)] * 2,
        scratch_shapes=[
            pltpu.VMEM(matrix.shape, bf16),
            pltpu.VMEM((lines, devices * cells), bf16),
            pltpu.SemaphoreType.DMA((pieces,)),
        ],
        compiler_params=limit(8),
        cost_estimate=pl.CostEstimate(flops=4 * matrix.size, bytes_accessed=2 * matrix.size, transcendentals=0),
        name="solve_first",
    )(matrix, gathered, next_rhs)


def layer_kernel(step, matrix, same, other, next_rhs, kept_before, kept, spread, vector):
    ordered(vector, same, other, lax.axis_index("row") % 2 == 0)
    full = vector[...]
    solved = combined(times(full, matrix[0]), times(full, matrix[1]))
    kept[...] = jnp.where(lax.axis_index("layer") == step, solved, kept_before[...])
    hand_on(solved, next_rhs, spread)


def solve_layer(step, matrix, same, other, next_rhs, kept):
    columns, lines, cells = same.shape
    return pl.pallas_call(
        functools.partial(layer_kernel, step),
        out_shape=(
            jax.ShapeDtypeStruct((lines, cells), f32),
            jax.ShapeDtypeStruct((columns, lines, cells), bf16),
        ),
        in_specs=[pl.BlockSpec(memory_space=VMEM)] * 5,
        scratch_shapes=[pltpu.VMEM((lines, 2 * columns * cells), bf16)],
        compiler_params=limit(3),
        cost_estimate=pl.CostEstimate(flops=4 * matrix.size, bytes_accessed=2 * matrix.size, transcendentals=0),
        name="solve_layer",
    )(matrix, same, other, next_rhs, kept)


def smooth_kernel(inside, residual, wavenumber, row_low, row_high, deep_low, deep_high, smoothed, gain, source, first, second):
    shots, _, depth, height, width = residual.shape
    top = ROWS
    start = top + ROWS
    total = height + 2 * ROWS
    planes = depth + 2 * HALO
    rest = LANES - width
    sides = (
        (0, HALO, deep_low, inside[0]),
        (HALO + depth, HALO, deep_high, inside[1]),
    )

    def gains(values, factor):
        real_part = 6.0 - values
        imag_part = -absorb * values
        scale = damping * factor / (real_part * real_part + imag_part * imag_part)
        return real_part * scale, -imag_part * scale

    def put_gain(plane, row, values, factor):
        real_part, imag_part = gains(values, factor)
        rows = values.shape[0]
        gain[0, plane, pl.ds(row, rows), 0:width] = real_part
        gain[1, plane, pl.ds(row, rows), 0:width] = imag_part

    blank = jnp.zeros((total, rest), f32)

    def clear(plane, _):
        for part in range(2):
            gain[part, plane, top : top + total, width:LANES] = blank
            source[part, plane, top : top + total, width:LANES] = blank
        return _

    lax.fori_loop(0, planes, clear, 0)

    def own_gain(plane, _):
        for row in range(0, height, 16):
            put_gain(HALO + plane, start + row, wavenumber[plane, row : row + 16, :], 1.0)
        return _

    lax.fori_loop(0, depth, own_gain, 0)
    for base, count, ghost, factor in sides:
        for plane in range(count):
            for row in range(0, height, 16):
                put_gain(base + plane, start + row, ghost[2 * shots, plane, row : row + 16, :].astype(f32), factor)
    for base, count, factor in ((0, HALO, inside[0]), (HALO, depth, 1.0), (HALO + depth, HALO, inside[1])):

        def row_gain(plane, _, factor=factor):
            put_gain(plane, top, row_low[2 * shots, plane].astype(f32), factor * inside[2])
            put_gain(plane, start + height, row_high[2 * shots, plane].astype(f32), factor * inside[3])
            return _

        lax.fori_loop(base, base + count, row_gain, 0)

    def sweep(old, plane, row, rows, store):
        here = pl.ds(row, rows)
        terms = []
        for part in range(2):
            centre = old[part, plane, here, :]
            beside = old[part, plane - 1, here, :] + old[part, plane + 1, here, :]
            beside = beside + old[part, plane, pl.ds(row - 1, rows), :] + old[part, plane, pl.ds(row + 1, rows), :]
            beside = beside + pltpu.roll(centre, 1, 1) + pltpu.roll(centre, LANES - 1, 1)
            terms.append((centre, source[part, plane, here, :] + beside))
        (centre_re, sum_re), (centre_im, sum_im) = terms
        gain_re, gain_im = gain[0, plane, here, :], gain[1, plane, here, :]
        store(0, (1.0 - damping) * centre_re + (gain_re * sum_re - gain_im * sum_im))
        store(1, (1.0 - damping) * centre_im + (gain_re * sum_im + gain_im * sum_re))

    for shot in range(shots):

        def own_source(plane, _):
            for part in range(2):
                source[part, HALO + plane, start : start + height, 0:width] = residual[shot, part, plane]
            return _

        def row_source(plane, _):
            for part in range(2):
                source[part, plane, top:start, 0:width] = row_low[2 * shot + part, plane].astype(f32)
                source[part, plane, start + height : start + height + ROWS, 0:width] = row_high[
                    2 * shot + part, plane
                ].astype(f32)
            return _

        lax.fori_loop(0, depth, own_source, 0)
        lax.fori_loop(0, planes, row_source, 0)
        for base, count, ghost, _ in sides:
            for plane in range(count):
                for part in range(2):
                    source[part, base + plane, start : start + height, 0:width] = ghost[2 * shot + part, plane].astype(f32)

        def begin(plane, _):
            for row in range(top, top + total, 16):
                here = pl.ds(row, 16)
                gain_re, gain_im = gain[0, plane, here, :], gain[1, plane, here, :]
                source_re, source_im = source[0, plane, here, :], source[1, plane, here, :]
                first[0, plane, here, :] = gain_re * source_re - gain_im * source_im
                first[1, plane, here, :] = gain_re * source_im + gain_im * source_re
            return _

        lax.fori_loop(0, planes, begin, 0)
        old, new = first, second
        for counter in range(1, SWEEPS):
            last = counter == SWEEPS - 1

            def one_plane(plane, _, old=old, new=new, last=last, shot=shot):
                low, high = (start, start + height) if last else (top, top + total)
                for row in range(low, high, 16):

                    def store(part, value, row=row):
                        if last:
                            smoothed[shot, part, plane - HALO, row - start : row - start + 16, :] = value[:, :width]
                        else:
                            new[part, plane, pl.ds(row, 16), :] = value

                    sweep(old, plane, row, 16, store)
                return _

            lax.fori_loop(counter, planes - counter, one_plane, 0)
            old, new = new, old


def smooth(inside, residual, wavenumber, row_low, row_high, deep_low, deep_high):
    shots, _, depth, height, width = residual.shape
    scratch = pltpu.VMEM((2, depth + 2 * HALO, height + 4 * ROWS, LANES), f32)
    return pl.pallas_call(
        smooth_kernel,
        out_shape=jax.ShapeDtypeStruct(residual.shape, f32),
        in_specs=[pl.BlockSpec(memory_space=pltpu.SMEM)] + [pl.BlockSpec(memory_space=VMEM)] * 6,
        scratch_shapes=[scratch] * 4,
        cost_estimate=pl.CostEstimate(flops=300 * residual.size, bytes_accessed=12 * residual.size, transcendentals=0),
        compiler_params=limit(28),
        name="smooth",
    )(inside, residual, wavenumber, row_low, row_high, deep_low, deep_high)


def lifted(smoothed, coarse, out, fine, wide, arrived, left, before=None):
    shots, _, depth, height, width = smoothed.shape
    strips, across = height // QY, width // PX
    blocks = [(shot, part) for part in range(2) for shot in range(shots)]
    comes = [
        pltpu.make_async_copy(smoothed.at[block], fine.at[at], arrived.at[at]) for at, block in enumerate(blocks)
    ]
    goes = [pltpu.make_async_copy(fine.at[at], out.at[block], left.at[at]) for at, block in enumerate(blocks)]
    for copy in comes:
        copy.start()
    if before is not None:
        before()
    values = coarse[...]
    lines = [values[:, strip * across : (strip + 1) * across] for strip in range(strips)]
    wide[...] = exact_dot(jnp.concatenate(lines, axis=0), membership(width, across), 1)
    for at in range(len(blocks)):
        comes[at].wait()
        for strip in range(strips):
            line = strip * 2 * shots + at
            value = jnp.broadcast_to(wide[line : line + 1, :], (QY, width))
            for plane in range(depth):
                rows = slice(strip * QY, (strip + 1) * QY)
                fine[at, plane, rows, :] = fine[at, plane, rows, :] + value
        goes[at].start()
    for copy in goes:
        copy.wait()


def lift_kernel(smoothed, coarse, out, fine, wide, arrived, left):
    lifted(smoothed, coarse, out, fine, wide, arrived, left)


def last_kernel(step, smoothed, kept_before, matrix, same, other, out, fine, wide, arrived, left, vector, coarse):
    def product():
        coarse[...] = kept_before[...]

        @pl.when(lax.axis_index("layer") == step)
        def _():
            ordered(vector, same, other, lax.axis_index("row") % 2 == 0)
            full = vector[...]
            coarse[...] = combined(times(full, matrix[0]), times(full, matrix[1]))

    lifted(smoothed, coarse, out, fine, wide, arrived, left, product)


def lift(smoothed, kept, step=None, *operands):
    shots, _, depth, height, width = smoothed.shape
    lines, cells = kept.shape
    scratch = [
        pltpu.VMEM((2 * shots, depth, height, width), f32),
        pltpu.VMEM((height // QY * lines, width), f32),
        pltpu.SemaphoreType.DMA((2 * shots,)),
        pltpu.SemaphoreType.DMA((2 * shots,)),
    ]
    kernel = lift_kernel
    if operands:
        columns = operands[1].shape[0]
        kernel = functools.partial(last_kernel, step)
        scratch += [pltpu.VMEM((lines, 2 * columns * cells), bf16), pltpu.VMEM((lines, cells), f32)]
    return pl.pallas_call(
        kernel,
        out_shape=pltpu.HBM(smoothed.shape, f32),
        in_specs=[pl.BlockSpec(memory_space=pltpu.HBM)] + [pl.BlockSpec(memory_space=VMEM)] * (1 + len(operands)),
        out_specs=pl.BlockSpec(memory_space=pltpu.HBM),
        scratch_shapes=scratch,
        compiler_params=limit(5),
        name="lift",
    )(smoothed, kept, *operands)


def pack_planes_kernel(residual, wavenumber, first, last):
    shots, _, depth, height, width = residual.shape
    for out, base in ((first, 0), (last, depth - HALO)):
        for plane in range(HALO):
            for shot in range(shots):
                for part in range(2):
                    out[2 * shot + part, plane] = residual[shot, part, base + plane].astype(bf16)
            out[2 * shots, plane] = wavenumber[base + plane].astype(bf16)


def pack_planes(residual, wavenumber):
    shots, _, _, height, width = residual.shape
    shape = jax.ShapeDtypeStruct((2 * shots + 1, HALO, height, width), bf16)
    return pl.pallas_call(
        pack_planes_kernel, out_shape=(shape, shape), compiler_params=limit(10), name="pack_planes"
    )(residual, wavenumber)


def pack_rows_kernel(residual, wavenumber, below, above, first, last):
    shots, _, depth, height, width = residual.shape
    for out, base in ((first, 0), (last, height - ROWS)):
        rows = slice(base, base + ROWS)
        for field in range(2 * shots + 1):
            for plane in range(HALO):
                out[field, plane] = below[field, plane, rows, :]
                out[field, HALO + depth + plane] = above[field, plane, rows, :]
            for plane in range(depth):
                own = wavenumber[plane, rows, :] if field == 2 * shots else residual[field // 2, field % 2, plane, rows, :]
                out[field, HALO + plane] = own.astype(bf16)


def pack_rows(residual, wavenumber, below, above):
    shots, _, depth, _, width = residual.shape
    shape = jax.ShapeDtypeStruct((2 * shots + 1, depth + 2 * HALO, ROWS, width), bf16)
    return pl.pallas_call(
        pack_rows_kernel, out_shape=(shape, shape), compiler_params=limit(10), name="pack_rows"
    )(residual, wavenumber, below, above)


def both_ways(low_block, high_block, axis):
    size = lax.axis_size(axis)
    up = [(i, i + 1) for i in range(size - 1)]
    return lax.ppermute(high_block, axis, up), lax.ppermute(low_block, axis, [(b, a) for a, b in up])


def every_layer(residual, wavenumber, inverse):
    layers, devices = lax.axis_size("layer"), lax.axis_size("row")
    layer, row = lax.axis_index("layer"), lax.axis_index("row")
    inside = jnp.stack([layer > 0, layer < layers - 1, row > 0, row < devices - 1]).astype(f32)

    rhs, spread = restrict(residual, devices)
    next_rhs = lax.ppermute(rhs, "layer", [(i + 1, i) for i in range(layers - 1)])
    matrix = pltpu.with_memory_space_constraint(inverse[:, 0], pltpu.HBM)
    gathered = lax.all_to_all(spread, "row", 0, 0, tiled=True)
    kept, spread = solve_first(matrix, gathered, next_rhs)

    ends = [[2 * column + end for column in range(devices // 2)] for end in range(2)]

    def gather(step, spread):
        return lax.cond(
            layer == step,
            lambda blocks: lax.all_to_all(blocks, "row", 0, 0, axis_index_groups=ends, tiled=True),
            lambda blocks: blocks,
            spread,
        )

    def swap(step, half):
        found = []
        for flip in (1, 0):
            way = [
                (i * devices + j, (i ^ (step - 1) ^ step) * devices + (j ^ flip))
                for i in range(layers)
                for j in range(devices)
            ]
            found.append(lax.ppermute(half, ("layer", "row"), way))
        return found

    def send(step, half):
        found = []
        for flip in (1, 0):
            way = [((step - 1) * devices + j, step * devices + (j ^ flip)) for j in range(devices)]
            found.append(lax.ppermute(half, ("layer", "row"), way))
        return found

    def solve(step, other, same, kept):
        held = hold(matrix)
        return solve_layer(step, held, same, other, next_rhs, kept)

    middle = layers // 2
    for step in range(1, layers - 1):
        half = gather(step - 1, spread)
        if step == middle:
            kept, spread = solve(step, *send(step, half), kept)
            continue
        kept, spread = lax.cond(
            (layer == step - 1) | (layer == step),
            lambda half, kept, step=step: tuple(solve(step, *swap(step, half), kept)),
            lambda half, kept: (kept, half),
            half,
            kept,
        )

    first, last = pack_planes(residual, wavenumber)
    below, above = both_ways(first, last, "layer")
    first, last = pack_rows(residual, wavenumber, below, above)
    row_low, row_high = both_ways(first, last, "row")
    smoothed = smooth(inside, residual, wavenumber, row_low, row_high, below, above)

    step = layers - 1
    half = gather(step - 1, spread)

    def finish(half, smoothed, kept):
        other, same = swap(step, half)
        held = hold(matrix)
        return lift(smoothed, kept, step, held, same, other)

    return lax.cond(
        layer >= step - 1, finish, lambda half, smoothed, kept: lift(smoothed, kept), half, smoothed, kept
    )


def solution(mesh):
    return jax.shard_map(
        every_layer,
        mesh=mesh,
        in_specs=(
            P(None, None, "layer", "row", None),
            P("layer", "row", None),
            P(None, "layer", "row", None),
        ),
        out_specs=P(None, None, "layer", "row", None),
        check_vma=False,
    )
```

```python
import functools

import jax
import jax.numpy as jnp
from jax import lax
from jax.experimental import pallas as pl
from jax.experimental.pallas import tpu as pltpu
from jax.sharding import PartitionSpec as P


QY = 16
PX = 4
SWEEPS = 4
HALO = SWEEPS - 1
ROWS = 8
LANES = 256

damping = 0.8
absorb = 0.5
coupling = 0.45

VMEM = pltpu.VMEM
f32 = jnp.float32
bf16 = jnp.bfloat16


def limit(mebibytes):
    return pltpu.CompilerParams(vmem_limit_bytes=mebibytes << 20)


def membership(fine, coarse):
    row = lax.broadcasted_iota(jnp.int32, (fine, coarse), 0)
    col = lax.broadcasted_iota(jnp.int32, (fine, coarse), 1)
    return jnp.where((row >= col * PX) & (row < col * PX + PX), 1.0, 0.0).astype(bf16)


def exact_dot(values, selection, contract):
    first = values.astype(bf16)
    rest = values - first.astype(f32)
    second = rest.astype(bf16)
    third = (rest - second.astype(f32)).astype(bf16)
    total = None
    for piece in (third, second, first):
        part = lax.dot_general(piece, selection, (((1,), (contract,)), ((), ())), preferred_element_type=f32)
        total = part if total is None else total + part
    return total


def restrict_kernel(residual, rhs, spread):
    shots, _, depth, height, width = residual.shape
    strips, across = height // QY, width // PX
    sums = []
    for strip in range(strips):
        for part in range(2):
            for shot in range(shots):
                total = residual[shot, part, 0, strip * QY : (strip + 1) * QY, :]
                for plane in range(1, depth):
                    total = total + residual[shot, part, plane, strip * QY : (strip + 1) * QY, :]
                sums.append(jnp.sum(total, axis=0, keepdims=True))
    means = exact_dot(jnp.concatenate(sums, axis=0), membership(width, across), 0) * (1.0 / (depth * QY * PX))
    lines = 2 * shots
    for strip in range(strips):
        rhs[:, strip * across : (strip + 1) * across] = means[strip * lines : (strip + 1) * lines, :]
    vector = rhs[...].astype(bf16)
    for device in range(spread.shape[0]):
        spread[device] = vector


def restrict(residual, devices):
    shots, _, _, height, width = residual.shape
    cells = (height // QY) * (width // PX)
    return pl.pallas_call(
        restrict_kernel,
        out_shape=(
            jax.ShapeDtypeStruct((2 * shots, cells), f32),
            jax.ShapeDtypeStruct((devices, 2 * shots, cells), bf16),
        ),
        compiler_params=limit(8),
        name="restrict",
    )(residual)


def hold_kernel(step, matrix, held, arrived):
    @pl.when(lax.axis_index("layer") == step)
    def _():
        copy = pltpu.make_async_copy(matrix, held, arrived)
        copy.start()
        copy.wait()


def hold(step, matrix):
    return pl.pallas_call(
        functools.partial(hold_kernel, step),
        out_shape=pltpu.VMEM(matrix.shape, matrix.dtype),
        in_specs=[pl.BlockSpec(memory_space=pltpu.HBM)],
        out_specs=pl.BlockSpec(memory_space=VMEM),
        scratch_shapes=[pltpu.SemaphoreType.DMA],
        compiler_params=limit(1),
        name="hold",
    )(matrix)


def ordered(vector, same, other, first_end):
    columns, _, cells = same.shape
    for column in range(columns):
        own, far = same[column], other[column]
        at = 2 * column * cells
        vector[:, at : at + cells] = jnp.where(first_end, own, far)
        vector[:, at + cells : at + 2 * cells] = jnp.where(first_end, far, own)


def combined(by_re, by_im):
    shots = by_re.shape[0] // 2
    return jnp.concatenate([by_re[:shots] - by_im[shots:], by_re[shots:] + by_im[:shots]], axis=0)


def hand_on(solved, next_rhs, spread):
    out = (next_rhs[...] + coupling * solved).astype(bf16)
    for column in range(spread.shape[0]):
        spread[column] = out


def times(part, rows):
    return lax.dot_general(part, rows, (((1,), (1,)), ((), ())), preferred_element_type=f32)


def first_kernel(matrix, gathered, next_rhs, kept, spread, held, vector, arrived):
    devices, _, cells = gathered.shape
    pieces = arrived.shape[0]
    across = matrix.shape[2] // pieces
    columns = [slice(piece * across, (piece + 1) * across) for piece in range(pieces)]
    copies = [
        pltpu.make_async_copy(matrix.at[:, :, columns[piece]], held.at[:, :, columns[piece]], arrived.at[piece])
        for piece in range(pieces)
    ]
    for copy in copies:
        copy.start()
    for device in range(devices):
        vector[:, device * cells : (device + 1) * cells] = gathered[device]
    by = [None, None]
    for piece in range(pieces):
        part = vector[:, columns[piece]]
        copies[piece].wait()
        for side in range(2):
            product = times(part, held[side, :, columns[piece]])
            by[side] = product if by[side] is None else by[side] + product
    solved = combined(by[0], by[1])
    kept[...] = solved
    hand_on(solved, next_rhs, spread)


def solve_first(matrix, gathered, next_rhs):
    devices, lines, cells = gathered.shape
    pieces = 6
    return pl.pallas_call(
        first_kernel,
        out_shape=(
            jax.ShapeDtypeStruct((lines, cells), f32),
            jax.ShapeDtypeStruct((devices // 2, lines, cells), bf16),
        ),
        in_specs=[pl.BlockSpec(memory_space=pltpu.HBM)] + [pl.BlockSpec(memory_space=VMEM)] * 2,
        scratch_shapes=[
            pltpu.VMEM(matrix.shape, bf16),
            pltpu.VMEM((lines, devices * cells), bf16),
            pltpu.SemaphoreType.DMA((pieces,)),
        ],
        compiler_params=limit(8),
        cost_estimate=pl.CostEstimate(flops=4 * matrix.size, bytes_accessed=2 * matrix.size, transcendentals=0),
        name="solve_first",
    )(matrix, gathered, next_rhs)


def layer_kernel(step, matrix, same, other, next_rhs, kept_before, kept, spread, vector):
    ordered(vector, same, other, lax.axis_index("row") % 2 == 0)
    full = vector[...]
    solved = combined(times(full, matrix[0]), times(full, matrix[1]))
    kept[...] = jnp.where(lax.axis_index("layer") == step, solved, kept_before[...])
    hand_on(solved, next_rhs, spread)


def solve_layer(step, matrix, same, other, next_rhs, kept):
    columns, lines, cells = same.shape
    return pl.pallas_call(
        functools.partial(layer_kernel, step),
        out_shape=(
            jax.ShapeDtypeStruct((lines, cells), f32),
            jax.ShapeDtypeStruct((columns, lines, cells), bf16),
        ),
        in_specs=[pl.BlockSpec(memory_space=VMEM)] * 5,
        scratch_shapes=[pltpu.VMEM((lines, 2 * columns * cells), bf16)],
        compiler_params=limit(3),
        cost_estimate=pl.CostEstimate(flops=4 * matrix.size, bytes_accessed=2 * matrix.size, transcendentals=0),
        name="solve_layer",
    )(matrix, same, other, next_rhs, kept)


def smooth_kernel(inside, residual, wavenumber, row_low, row_high, deep_low, deep_high, smoothed, gain, source, first, second):
    shots, _, depth, height, width = residual.shape
    top = ROWS
    start = top + ROWS
    total = height + 2 * ROWS
    planes = depth + 2 * HALO
    rest = LANES - width
    sides = (
        (0, HALO, deep_low, inside[0]),
        (HALO + depth, HALO, deep_high, inside[1]),
    )

    def gains(values, factor):
        real_part = 6.0 - values
        imag_part = -absorb * values
        scale = damping * factor / (real_part * real_part + imag_part * imag_part)
        return real_part * scale, -imag_part * scale

    def put_gain(plane, row, values, factor):
        real_part, imag_part = gains(values, factor)
        rows = values.shape[0]
        gain[0, plane, pl.ds(row, rows), 0:width] = real_part
        gain[1, plane, pl.ds(row, rows), 0:width] = imag_part

    blank = jnp.zeros((total, rest), f32)

    def clear(plane, _):
        for part in range(2):
            gain[part, plane, top : top + total, width:LANES] = blank
            source[part, plane, top : top + total, width:LANES] = blank
        return _

    lax.fori_loop(0, planes, clear, 0)

    def own_gain(plane, _):
        for row in range(0, height, 16):
            put_gain(HALO + plane, start + row, wavenumber[plane, row : row + 16, :], 1.0)
        return _

    lax.fori_loop(0, depth, own_gain, 0)
    for base, count, ghost, factor in sides:
        for plane in range(count):
            for row in range(0, height, 16):
                put_gain(base + plane, start + row, ghost[2 * shots, plane, row : row + 16, :].astype(f32), factor)
    for base, count, factor in ((0, HALO, inside[0]), (HALO, depth, 1.0), (HALO + depth, HALO, inside[1])):

        def row_gain(plane, _, factor=factor):
            put_gain(plane, top, row_low[2 * shots, plane].astype(f32), factor * inside[2])
            put_gain(plane, start + height, row_high[2 * shots, plane].astype(f32), factor * inside[3])
            return _

        lax.fori_loop(base, base + count, row_gain, 0)

    def sweep(old, plane, row, rows, store):
        here = pl.ds(row, rows)
        terms = []
        for part in range(2):
            centre = old[part, plane, here, :]
            beside = old[part, plane - 1, here, :] + old[part, plane + 1, here, :]
            beside = beside + old[part, plane, pl.ds(row - 1, rows), :] + old[part, plane, pl.ds(row + 1, rows), :]
            beside = beside + pltpu.roll(centre, 1, 1) + pltpu.roll(centre, LANES - 1, 1)
            terms.append((centre, source[part, plane, here, :] + beside))
        (centre_re, sum_re), (centre_im, sum_im) = terms
        gain_re, gain_im = gain[0, plane, here, :], gain[1, plane, here, :]
        store(0, (1.0 - damping) * centre_re + (gain_re * sum_re - gain_im * sum_im))
        store(1, (1.0 - damping) * centre_im + (gain_re * sum_im + gain_im * sum_re))

    for shot in range(shots):

        def own_source(plane, _):
            for part in range(2):
                source[part, HALO + plane, start : start + height, 0:width] = residual[shot, part, plane]
            return _

        def row_source(plane, _):
            for part in range(2):
                source[part, plane, top:start, 0:width] = row_low[2 * shot + part, plane].astype(f32)
                source[part, plane, start + height : start + height + ROWS, 0:width] = row_high[
                    2 * shot + part, plane
                ].astype(f32)
            return _

        lax.fori_loop(0, depth, own_source, 0)
        lax.fori_loop(0, planes, row_source, 0)
        for base, count, ghost, _ in sides:
            for plane in range(count):
                for part in range(2):
                    source[part, base + plane, start : start + height, 0:width] = ghost[2 * shot + part, plane].astype(f32)

        def begin(plane, _):
            for row in range(top, top + total, 16):
                here = pl.ds(row, 16)
                gain_re, gain_im = gain[0, plane, here, :], gain[1, plane, here, :]
                source_re, source_im = source[0, plane, here, :], source[1, plane, here, :]
                first[0, plane, here, :] = gain_re * source_re - gain_im * source_im
                first[1, plane, here, :] = gain_re * source_im + gain_im * source_re
            return _

        lax.fori_loop(0, planes, begin, 0)
        old, new = first, second
        for counter in range(1, SWEEPS):
            last = counter == SWEEPS - 1

            def one_plane(plane, _, old=old, new=new, last=last, shot=shot):
                low, high = (start, start + height) if last else (top, top + total)
                for row in range(low, high, 16):

                    def store(part, value, row=row):
                        if last:
                            smoothed[shot, part, plane - HALO, row - start : row - start + 16, :] = value[:, :width]
                        else:
                            new[part, plane, pl.ds(row, 16), :] = value

                    sweep(old, plane, row, 16, store)
                return _

            lax.fori_loop(counter, planes - counter, one_plane, 0)
            old, new = new, old


def smooth(inside, residual, wavenumber, row_low, row_high, deep_low, deep_high):
    shots, _, depth, height, width = residual.shape
    scratch = pltpu.VMEM((2, depth + 2 * HALO, height + 4 * ROWS, LANES), f32)
    return pl.pallas_call(
        smooth_kernel,
        out_shape=jax.ShapeDtypeStruct(residual.shape, f32),
        in_specs=[pl.BlockSpec(memory_space=pltpu.SMEM)] + [pl.BlockSpec(memory_space=VMEM)] * 6,
        scratch_shapes=[scratch] * 4,
        cost_estimate=pl.CostEstimate(flops=300 * residual.size, bytes_accessed=12 * residual.size, transcendentals=0),
        compiler_params=limit(28),
        name="smooth",
    )(inside, residual, wavenumber, row_low, row_high, deep_low, deep_high)


def lifted(smoothed, values, out, fine, wide, left):
    shots, _, depth, height, width = smoothed.shape
    strips, across = height // QY, width // PX
    blocks = [(shot, part) for part in range(2) for shot in range(shots)]
    goes = [pltpu.make_async_copy(fine.at[at], out.at[block], left.at[at]) for at, block in enumerate(blocks)]
    lines = [values[:, strip * across : (strip + 1) * across] for strip in range(strips)]
    wide[...] = exact_dot(jnp.concatenate(lines, axis=0), membership(width, across), 1)
    for at, (shot, part) in enumerate(blocks):
        for strip in range(strips):
            line = strip * 2 * shots + at
            value = jnp.broadcast_to(wide[line : line + 1, :], (QY, width))
            for plane in range(depth):
                rows = slice(strip * QY, (strip + 1) * QY)
                fine[at, plane, rows, :] = smoothed[shot, part, plane, rows, :] + value
        goes[at].start()
    for copy in goes:
        copy.wait()


def lift_kernel(smoothed, coarse, out, fine, wide, left):
    lifted(smoothed, coarse[...], out, fine, wide, left)


def last_kernel(step, smoothed, kept_before, matrix, same, other, out, fine, wide, left, vector, coarse):
    coarse[...] = kept_before[...]

    @pl.when(lax.axis_index("layer") == step)
    def _():
        ordered(vector, same, other, lax.axis_index("row") % 2 == 0)
        full = vector[...]
        coarse[...] = combined(times(full, matrix[0]), times(full, matrix[1]))

    lifted(smoothed, coarse[...], out, fine, wide, left)


def lift(smoothed, kept, step=None, *operands):
    shots, _, depth, height, width = smoothed.shape
    lines, cells = kept.shape
    scratch = [
        pltpu.VMEM((2 * shots, depth, height, width), f32),
        pltpu.VMEM((height // QY * lines, width), f32),
        pltpu.SemaphoreType.DMA((2 * shots,)),
    ]
    kernel = lift_kernel
    if operands:
        columns = operands[1].shape[0]
        kernel = functools.partial(last_kernel, step)
        scratch += [pltpu.VMEM((lines, 2 * columns * cells), bf16), pltpu.VMEM((lines, cells), f32)]
    return pl.pallas_call(
        kernel,
        out_shape=pltpu.HBM(smoothed.shape, f32),
        in_specs=[pl.BlockSpec(memory_space=VMEM)] * (2 + len(operands)),
        out_specs=pl.BlockSpec(memory_space=pltpu.HBM),
        scratch_shapes=scratch,
        compiler_params=limit(6),
        name="lift",
    )(smoothed, kept, *operands)


def pack_planes_kernel(residual, wavenumber, first, last):
    shots, _, depth, height, width = residual.shape
    for out, base in ((first, 0), (last, depth - HALO)):
        for plane in range(HALO):
            for shot in range(shots):
                for part in range(2):
                    out[2 * shot + part, plane] = residual[shot, part, base + plane].astype(bf16)
            out[2 * shots, plane] = wavenumber[base + plane].astype(bf16)


def pack_planes(residual, wavenumber):
    shots, _, _, height, width = residual.shape
    shape = jax.ShapeDtypeStruct((2 * shots + 1, HALO, height, width), bf16)
    return pl.pallas_call(
        pack_planes_kernel, out_shape=(shape, shape), compiler_params=limit(10), name="pack_planes"
    )(residual, wavenumber)


def pack_rows_kernel(residual, wavenumber, below, above, first, last):
    shots, _, depth, height, width = residual.shape
    for out, base in ((first, 0), (last, height - ROWS)):
        rows = slice(base, base + ROWS)
        for field in range(2 * shots + 1):
            for plane in range(HALO):
                out[field, plane] = below[field, plane, rows, :]
                out[field, HALO + depth + plane] = above[field, plane, rows, :]
            for plane in range(depth):
                own = wavenumber[plane, rows, :] if field == 2 * shots else residual[field // 2, field % 2, plane, rows, :]
                out[field, HALO + plane] = own.astype(bf16)


def pack_rows(residual, wavenumber, below, above):
    shots, _, depth, _, width = residual.shape
    shape = jax.ShapeDtypeStruct((2 * shots + 1, depth + 2 * HALO, ROWS, width), bf16)
    return pl.pallas_call(
        pack_rows_kernel, out_shape=(shape, shape), compiler_params=limit(10), name="pack_rows"
    )(residual, wavenumber, below, above)


def both_ways(low_block, high_block, axis):
    size = lax.axis_size(axis)
    up = [(i, i + 1) for i in range(size - 1)]
    return lax.ppermute(high_block, axis, up), lax.ppermute(low_block, axis, [(b, a) for a, b in up])


def every_layer(residual, wavenumber, inverse):
    layers, devices = lax.axis_size("layer"), lax.axis_size("row")
    layer, row = lax.axis_index("layer"), lax.axis_index("row")
    inside = jnp.stack([layer > 0, layer < layers - 1, row > 0, row < devices - 1]).astype(f32)

    rhs, spread = restrict(residual, devices)
    next_rhs = lax.ppermute(rhs, "layer", [(i + 1, i) for i in range(layers - 1)])
    matrix = pltpu.with_memory_space_constraint(inverse[:, 0], pltpu.HBM)
    gathered = lax.all_to_all(spread, "row", 0, 0, tiled=True)
    kept, spread = solve_first(matrix, gathered, next_rhs)

    ends = [[2 * column + end for column in range(devices // 2)] for end in range(2)]

    def gather(step, spread):
        return lax.cond(
            layer == step,
            lambda blocks: lax.all_to_all(blocks, "row", 0, 0, axis_index_groups=ends, tiled=True),
            lambda blocks: blocks,
            spread,
        )

    def swap(step, half):
        found = []
        for flip in (1, 0):
            way = [
                (i * devices + j, (i ^ (step - 1) ^ step) * devices + (j ^ flip))
                for i in range(layers)
                for j in range(devices)
            ]
            found.append(lax.ppermute(half, ("layer", "row"), way))
        return found

    def send(step, half):
        found = []
        for flip in (1, 0):
            way = [((step - 1) * devices + j, step * devices + (j ^ flip)) for j in range(devices)]
            found.append(lax.ppermute(half, ("layer", "row"), way))
        return found

    def solve(step, other, same, kept):
        held = hold(step, matrix)
        return solve_layer(step, held, same, other, next_rhs, kept)

    middle = layers // 2
    for step in range(1, layers - 1):
        half = gather(step - 1, spread)
        if step == middle:
            kept, spread = solve(step, *send(step, half), kept)
            continue
        kept, spread = lax.cond(
            (layer == step - 1) | (layer == step),
            lambda half, kept, step=step: tuple(solve(step, *swap(step, half), kept)),
            lambda half, kept: (kept, half),
            half,
            kept,
        )

    first, last = pack_planes(residual, wavenumber)
    below, above = both_ways(first, last, "layer")
    first, last = pack_rows(residual, wavenumber, below, above)
    row_low, row_high = both_ways(first, last, "row")
    smoothed = smooth(inside, residual, wavenumber, row_low, row_high, below, above)

    step = layers - 1
    half = gather(step - 1, spread)

    def finish(half, smoothed, kept):
        other, same = swap(step, half)
        held = hold(step, matrix)
        return lift(smoothed, kept, step, held, same, other)

    return lax.cond(
        layer >= step - 1, finish, lambda half, smoothed, kept: lift(smoothed, kept), half, smoothed, kept
    )


def solution(mesh):
    return jax.shard_map(
        every_layer,
        mesh=mesh,
        in_specs=(
            P(None, None, "layer", "row", None),
            P("layer", "row", None),
            P(None, "layer", "row", None),
        ),
        out_specs=P(None, None, "layer", "row", None),
        check_vma=False,
    )
```

```python
import functools

import jax
import jax.numpy as jnp
from jax import lax
from jax.experimental import pallas as pl
from jax.experimental.pallas import tpu as pltpu
from jax.sharding import PartitionSpec as P


QY = 16
PX = 4
SWEEPS = 4
HALO = SWEEPS - 1
ROWS = 8
LANES = 256

damping = 0.8
absorb = 0.5
coupling = 0.45

VMEM = pltpu.VMEM
f32 = jnp.float32
bf16 = jnp.bfloat16


def limit(mebibytes):
    return pltpu.CompilerParams(vmem_limit_bytes=mebibytes << 20)


def membership(fine, coarse):
    row = lax.broadcasted_iota(jnp.int32, (fine, coarse), 0)
    col = lax.broadcasted_iota(jnp.int32, (fine, coarse), 1)
    return jnp.where((row >= col * PX) & (row < col * PX + PX), 1.0, 0.0).astype(bf16)


def exact_dot(values, selection, contract):
    first = values.astype(bf16)
    rest = values - first.astype(f32)
    second = rest.astype(bf16)
    third = (rest - second.astype(f32)).astype(bf16)
    total = None
    for piece in (third, second, first):
        part = lax.dot_general(piece, selection, (((1,), (contract,)), ((), ())), preferred_element_type=f32)
        total = part if total is None else total + part
    return total


def restrict_kernel(residual, rhs, spread):
    shots, _, depth, height, width = residual.shape
    strips, across = height // QY, width // PX
    sums = []
    for strip in range(strips):
        for part in range(2):
            for shot in range(shots):
                total = residual[shot, part, 0, strip * QY : (strip + 1) * QY, :]
                for plane in range(1, depth):
                    total = total + residual[shot, part, plane, strip * QY : (strip + 1) * QY, :]
                sums.append(jnp.sum(total, axis=0, keepdims=True))
    means = exact_dot(jnp.concatenate(sums, axis=0), membership(width, across), 0) * (1.0 / (depth * QY * PX))
    lines = 2 * shots
    for strip in range(strips):
        rhs[:, strip * across : (strip + 1) * across] = means[strip * lines : (strip + 1) * lines, :]
    vector = rhs[...].astype(bf16)
    for device in range(spread.shape[0]):
        spread[device] = vector


def restrict(residual, devices):
    shots, _, _, height, width = residual.shape
    cells = (height // QY) * (width // PX)
    return pl.pallas_call(
        restrict_kernel,
        out_shape=(
            jax.ShapeDtypeStruct((2 * shots, cells), f32),
            jax.ShapeDtypeStruct((devices, 2 * shots, cells), bf16),
        ),
        compiler_params=limit(8),
        name="restrict",
    )(residual)


def hold_kernel(step, matrix, held, arrived):
    @pl.when(lax.axis_index("layer") == step)
    def _():
        copy = pltpu.make_async_copy(matrix, held, arrived)
        copy.start()
        copy.wait()


def hold(step, matrix):
    return pl.pallas_call(
        functools.partial(hold_kernel, step),
        out_shape=pltpu.VMEM(matrix.shape, matrix.dtype),
        in_specs=[pl.BlockSpec(memory_space=pltpu.HBM)],
        out_specs=pl.BlockSpec(memory_space=VMEM),
        scratch_shapes=[pltpu.SemaphoreType.DMA],
        compiler_params=limit(1),
        name="hold",
    )(matrix)


def ordered(vector, both):
    columns, lines, cells = both.shape
    half = lines // 2
    first_end = lax.axis_index("row") % 2 == 0
    for column in range(columns):
        own, far = both[column, :half], both[column, half:]
        at = 2 * column * cells
        vector[:, at : at + cells] = jnp.where(first_end, own, far)
        vector[:, at + cells : at + 2 * cells] = jnp.where(first_end, far, own)


def ordered_two(vector, same, other):
    columns, _, cells = same.shape
    first_end = lax.axis_index("row") % 2 == 0
    for column in range(columns):
        own, far = same[column], other[column]
        at = 2 * column * cells
        vector[:, at : at + cells] = jnp.where(first_end, own, far)
        vector[:, at + cells : at + 2 * cells] = jnp.where(first_end, far, own)


def combined(by_re, by_im):
    shots = by_re.shape[0] // 2
    return jnp.concatenate([by_re[:shots] - by_im[shots:], by_re[shots:] + by_im[:shots]], axis=0)


def hand_on(solved, next_rhs, spread):
    out = (next_rhs[...] + coupling * solved).astype(bf16)
    for column in range(spread.shape[0]):
        spread[column] = out


def times(part, rows):
    return lax.dot_general(part, rows, (((1,), (1,)), ((), ())), preferred_element_type=f32)


def first_kernel(matrix, gathered, solved, held, vector, arrived):
    devices, _, cells = gathered.shape
    pieces = arrived.shape[0]
    across = matrix.shape[2] // pieces
    columns = [slice(piece * across, (piece + 1) * across) for piece in range(pieces)]
    copies = [
        pltpu.make_async_copy(matrix.at[:, :, columns[piece]], held.at[:, :, columns[piece]], arrived.at[piece])
        for piece in range(pieces)
    ]
    for copy in copies:
        copy.start()
    for device in range(devices):
        vector[:, device * cells : (device + 1) * cells] = gathered[device]
    by = [None, None]
    for piece in range(pieces):
        part = vector[:, columns[piece]]
        copies[piece].wait()
        for side in range(2):
            product = times(part, held[side, :, columns[piece]])
            by[side] = product if by[side] is None else by[side] + product
    solved[...] = combined(by[0], by[1])


def solve_first(matrix, gathered):
    devices, lines, cells = gathered.shape
    pieces = 6
    return pl.pallas_call(
        first_kernel,
        out_shape=jax.ShapeDtypeStruct((lines, cells), f32),
        in_specs=[pl.BlockSpec(memory_space=pltpu.HBM), pl.BlockSpec(memory_space=VMEM)],
        scratch_shapes=[
            pltpu.VMEM(matrix.shape, bf16),
            pltpu.VMEM((lines, devices * cells), bf16),
            pltpu.SemaphoreType.DMA((pieces,)),
        ],
        compiler_params=limit(8),
        cost_estimate=pl.CostEstimate(flops=4 * matrix.size, bytes_accessed=2 * matrix.size, transcendentals=0),
        name="solve_first",
    )(matrix, gathered)


def meet_kernel(near, far, rhs, far_rhs, spread):
    lines = rhs.shape[0]
    own = (rhs[...] + coupling * near[...]).astype(bf16)
    partner = (far_rhs[...] + coupling * far[...]).astype(bf16)
    for column in range(spread.shape[0]):
        spread[column, :lines] = own
        spread[column, lines:] = partner


def meet(near, far, rhs, far_rhs, columns):
    lines, cells = rhs.shape
    return pl.pallas_call(
        meet_kernel,
        out_shape=jax.ShapeDtypeStruct((columns, 2 * lines, cells), bf16),
        compiler_params=limit(2),
        name="meet",
    )(near, far, rhs, far_rhs)


def odd_kernel(step, matrix, both, next_rhs, kept_before, kept, spread, vector):
    ordered(vector, both)
    full = vector[...]
    solved = combined(times(full, matrix[0]), times(full, matrix[1]))
    kept[...] = jnp.where(lax.axis_index("layer") == step, solved, kept_before[...])
    hand_on(solved, next_rhs, spread)


def solve_odd(step, matrix, both, next_rhs, kept):
    columns, lines, cells = both.shape
    return pl.pallas_call(
        functools.partial(odd_kernel, step),
        out_shape=(
            jax.ShapeDtypeStruct((lines // 2, cells), f32),
            jax.ShapeDtypeStruct((columns, lines // 2, cells), bf16),
        ),
        in_specs=[pl.BlockSpec(memory_space=VMEM)] * 4,
        scratch_shapes=[pltpu.VMEM((lines // 2, 2 * columns * cells), bf16)],
        compiler_params=limit(3),
        cost_estimate=pl.CostEstimate(flops=4 * matrix.size, bytes_accessed=2 * matrix.size, transcendentals=0),
        name="solve_odd",
    )(matrix, both, next_rhs, kept)


def even_kernel(step, matrix, same, other, kept_before, kept, vector):
    ordered_two(vector, same, other)
    full = vector[...]
    solved = combined(times(full, matrix[0]), times(full, matrix[1]))
    kept[...] = jnp.where(lax.axis_index("layer") == step, solved, kept_before[...])


def solve_even(step, matrix, same, other, kept):
    columns, lines, cells = same.shape
    return pl.pallas_call(
        functools.partial(even_kernel, step),
        out_shape=jax.ShapeDtypeStruct((lines, cells), f32),
        in_specs=[pl.BlockSpec(memory_space=VMEM)] * 4,
        scratch_shapes=[pltpu.VMEM((lines, 2 * columns * cells), bf16)],
        compiler_params=limit(3),
        cost_estimate=pl.CostEstimate(flops=4 * matrix.size, bytes_accessed=2 * matrix.size, transcendentals=0),
        name="solve_even",
    )(matrix, same, other, kept)


def smooth_kernel(inside, residual, wavenumber, row_low, row_high, deep_low, deep_high, smoothed, gain, source, first, second):
    shots, _, depth, height, width = residual.shape
    top = ROWS
    start = top + ROWS
    total = height + 2 * ROWS
    planes = depth + 2 * HALO
    rest = LANES - width
    sides = (
        (0, HALO, deep_low, inside[0]),
        (HALO + depth, HALO, deep_high, inside[1]),
    )

    def gains(values, factor):
        real_part = 6.0 - values
        imag_part = -absorb * values
        scale = damping * factor / (real_part * real_part + imag_part * imag_part)
        return real_part * scale, -imag_part * scale

    def put_gain(plane, row, values, factor):
        real_part, imag_part = gains(values, factor)
        rows = values.shape[0]
        gain[0, plane, pl.ds(row, rows), 0:width] = real_part
        gain[1, plane, pl.ds(row, rows), 0:width] = imag_part

    blank = jnp.zeros((total, rest), f32)

    def clear(plane, _):
        for part in range(2):
            gain[part, plane, top : top + total, width:LANES] = blank
            source[part, plane, top : top + total, width:LANES] = blank
        return _

    lax.fori_loop(0, planes, clear, 0)

    def own_gain(plane, _):
        for row in range(0, height, 16):
            put_gain(HALO + plane, start + row, wavenumber[plane, row : row + 16, :], 1.0)
        return _

    lax.fori_loop(0, depth, own_gain, 0)
    for base, count, ghost, factor in sides:
        for plane in range(count):
            for row in range(0, height, 16):
                put_gain(base + plane, start + row, ghost[2 * shots, plane, row : row + 16, :].astype(f32), factor)
    for base, count, factor in ((0, HALO, inside[0]), (HALO, depth, 1.0), (HALO + depth, HALO, inside[1])):

        def row_gain(plane, _, factor=factor):
            put_gain(plane, top, row_low[2 * shots, plane].astype(f32), factor * inside[2])
            put_gain(plane, start + height, row_high[2 * shots, plane].astype(f32), factor * inside[3])
            return _

        lax.fori_loop(base, base + count, row_gain, 0)

    def sweep(old, plane, row, rows, store):
        here = pl.ds(row, rows)
        terms = []
        for part in range(2):
            centre = old[part, plane, here, :]
            beside = old[part, plane - 1, here, :] + old[part, plane + 1, here, :]
            beside = beside + old[part, plane, pl.ds(row - 1, rows), :] + old[part, plane, pl.ds(row + 1, rows), :]
            beside = beside + pltpu.roll(centre, 1, 1) + pltpu.roll(centre, LANES - 1, 1)
            terms.append((centre, source[part, plane, here, :] + beside))
        (centre_re, sum_re), (centre_im, sum_im) = terms
        gain_re, gain_im = gain[0, plane, here, :], gain[1, plane, here, :]
        store(0, (1.0 - damping) * centre_re + (gain_re * sum_re - gain_im * sum_im))
        store(1, (1.0 - damping) * centre_im + (gain_re * sum_im + gain_im * sum_re))

    for shot in range(shots):

        def own_source(plane, _):
            for part in range(2):
                source[part, HALO + plane, start : start + height, 0:width] = residual[shot, part, plane]
            return _

        def row_source(plane, _):
            for part in range(2):
                source[part, plane, top:start, 0:width] = row_low[2 * shot + part, plane].astype(f32)
                source[part, plane, start + height : start + height + ROWS, 0:width] = row_high[
                    2 * shot + part, plane
                ].astype(f32)
            return _

        lax.fori_loop(0, depth, own_source, 0)
        lax.fori_loop(0, planes, row_source, 0)
        for base, count, ghost, _ in sides:
            for plane in range(count):
                for part in range(2):
                    source[part, base + plane, start : start + height, 0:width] = ghost[2 * shot + part, plane].astype(f32)

        def begin(plane, _):
            for row in range(top, top + total, 16):
                here = pl.ds(row, 16)
                gain_re, gain_im = gain[0, plane, here, :], gain[1, plane, here, :]
                source_re, source_im = source[0, plane, here, :], source[1, plane, here, :]
                first[0, plane, here, :] = gain_re * source_re - gain_im * source_im
                first[1, plane, here, :] = gain_re * source_im + gain_im * source_re
            return _

        lax.fori_loop(0, planes, begin, 0)
        old, new = first, second
        for counter in range(1, SWEEPS):
            last = counter == SWEEPS - 1

            def one_plane(plane, _, old=old, new=new, last=last, shot=shot):
                low, high = (start, start + height) if last else (top, top + total)
                for row in range(low, high, 16):

                    def store(part, value, row=row):
                        if last:
                            smoothed[shot, part, plane - HALO, row - start : row - start + 16, :] = value[:, :width]
                        else:
                            new[part, plane, pl.ds(row, 16), :] = value

                    sweep(old, plane, row, 16, store)
                return _

            lax.fori_loop(counter, planes - counter, one_plane, 0)
            old, new = new, old


def smooth(inside, residual, wavenumber, row_low, row_high, deep_low, deep_high):
    shots, _, depth, height, width = residual.shape
    scratch = pltpu.VMEM((2, depth + 2 * HALO, height + 4 * ROWS, LANES), f32)
    return pl.pallas_call(
        smooth_kernel,
        out_shape=jax.ShapeDtypeStruct(residual.shape, f32),
        in_specs=[pl.BlockSpec(memory_space=pltpu.SMEM)] + [pl.BlockSpec(memory_space=VMEM)] * 6,
        scratch_shapes=[scratch] * 4,
        cost_estimate=pl.CostEstimate(flops=300 * residual.size, bytes_accessed=12 * residual.size, transcendentals=0),
        compiler_params=limit(28),
        name="smooth",
    )(inside, residual, wavenumber, row_low, row_high, deep_low, deep_high)


def lifted(smoothed, values, out, fine, wide, left):
    shots, _, depth, height, width = smoothed.shape
    strips, across = height // QY, width // PX
    blocks = [(shot, part) for part in range(2) for shot in range(shots)]
    goes = [pltpu.make_async_copy(fine.at[at], out.at[block], left.at[at]) for at, block in enumerate(blocks)]
    lines = [values[:, strip * across : (strip + 1) * across] for strip in range(strips)]
    wide[...] = exact_dot(jnp.concatenate(lines, axis=0), membership(width, across), 1)
    for at, (shot, part) in enumerate(blocks):
        for strip in range(strips):
            line = strip * 2 * shots + at
            value = jnp.broadcast_to(wide[line : line + 1, :], (QY, width))
            for plane in range(depth):
                rows = slice(strip * QY, (strip + 1) * QY)
                fine[at, plane, rows, :] = smoothed[shot, part, plane, rows, :] + value
        goes[at].start()
    for copy in goes:
        copy.wait()


def lift_kernel(smoothed, coarse, out, fine, wide, left):
    lifted(smoothed, coarse[...], out, fine, wide, left)


def last_kernel(step, smoothed, kept_before, matrix, both, out, fine, wide, left, vector, coarse):
    coarse[...] = kept_before[...]

    @pl.when(lax.axis_index("layer") == step)
    def _():
        ordered(vector, both)
        full = vector[...]
        coarse[...] = combined(times(full, matrix[0]), times(full, matrix[1]))

    lifted(smoothed, coarse[...], out, fine, wide, left)


def lift(smoothed, kept, step=None, *operands):
    shots, _, depth, height, width = smoothed.shape
    lines, cells = kept.shape
    scratch = [
        pltpu.VMEM((2 * shots, depth, height, width), f32),
        pltpu.VMEM((height // QY * lines, width), f32),
        pltpu.SemaphoreType.DMA((2 * shots,)),
    ]
    kernel = lift_kernel
    if operands:
        columns = operands[1].shape[0]
        kernel = functools.partial(last_kernel, step)
        scratch += [pltpu.VMEM((lines, 2 * columns * cells), bf16), pltpu.VMEM((lines, cells), f32)]
    return pl.pallas_call(
        kernel,
        out_shape=pltpu.HBM(smoothed.shape, f32),
        in_specs=[pl.BlockSpec(memory_space=VMEM)] * (2 + len(operands)),
        out_specs=pl.BlockSpec(memory_space=pltpu.HBM),
        scratch_shapes=scratch,
        compiler_params=limit(6),
        name="lift",
    )(smoothed, kept, *operands)


def pack_planes_kernel(residual, wavenumber, first, last):
    shots, _, depth, height, width = residual.shape
    for out, base in ((first, 0), (last, depth - HALO)):
        for plane in range(HALO):
            for shot in range(shots):
                for part in range(2):
                    out[2 * shot + part, plane] = residual[shot, part, base + plane].astype(bf16)
            out[2 * shots, plane] = wavenumber[base + plane].astype(bf16)


def pack_planes(residual, wavenumber):
    shots, _, _, height, width = residual.shape
    shape = jax.ShapeDtypeStruct((2 * shots + 1, HALO, height, width), bf16)
    return pl.pallas_call(
        pack_planes_kernel, out_shape=(shape, shape), compiler_params=limit(10), name="pack_planes"
    )(residual, wavenumber)


def pack_rows_kernel(residual, wavenumber, below, above, first, last):
    shots, _, depth, height, width = residual.shape
    for out, base in ((first, 0), (last, height - ROWS)):
        rows = slice(base, base + ROWS)
        for field in range(2 * shots + 1):
            for plane in range(HALO):
                out[field, plane] = below[field, plane, rows, :]
                out[field, HALO + depth + plane] = above[field, plane, rows, :]
            for plane in range(depth):
                own = wavenumber[plane, rows, :] if field == 2 * shots else residual[field // 2, field % 2, plane, rows, :]
                out[field, HALO + plane] = own.astype(bf16)


def pack_rows(residual, wavenumber, below, above):
    shots, _, depth, _, width = residual.shape
    shape = jax.ShapeDtypeStruct((2 * shots + 1, depth + 2 * HALO, ROWS, width), bf16)
    return pl.pallas_call(
        pack_rows_kernel, out_shape=(shape, shape), compiler_params=limit(10), name="pack_rows"
    )(residual, wavenumber, below, above)


def both_ways(low_block, high_block, axis, lowest=0):
    up = [(i, i + 1) for i in range(lowest, lax.axis_size(axis) - 1)]
    return lax.ppermute(high_block, axis, up), lax.ppermute(low_block, axis, [(b, a) for a, b in up])


def every_layer(residual, wavenumber, inverse):
    layers, devices = lax.axis_size("layer"), lax.axis_size("row")
    layer, row = lax.axis_index("layer"), lax.axis_index("row")
    inside = jnp.stack([layer > 0, layer < layers - 1, row > 0, row < devices - 1]).astype(f32)
    matrix = pltpu.with_memory_space_constraint(inverse[:, 0], pltpu.HBM)
    columns = devices // 2

    rhs, spread = restrict(residual, devices)

    def early(residual, wavenumber, rhs):
        first, last = pack_planes(residual, wavenumber)
        below, above = both_ways(first, last, "layer", 1)
        next_rhs = lax.ppermute(rhs, "layer", [(i + 1, i) for i in range(1, layers - 1, 2)])
        ways = [(i, i ^ 1) for i in range(devices)]
        return below, above, next_rhs, lax.ppermute(rhs, "row", ways)

    def nothing(residual, wavenumber, rhs):
        planes = jnp.zeros((2 * residual.shape[0] + 1, HALO, *residual.shape[3:]), bf16)
        return planes, planes, rhs, rhs

    below, above, next_rhs, far_rhs = lax.cond(layer > 0, early, nothing, residual, wavenumber, rhs)

    gathered = lax.cond(
        layer == 0,
        lambda blocks: lax.all_to_all(blocks, "row", 0, 0, tiled=True),
        lambda blocks: blocks,
        spread,
    )
    kept = solve_first(matrix, gathered)

    ends = [[2 * column + end for column in range(columns)] for end in range(2)]

    def gather(blocks):
        return lax.all_to_all(blocks, "row", 0, 0, axis_index_groups=ends, tiled=True)

    def swap(step, block):
        found = []
        for flip in (1, 0):
            way = [
                (i * devices + j, (i ^ (step - 1) ^ step) * devices + (j ^ flip))
                for i in range(layers)
                for j in range(devices)
            ]
            found.append(lax.ppermute(block, ("layer", "row"), way))
        return found

    def send(step, block):
        found = []
        for flip in (1, 0):
            way = [((step - 1) * devices + j, step * devices + (j ^ flip)) for j in range(devices)]
            found.append(lax.ppermute(block, ("layer", "row"), way))
        return found

    def held(step):
        return hold(step, matrix)

    def to_odd(step, kept):
        far, near = swap(step, kept)
        return gather(meet(near, far, rhs, far_rhs, columns))

    def odd_step(step, kept):
        own = held(step)
        return tuple(solve_odd(step, own, to_odd(step, kept), next_rhs, kept))

    middle = layers // 2
    for step in range(1, layers - 1):
        takes_part = (layer == step - 1) | (layer == step)
        if step % 2:
            kept, spread = lax.cond(
                takes_part,
                lambda kept, spread, step=step: odd_step(step, kept),
                lambda kept, spread: (kept, spread),
                kept,
                spread[:columns] if step == 1 else spread,
            )
            continue
        half = lax.cond(layer == step - 1, gather, lambda blocks: blocks, spread)
        if step == middle:
            other, same = send(step, half)
            kept = solve_even(step, held(step), same, other, kept)
            continue

        def even_step(half, kept, step=step):
            own = held(step)
            other, same = swap(step, half)
            return solve_even(step, own, same, other, kept)

        kept = lax.cond(takes_part, even_step, lambda half, kept: kept, half, kept)

    first, last = pack_planes(residual, wavenumber)
    below = jnp.where(layer == 1, lax.ppermute(last, "layer", [(0, 1)]), below)
    above = jnp.where(layer == 0, lax.ppermute(first, "layer", [(1, 0)]), above)
    first, last = pack_rows(residual, wavenumber, below, above)
    row_low, row_high = both_ways(first, last, "row")
    smoothed = smooth(inside, residual, wavenumber, row_low, row_high, below, above)

    step = layers - 1

    def finish(smoothed, kept):
        own = held(step)
        both = to_odd(step, kept)
        return lift(smoothed, kept, step, own, both)

    return lax.cond(layer >= step - 1, finish, lambda smoothed, kept: lift(smoothed, kept), smoothed, kept)


def solution(mesh):
    return jax.shard_map(
        every_layer,
        mesh=mesh,
        in_specs=(
            P(None, None, "layer", "row", None),
            P("layer", "row", None),
            P(None, "layer", "row", None),
        ),
        out_specs=P(None, None, "layer", "row", None),
        check_vma=False,
    )
```

```python
import functools

import jax
import jax.numpy as jnp
from jax import lax
from jax.experimental import pallas as pl
from jax.experimental.pallas import tpu as pltpu
from jax.sharding import PartitionSpec as P


QY = 16
PX = 4
SWEEPS = 4
HALO = SWEEPS - 1
ROWS = 8
LANES = 256

damping = 0.8
absorb = 0.5
coupling = 0.45

VMEM = pltpu.VMEM
f32 = jnp.float32
bf16 = jnp.bfloat16


def limit(mebibytes):
    return pltpu.CompilerParams(vmem_limit_bytes=mebibytes << 20)


def fast(array):
    return pltpu.with_memory_space_constraint(array, VMEM)


def membership(fine, coarse):
    row = lax.broadcasted_iota(jnp.int32, (fine, coarse), 0)
    col = lax.broadcasted_iota(jnp.int32, (fine, coarse), 1)
    return jnp.where((row >= col * PX) & (row < col * PX + PX), 1.0, 0.0).astype(bf16)


def exact_dot(values, selection, contract):
    first = values.astype(bf16)
    rest = values - first.astype(f32)
    second = rest.astype(bf16)
    third = (rest - second.astype(f32)).astype(bf16)
    total = None
    for piece in (third, second, first):
        part = lax.dot_general(piece, selection, (((1,), (contract,)), ((), ())), preferred_element_type=f32)
        total = part if total is None else total + part
    return total


def restrict_kernel(residual, rhs, spread):
    shots, _, depth, height, width = residual.shape
    strips, across = height // QY, width // PX
    sums = []
    for strip in range(strips):
        for part in range(2):
            for shot in range(shots):
                total = residual[shot, part, 0, strip * QY : (strip + 1) * QY, :]
                for plane in range(1, depth):
                    total = total + residual[shot, part, plane, strip * QY : (strip + 1) * QY, :]
                sums.append(jnp.sum(total, axis=0, keepdims=True))
    means = exact_dot(jnp.concatenate(sums, axis=0), membership(width, across), 0) * (1.0 / (depth * QY * PX))
    lines = 2 * shots
    for strip in range(strips):
        rhs[:, strip * across : (strip + 1) * across] = means[strip * lines : (strip + 1) * lines, :]
    vector = rhs[...].astype(bf16)
    for device in range(spread.shape[0]):
        spread[device] = vector


def restrict(residual, devices):
    shots, _, _, height, width = residual.shape
    cells = (height // QY) * (width // PX)
    return pl.pallas_call(
        restrict_kernel,
        out_shape=(
            pltpu.VMEM((2 * shots, cells), f32),
            pltpu.VMEM((devices, 2 * shots, cells), bf16),
        ),
        out_specs=[pl.BlockSpec(memory_space=VMEM)] * 2,
        compiler_params=limit(8),
        name="restrict",
    )(residual)


def hold_kernel(step, matrix, held, arrived):
    @pl.when(lax.axis_index("layer") == step)
    def _():
        copy = pltpu.make_async_copy(matrix, held, arrived)
        copy.start()
        copy.wait()


def hold(step, matrix):
    return pl.pallas_call(
        functools.partial(hold_kernel, step),
        out_shape=pltpu.VMEM(matrix.shape, matrix.dtype),
        in_specs=[pl.BlockSpec(memory_space=pltpu.HBM)],
        out_specs=pl.BlockSpec(memory_space=VMEM),
        scratch_shapes=[pltpu.SemaphoreType.DMA],
        compiler_params=limit(1),
        name="hold",
    )(matrix)


def ordered(vector, both):
    columns, lines, cells = both.shape
    half = lines // 2
    first_end = lax.axis_index("row") % 2 == 0
    for column in range(columns):
        own, far = both[column, :half], both[column, half:]
        at = 2 * column * cells
        vector[:, at : at + cells] = jnp.where(first_end, own, far)
        vector[:, at + cells : at + 2 * cells] = jnp.where(first_end, far, own)


def ordered_two(vector, same, other):
    columns, _, cells = same.shape
    first_end = lax.axis_index("row") % 2 == 0
    for column in range(columns):
        own, far = same[column], other[column]
        at = 2 * column * cells
        vector[:, at : at + cells] = jnp.where(first_end, own, far)
        vector[:, at + cells : at + 2 * cells] = jnp.where(first_end, far, own)


def combined(by_re, by_im):
    shots = by_re.shape[0] // 2
    return jnp.concatenate([by_re[:shots] - by_im[shots:], by_re[shots:] + by_im[:shots]], axis=0)


def hand_on(solved, next_rhs, spread):
    out = (next_rhs[...] + coupling * solved).astype(bf16)
    for column in range(spread.shape[0]):
        spread[column] = out


def times(part, rows):
    return lax.dot_general(part, rows, (((1,), (1,)), ((), ())), preferred_element_type=f32)


def first_kernel(matrix, gathered, solved, held, vector, arrived):
    devices, _, cells = gathered.shape
    pieces = arrived.shape[0]
    across = matrix.shape[2] // pieces
    columns = [slice(piece * across, (piece + 1) * across) for piece in range(pieces)]
    copies = [
        pltpu.make_async_copy(matrix.at[:, :, columns[piece]], held.at[:, :, columns[piece]], arrived.at[piece])
        for piece in range(pieces)
    ]
    for copy in copies:
        copy.start()
    for device in range(devices):
        vector[:, device * cells : (device + 1) * cells] = gathered[device]
    by = [None, None]
    for piece in range(pieces):
        part = vector[:, columns[piece]]
        copies[piece].wait()
        for side in range(2):
            product = times(part, held[side, :, columns[piece]])
            by[side] = product if by[side] is None else by[side] + product
    solved[...] = combined(by[0], by[1])


def solve_first(matrix, gathered):
    devices, lines, cells = gathered.shape
    pieces = 6
    return pl.pallas_call(
        first_kernel,
        out_shape=pltpu.VMEM((lines, cells), f32),
        in_specs=[pl.BlockSpec(memory_space=pltpu.HBM), pl.BlockSpec(memory_space=VMEM)],
        out_specs=pl.BlockSpec(memory_space=VMEM),
        scratch_shapes=[
            pltpu.VMEM(matrix.shape, bf16),
            pltpu.VMEM((lines, devices * cells), bf16),
            pltpu.SemaphoreType.DMA((pieces,)),
        ],
        compiler_params=limit(8),
        cost_estimate=pl.CostEstimate(flops=4 * matrix.size, bytes_accessed=2 * matrix.size, transcendentals=0),
        name="solve_first",
    )(matrix, fast(gathered))


def meet_kernel(near, far, rhs, far_rhs, spread):
    lines = rhs.shape[0]
    own = (rhs[...] + coupling * near[...]).astype(bf16)
    partner = (far_rhs[...] + coupling * far[...]).astype(bf16)
    for column in range(spread.shape[0]):
        spread[column, :lines] = own
        spread[column, lines:] = partner


def meet(near, far, rhs, far_rhs, columns):
    lines, cells = rhs.shape
    return pl.pallas_call(
        meet_kernel,
        out_shape=pltpu.VMEM((columns, 2 * lines, cells), bf16),
        in_specs=[pl.BlockSpec(memory_space=VMEM)] * 4,
        out_specs=pl.BlockSpec(memory_space=VMEM),
        compiler_params=limit(2),
        name="meet",
    )(fast(near), fast(far), fast(rhs), fast(far_rhs))


def odd_kernel(step, matrix, both, next_rhs, kept_before, kept, spread, vector):
    ordered(vector, both)
    full = vector[...]
    solved = combined(times(full, matrix[0]), times(full, matrix[1]))
    kept[...] = jnp.where(lax.axis_index("layer") == step, solved, kept_before[...])
    hand_on(solved, next_rhs, spread)


def solve_odd(step, matrix, both, next_rhs, kept):
    columns, lines, cells = both.shape
    return pl.pallas_call(
        functools.partial(odd_kernel, step),
        out_shape=(
            pltpu.VMEM((lines // 2, cells), f32),
            pltpu.VMEM((columns, lines // 2, cells), bf16),
        ),
        in_specs=[pl.BlockSpec(memory_space=VMEM)] * 4,
        out_specs=[pl.BlockSpec(memory_space=VMEM)] * 2,
        scratch_shapes=[pltpu.VMEM((lines // 2, 2 * columns * cells), bf16)],
        compiler_params=limit(3),
        cost_estimate=pl.CostEstimate(flops=4 * matrix.size, bytes_accessed=2 * matrix.size, transcendentals=0),
        name="solve_odd",
    )(matrix, fast(both), fast(next_rhs), fast(kept))


def even_kernel(step, matrix, same, other, kept_before, kept, vector):
    ordered_two(vector, same, other)
    full = vector[...]
    solved = combined(times(full, matrix[0]), times(full, matrix[1]))
    kept[...] = jnp.where(lax.axis_index("layer") == step, solved, kept_before[...])


def solve_even(step, matrix, same, other, kept):
    columns, lines, cells = same.shape
    return pl.pallas_call(
        functools.partial(even_kernel, step),
        out_shape=pltpu.VMEM((lines, cells), f32),
        in_specs=[pl.BlockSpec(memory_space=VMEM)] * 4,
        out_specs=pl.BlockSpec(memory_space=VMEM),
        scratch_shapes=[pltpu.VMEM((lines, 2 * columns * cells), bf16)],
        compiler_params=limit(3),
        cost_estimate=pl.CostEstimate(flops=4 * matrix.size, bytes_accessed=2 * matrix.size, transcendentals=0),
        name="solve_even",
    )(matrix, fast(same), fast(other), fast(kept))


def smooth_kernel(inside, residual, wavenumber, row_low, row_high, deep_low, deep_high, smoothed, gain, source, first, second):
    shots, _, depth, height, width = residual.shape
    top = ROWS
    start = top + ROWS
    total = height + 2 * ROWS
    planes = depth + 2 * HALO
    rest = LANES - width
    sides = (
        (0, HALO, deep_low, inside[0]),
        (HALO + depth, HALO, deep_high, inside[1]),
    )

    def gains(values, factor):
        real_part = 6.0 - values
        imag_part = -absorb * values
        scale = damping * factor / (real_part * real_part + imag_part * imag_part)
        return real_part * scale, -imag_part * scale

    def put_gain(plane, row, values, factor):
        real_part, imag_part = gains(values, factor)
        rows = values.shape[0]
        gain[0, plane, pl.ds(row, rows), 0:width] = real_part
        gain[1, plane, pl.ds(row, rows), 0:width] = imag_part

    blank = jnp.zeros((total, rest), f32)

    def clear(plane, _):
        for part in range(2):
            gain[part, plane, top : top + total, width:LANES] = blank
            source[part, plane, top : top + total, width:LANES] = blank
        return _

    lax.fori_loop(0, planes, clear, 0)

    def own_gain(plane, _):
        for row in range(0, height, 16):
            put_gain(HALO + plane, start + row, wavenumber[plane, row : row + 16, :], 1.0)
        return _

    lax.fori_loop(0, depth, own_gain, 0)
    for base, count, ghost, factor in sides:
        for plane in range(count):
            for row in range(0, height, 16):
                put_gain(base + plane, start + row, ghost[2 * shots, plane, row : row + 16, :].astype(f32), factor)
    for base, count, factor in ((0, HALO, inside[0]), (HALO, depth, 1.0), (HALO + depth, HALO, inside[1])):

        def row_gain(plane, _, factor=factor):
            put_gain(plane, top, row_low[2 * shots, plane].astype(f32), factor * inside[2])
            put_gain(plane, start + height, row_high[2 * shots, plane].astype(f32), factor * inside[3])
            return _

        lax.fori_loop(base, base + count, row_gain, 0)

    def sweep(old, plane, row, rows, store):
        here = pl.ds(row, rows)
        terms = []
        for part in range(2):
            centre = old[part, plane, here, :]
            beside = old[part, plane - 1, here, :] + old[part, plane + 1, here, :]
            beside = beside + old[part, plane, pl.ds(row - 1, rows), :] + old[part, plane, pl.ds(row + 1, rows), :]
            beside = beside + pltpu.roll(centre, 1, 1) + pltpu.roll(centre, LANES - 1, 1)
            terms.append((centre, source[part, plane, here, :] + beside))
        (centre_re, sum_re), (centre_im, sum_im) = terms
        gain_re, gain_im = gain[0, plane, here, :], gain[1, plane, here, :]
        store(0, (1.0 - damping) * centre_re + (gain_re * sum_re - gain_im * sum_im))
        store(1, (1.0 - damping) * centre_im + (gain_re * sum_im + gain_im * sum_re))

    for shot in range(shots):

        def own_source(plane, _):
            for part in range(2):
                source[part, HALO + plane, start : start + height, 0:width] = residual[shot, part, plane]
            return _

        def row_source(plane, _):
            for part in range(2):
                source[part, plane, top:start, 0:width] = row_low[2 * shot + part, plane].astype(f32)
                source[part, plane, start + height : start + height + ROWS, 0:width] = row_high[
                    2 * shot + part, plane
                ].astype(f32)
            return _

        lax.fori_loop(0, depth, own_source, 0)
        lax.fori_loop(0, planes, row_source, 0)
        for base, count, ghost, _ in sides:
            for plane in range(count):
                for part in range(2):
                    source[part, base + plane, start : start + height, 0:width] = ghost[2 * shot + part, plane].astype(f32)

        def begin(plane, _):
            for row in range(top, top + total, 16):
                here = pl.ds(row, 16)
                gain_re, gain_im = gain[0, plane, here, :], gain[1, plane, here, :]
                source_re, source_im = source[0, plane, here, :], source[1, plane, here, :]
                first[0, plane, here, :] = gain_re * source_re - gain_im * source_im
                first[1, plane, here, :] = gain_re * source_im + gain_im * source_re
            return _

        lax.fori_loop(0, planes, begin, 0)
        old, new = first, second
        for counter in range(1, SWEEPS):
            last = counter == SWEEPS - 1

            def one_plane(plane, _, old=old, new=new, last=last, shot=shot):
                low, high = (start, start + height) if last else (top, top + total)
                for row in range(low, high, 16):

                    def store(part, value, row=row):
                        if last:
                            smoothed[shot, part, plane - HALO, row - start : row - start + 16, :] = value[:, :width]
                        else:
                            new[part, plane, pl.ds(row, 16), :] = value

                    sweep(old, plane, row, 16, store)
                return _

            lax.fori_loop(counter, planes - counter, one_plane, 0)
            old, new = new, old


def smooth(inside, residual, wavenumber, row_low, row_high, deep_low, deep_high):
    shots, _, depth, height, width = residual.shape
    scratch = pltpu.VMEM((2, depth + 2 * HALO, height + 4 * ROWS, LANES), f32)
    return pl.pallas_call(
        smooth_kernel,
        out_shape=jax.ShapeDtypeStruct(residual.shape, f32),
        in_specs=[pl.BlockSpec(memory_space=pltpu.SMEM)] + [pl.BlockSpec(memory_space=VMEM)] * 6,
        scratch_shapes=[scratch] * 4,
        cost_estimate=pl.CostEstimate(flops=300 * residual.size, bytes_accessed=12 * residual.size, transcendentals=0),
        compiler_params=limit(28),
        name="smooth",
    )(inside, residual, wavenumber, row_low, row_high, deep_low, deep_high)


def lifted(smoothed, values, out, fine, wide, left):
    shots, _, depth, height, width = smoothed.shape
    strips, across = height // QY, width // PX
    blocks = [(shot, part) for part in range(2) for shot in range(shots)]
    goes = [pltpu.make_async_copy(fine.at[at], out.at[block], left.at[at]) for at, block in enumerate(blocks)]
    lines = [values[:, strip * across : (strip + 1) * across] for strip in range(strips)]
    wide[...] = exact_dot(jnp.concatenate(lines, axis=0), membership(width, across), 1)
    for at, (shot, part) in enumerate(blocks):
        for strip in range(strips):
            line = strip * 2 * shots + at
            value = jnp.broadcast_to(wide[line : line + 1, :], (QY, width))
            for plane in range(depth):
                rows = slice(strip * QY, (strip + 1) * QY)
                fine[at, plane, rows, :] = smoothed[shot, part, plane, rows, :] + value
        goes[at].start()
    for copy in goes:
        copy.wait()


def lift_kernel(smoothed, coarse, out, fine, wide, left):
    lifted(smoothed, coarse[...], out, fine, wide, left)


def last_kernel(step, smoothed, kept_before, matrix, both, out, fine, wide, left, vector, coarse):
    coarse[...] = kept_before[...]

    @pl.when(lax.axis_index("layer") == step)
    def _():
        ordered(vector, both)
        full = vector[...]
        coarse[...] = combined(times(full, matrix[0]), times(full, matrix[1]))

    lifted(smoothed, coarse[...], out, fine, wide, left)


def lift(smoothed, kept, step=None, *operands):
    shots, _, depth, height, width = smoothed.shape
    lines, cells = kept.shape
    scratch = [
        pltpu.VMEM((2 * shots, depth, height, width), f32),
        pltpu.VMEM((height // QY * lines, width), f32),
        pltpu.SemaphoreType.DMA((2 * shots,)),
    ]
    kernel = lift_kernel
    if operands:
        columns = operands[1].shape[0]
        kernel = functools.partial(last_kernel, step)
        scratch += [pltpu.VMEM((lines, 2 * columns * cells), bf16), pltpu.VMEM((lines, cells), f32)]
    return pl.pallas_call(
        kernel,
        out_shape=pltpu.HBM(smoothed.shape, f32),
        in_specs=[pl.BlockSpec(memory_space=VMEM)] * (2 + len(operands)),
        out_specs=pl.BlockSpec(memory_space=pltpu.HBM),
        scratch_shapes=scratch,
        compiler_params=limit(6),
        name="lift",
    )(smoothed, fast(kept), *operands)


def pack_planes_kernel(residual, wavenumber, first, last):
    shots, _, depth, height, width = residual.shape
    for out, base in ((first, 0), (last, depth - HALO)):
        for plane in range(HALO):
            for shot in range(shots):
                for part in range(2):
                    out[2 * shot + part, plane] = residual[shot, part, base + plane].astype(bf16)
            out[2 * shots, plane] = wavenumber[base + plane].astype(bf16)


def pack_planes(residual, wavenumber):
    shots, _, _, height, width = residual.shape
    shape = jax.ShapeDtypeStruct((2 * shots + 1, HALO, height, width), bf16)
    return pl.pallas_call(
        pack_planes_kernel, out_shape=(shape, shape), compiler_params=limit(10), name="pack_planes"
    )(residual, wavenumber)


def pack_rows_kernel(residual, wavenumber, below, above, first, last):
    shots, _, depth, height, width = residual.shape
    for out, base in ((first, 0), (last, height - ROWS)):
        rows = slice(base, base + ROWS)
        for field in range(2 * shots + 1):
            for plane in range(HALO):
                out[field, plane] = below[field, plane, rows, :]
                out[field, HALO + depth + plane] = above[field, plane, rows, :]
            for plane in range(depth):
                own = wavenumber[plane, rows, :] if field == 2 * shots else residual[field // 2, field % 2, plane, rows, :]
                out[field, HALO + plane] = own.astype(bf16)


def pack_rows(residual, wavenumber, below, above):
    shots, _, depth, _, width = residual.shape
    shape = jax.ShapeDtypeStruct((2 * shots + 1, depth + 2 * HALO, ROWS, width), bf16)
    return pl.pallas_call(
        pack_rows_kernel, out_shape=(shape, shape), compiler_params=limit(10), name="pack_rows"
    )(residual, wavenumber, below, above)


def both_ways(low_block, high_block, axis, lowest=0):
    up = [(i, i + 1) for i in range(lowest, lax.axis_size(axis) - 1)]
    return lax.ppermute(high_block, axis, up), lax.ppermute(low_block, axis, [(b, a) for a, b in up])


def every_layer(residual, wavenumber, inverse):
    layers, devices = lax.axis_size("layer"), lax.axis_size("row")
    layer, row = lax.axis_index("layer"), lax.axis_index("row")
    inside = jnp.stack([layer > 0, layer < layers - 1, row > 0, row < devices - 1]).astype(f32)
    matrix = pltpu.with_memory_space_constraint(inverse[:, 0], pltpu.HBM)
    columns = devices // 2

    rhs, spread = restrict(residual, devices)

    def early(rhs):
        next_rhs = lax.ppermute(rhs, "layer", [(i + 1, i) for i in range(1, layers - 1, 2)])
        ways = [(i, i ^ 1) for i in range(devices)]
        return next_rhs, lax.ppermute(rhs, "row", ways)

    next_rhs, far_rhs = lax.cond(layer > 0, early, lambda rhs: (rhs, rhs), rhs)

    gathered = lax.cond(
        layer == 0,
        lambda blocks: lax.all_to_all(blocks, "row", 0, 0, tiled=True),
        lambda blocks: blocks,
        spread,
    )
    kept = solve_first(matrix, gathered)

    ends = [[2 * column + end for column in range(columns)] for end in range(2)]

    def gather(blocks):
        return lax.all_to_all(blocks, "row", 0, 0, axis_index_groups=ends, tiled=True)

    def swap(step, block):
        found = []
        for flip in (1, 0):
            way = [
                (i * devices + j, (i ^ (step - 1) ^ step) * devices + (j ^ flip))
                for i in range(layers)
                for j in range(devices)
            ]
            found.append(lax.ppermute(block, ("layer", "row"), way))
        return found

    def send(step, block):
        found = []
        for flip in (1, 0):
            way = [((step - 1) * devices + j, step * devices + (j ^ flip)) for j in range(devices)]
            found.append(lax.ppermute(block, ("layer", "row"), way))
        return found

    def held(step):
        return hold(step, matrix)

    def to_odd(step, kept):
        far, near = swap(step, kept)
        return gather(meet(near, far, rhs, far_rhs, columns))

    def odd_step(step, kept):
        own = held(step)
        return tuple(solve_odd(step, own, to_odd(step, kept), next_rhs, kept))

    open_hops = (2, layers // 2)
    for step in range(1, layers - 1):
        takes_part = (layer == step - 1) | (layer == step)
        if step % 2:
            kept, spread = lax.cond(
                takes_part,
                lambda kept, spread, step=step: odd_step(step, kept),
                lambda kept, spread: (kept, spread),
                kept,
                spread[:columns] if step == 1 else spread,
            )
            continue
        half = lax.cond(layer == step - 1, gather, lambda blocks: blocks, spread)
        if step in open_hops:
            other, same = send(step, half)
            kept = solve_even(step, held(step), same, other, kept)
            continue

        def even_step(half, kept, step=step):
            own = held(step)
            other, same = swap(step, half)
            return solve_even(step, own, same, other, kept)

        kept = lax.cond(takes_part, even_step, lambda half, kept: kept, half, kept)

    def planes_of(first, last, pairs):
        back = [(high, low) for low, high in pairs]
        return lax.ppermute(last, "layer", pairs), lax.ppermute(first, "layer", back)

    first, last = pack_planes(residual, wavenumber)
    pairs = [(i, i + 1) for i in range(layers - 1) if i != 1]
    below, above = planes_of(first, last, pairs)
    late_below, late_above = planes_of(first, last, [(1, 2)])
    below = jnp.where(layer == 2, late_below, below)
    above = jnp.where(layer == 1, late_above, above)
    first, last = pack_rows(residual, wavenumber, below, above)
    row_low, row_high = both_ways(first, last, "row")
    smoothed = smooth(inside, residual, wavenumber, row_low, row_high, below, above)

    step = layers - 1

    def finish(smoothed, kept):
        own = held(step)
        both = to_odd(step, kept)
        return lift(smoothed, kept, step, own, both)

    return lax.cond(layer >= step - 1, finish, lambda smoothed, kept: lift(smoothed, kept), smoothed, kept)


def solution(mesh):
    return jax.shard_map(
        every_layer,
        mesh=mesh,
        in_specs=(
            P(None, None, "layer", "row", None),
            P("layer", "row", None),
            P(None, "layer", "row", None),
        ),
        out_specs=P(None, None, "layer", "row", None),
        check_vma=False,
    )
```

```python
import functools

import jax
import jax.numpy as jnp
from jax import lax
from jax.experimental import pallas as pl
from jax.experimental.pallas import tpu as pltpu
from jax.sharding import PartitionSpec as P


QY = 16
PX = 4
SWEEPS = 4
HALO = SWEEPS - 1
ROWS = 8
LANES = 256

damping = 0.8
absorb = 0.5
coupling = 0.45

VMEM = pltpu.VMEM
f32 = jnp.float32
bf16 = jnp.bfloat16


def limit(mebibytes):
    return pltpu.CompilerParams(vmem_limit_bytes=mebibytes << 20)


def membership(fine, coarse):
    row = lax.broadcasted_iota(jnp.int32, (fine, coarse), 0)
    col = lax.broadcasted_iota(jnp.int32, (fine, coarse), 1)
    return jnp.where((row >= col * PX) & (row < col * PX + PX), 1.0, 0.0).astype(bf16)


def exact_dot(values, selection, contract):
    first = values.astype(bf16)
    rest = values - first.astype(f32)
    second = rest.astype(bf16)
    third = (rest - second.astype(f32)).astype(bf16)
    total = None
    for piece in (third, second, first):
        part = lax.dot_general(piece, selection, (((1,), (contract,)), ((), ())), preferred_element_type=f32)
        total = part if total is None else total + part
    return total


def restrict_kernel(residual, rhs, spread):
    shots, _, depth, height, width = residual.shape
    strips, across = height // QY, width // PX
    sums = []
    for strip in range(strips):
        for part in range(2):
            for shot in range(shots):
                total = residual[shot, part, 0, strip * QY : (strip + 1) * QY, :]
                for plane in range(1, depth):
                    total = total + residual[shot, part, plane, strip * QY : (strip + 1) * QY, :]
                sums.append(jnp.sum(total, axis=0, keepdims=True))
    means = exact_dot(jnp.concatenate(sums, axis=0), membership(width, across), 0) * (1.0 / (depth * QY * PX))
    lines = 2 * shots
    for strip in range(strips):
        rhs[:, strip * across : (strip + 1) * across] = means[strip * lines : (strip + 1) * lines, :]
    vector = rhs[...].astype(bf16)
    for device in range(spread.shape[0]):
        spread[device] = vector


def restrict(residual, devices):
    shots, _, _, height, width = residual.shape
    cells = (height // QY) * (width // PX)
    return pl.pallas_call(
        restrict_kernel,
        out_shape=(
            jax.ShapeDtypeStruct((2 * shots, cells), f32),
            jax.ShapeDtypeStruct((devices, 2 * shots, cells), bf16),
        ),
        compiler_params=limit(8),
        name="restrict",
    )(residual)


def hold_kernel(step, matrix, held, arrived):
    @pl.when(lax.axis_index("layer") == step)
    def _():
        copy = pltpu.make_async_copy(matrix, held, arrived)
        copy.start()
        copy.wait()


def hold(step, matrix):
    return pl.pallas_call(
        functools.partial(hold_kernel, step),
        out_shape=pltpu.VMEM(matrix.shape, matrix.dtype),
        in_specs=[pl.BlockSpec(memory_space=pltpu.HBM)],
        out_specs=pl.BlockSpec(memory_space=VMEM),
        scratch_shapes=[pltpu.SemaphoreType.DMA],
        compiler_params=limit(1),
        name="hold",
    )(matrix)


def ordered(vector, same, other, first_end):
    columns, _, cells = same.shape
    for column in range(columns):
        own, far = same[column], other[column]
        at = 2 * column * cells
        vector[:, at : at + cells] = jnp.where(first_end, own, far)
        vector[:, at + cells : at + 2 * cells] = jnp.where(first_end, far, own)


def combined(by_re, by_im):
    shots = by_re.shape[0] // 2
    return jnp.concatenate([by_re[:shots] - by_im[shots:], by_re[shots:] + by_im[:shots]], axis=0)


def hand_on(solved, next_rhs, spread):
    out = (next_rhs[...] + coupling * solved).astype(bf16)
    for column in range(spread.shape[0]):
        spread[column] = out


def times(part, rows):
    return lax.dot_general(part, rows, (((1,), (1,)), ((), ())), preferred_element_type=f32)


def first_kernel(matrix, gathered, next_rhs, kept, spread, held, vector, arrived):
    devices, _, cells = gathered.shape
    pieces = arrived.shape[0]
    across = matrix.shape[2] // pieces
    columns = [slice(piece * across, (piece + 1) * across) for piece in range(pieces)]
    copies = [
        pltpu.make_async_copy(matrix.at[:, :, columns[piece]], held.at[:, :, columns[piece]], arrived.at[piece])
        for piece in range(pieces)
    ]
    for copy in copies:
        copy.start()
    for device in range(devices):
        vector[:, device * cells : (device + 1) * cells] = gathered[device]
    by = [None, None]
    for piece in range(pieces):
        part = vector[:, columns[piece]]
        copies[piece].wait()
        for side in range(2):
            product = times(part, held[side, :, columns[piece]])
            by[side] = product if by[side] is None else by[side] + product
    solved = combined(by[0], by[1])
    kept[...] = solved
    hand_on(solved, next_rhs, spread)


def solve_first(matrix, gathered, next_rhs):
    devices, lines, cells = gathered.shape
    pieces = 6
    return pl.pallas_call(
        first_kernel,
        out_shape=(
            jax.ShapeDtypeStruct((lines, cells), f32),
            jax.ShapeDtypeStruct((devices // 2, lines, cells), bf16),
        ),
        in_specs=[pl.BlockSpec(memory_space=pltpu.HBM)] + [pl.BlockSpec(memory_space=VMEM)] * 2,
        scratch_shapes=[
            pltpu.VMEM(matrix.shape, bf16),
            pltpu.VMEM((lines, devices * cells), bf16),
            pltpu.SemaphoreType.DMA((pieces,)),
        ],
        compiler_params=limit(8),
        cost_estimate=pl.CostEstimate(flops=4 * matrix.size, bytes_accessed=2 * matrix.size, transcendentals=0),
        name="solve_first",
    )(matrix, gathered, next_rhs)


def layer_kernel(step, matrix, same, other, next_rhs, kept_before, kept, spread, vector):
    ordered(vector, same, other, lax.axis_index("row") % 2 == 0)
    full = vector[...]
    solved = combined(times(full, matrix[0]), times(full, matrix[1]))
    kept[...] = jnp.where(lax.axis_index("layer") == step, solved, kept_before[...])
    hand_on(solved, next_rhs, spread)


def solve_layer(step, matrix, same, other, next_rhs, kept):
    columns, lines, cells = same.shape
    return pl.pallas_call(
        functools.partial(layer_kernel, step),
        out_shape=(
            jax.ShapeDtypeStruct((lines, cells), f32),
            jax.ShapeDtypeStruct((columns, lines, cells), bf16),
        ),
        in_specs=[pl.BlockSpec(memory_space=VMEM)] * 5,
        scratch_shapes=[pltpu.VMEM((lines, 2 * columns * cells), bf16)],
        compiler_params=limit(3),
        cost_estimate=pl.CostEstimate(flops=4 * matrix.size, bytes_accessed=2 * matrix.size, transcendentals=0),
        name="solve_layer",
    )(matrix, same, other, next_rhs, kept)


def smooth_kernel(inside, residual, wavenumber, row_low, row_high, deep_low, deep_high, smoothed, gain, source, first, second):
    shots, _, depth, height, width = residual.shape
    top = ROWS
    start = top + ROWS
    total = height + 2 * ROWS
    planes = depth + 2 * HALO
    rest = LANES - width
    sides = (
        (0, HALO, deep_low, inside[0]),
        (HALO + depth, HALO, deep_high, inside[1]),
    )

    def gains(values, factor):
        real_part = 6.0 - values
        imag_part = -absorb * values
        scale = damping * factor / (real_part * real_part + imag_part * imag_part)
        return real_part * scale, -imag_part * scale

    def put_gain(plane, row, values, factor):
        real_part, imag_part = gains(values, factor)
        rows = values.shape[0]
        gain[0, plane, pl.ds(row, rows), 0:width] = real_part
        gain[1, plane, pl.ds(row, rows), 0:width] = imag_part

    blank = jnp.zeros((total, rest), f32)

    def clear(plane, _):
        for part in range(2):
            gain[part, plane, top : top + total, width:LANES] = blank
            source[part, plane, top : top + total, width:LANES] = blank
        return _

    lax.fori_loop(0, planes, clear, 0)

    def own_gain(plane, _):
        for row in range(0, height, 16):
            put_gain(HALO + plane, start + row, wavenumber[plane, row : row + 16, :], 1.0)
        return _

    lax.fori_loop(0, depth, own_gain, 0)
    for base, count, ghost, factor in sides:
        for plane in range(count):
            for row in range(0, height, 16):
                put_gain(base + plane, start + row, ghost[2 * shots, plane, row : row + 16, :].astype(f32), factor)
    for base, count, factor in ((0, HALO, inside[0]), (HALO, depth, 1.0), (HALO + depth, HALO, inside[1])):

        def row_gain(plane, _, factor=factor):
            put_gain(plane, top, row_low[2 * shots, plane].astype(f32), factor * inside[2])
            put_gain(plane, start + height, row_high[2 * shots, plane].astype(f32), factor * inside[3])
            return _

        lax.fori_loop(base, base + count, row_gain, 0)

    def sweep(old, plane, row, rows, store):
        here = pl.ds(row, rows)
        terms = []
        for part in range(2):
            centre = old[part, plane, here, :]
            beside = old[part, plane - 1, here, :] + old[part, plane + 1, here, :]
            beside = beside + old[part, plane, pl.ds(row - 1, rows), :] + old[part, plane, pl.ds(row + 1, rows), :]
            beside = beside + pltpu.roll(centre, 1, 1) + pltpu.roll(centre, LANES - 1, 1)
            terms.append((centre, source[part, plane, here, :] + beside))
        (centre_re, sum_re), (centre_im, sum_im) = terms
        gain_re, gain_im = gain[0, plane, here, :], gain[1, plane, here, :]
        store(0, (1.0 - damping) * centre_re + (gain_re * sum_re - gain_im * sum_im))
        store(1, (1.0 - damping) * centre_im + (gain_re * sum_im + gain_im * sum_re))

    for shot in range(shots):

        def own_source(plane, _):
            for part in range(2):
                source[part, HALO + plane, start : start + height, 0:width] = residual[shot, part, plane]
            return _

        def row_source(plane, _):
            for part in range(2):
                source[part, plane, top:start, 0:width] = row_low[2 * shot + part, plane].astype(f32)
                source[part, plane, start + height : start + height + ROWS, 0:width] = row_high[
                    2 * shot + part, plane
                ].astype(f32)
            return _

        lax.fori_loop(0, depth, own_source, 0)
        lax.fori_loop(0, planes, row_source, 0)
        for base, count, ghost, _ in sides:
            for plane in range(count):
                for part in range(2):
                    source[part, base + plane, start : start + height, 0:width] = ghost[2 * shot + part, plane].astype(f32)

        def begin(plane, _):
            for row in range(top, top + total, 16):
                here = pl.ds(row, 16)
                gain_re, gain_im = gain[0, plane, here, :], gain[1, plane, here, :]
                source_re, source_im = source[0, plane, here, :], source[1, plane, here, :]
                first[0, plane, here, :] = gain_re * source_re - gain_im * source_im
                first[1, plane, here, :] = gain_re * source_im + gain_im * source_re
            return _

        lax.fori_loop(0, planes, begin, 0)
        old, new = first, second
        for counter in range(1, SWEEPS):
            last = counter == SWEEPS - 1

            def one_plane(plane, _, old=old, new=new, last=last, shot=shot):
                low, high = (start, start + height) if last else (top, top + total)
                for row in range(low, high, 16):

                    def store(part, value, row=row):
                        if last:
                            smoothed[shot, part, plane - HALO, row - start : row - start + 16, :] = value[:, :width]
                        else:
                            new[part, plane, pl.ds(row, 16), :] = value

                    sweep(old, plane, row, 16, store)
                return _

            lax.fori_loop(counter, planes - counter, one_plane, 0)
            old, new = new, old


def smooth(inside, residual, wavenumber, row_low, row_high, deep_low, deep_high):
    shots, _, depth, height, width = residual.shape
    scratch = pltpu.VMEM((2, depth + 2 * HALO, height + 4 * ROWS, LANES), f32)
    return pl.pallas_call(
        smooth_kernel,
        out_shape=jax.ShapeDtypeStruct(residual.shape, f32),
        in_specs=[pl.BlockSpec(memory_space=pltpu.SMEM)] + [pl.BlockSpec(memory_space=VMEM)] * 6,
        scratch_shapes=[scratch] * 4,
        cost_estimate=pl.CostEstimate(flops=300 * residual.size, bytes_accessed=12 * residual.size, transcendentals=0),
        compiler_params=limit(28),
        name="smooth",
    )(inside, residual, wavenumber, row_low, row_high, deep_low, deep_high)


def lifted(smoothed, values, out, fine, wide, left):
    shots, _, depth, height, width = smoothed.shape
    strips, across = height // QY, width // PX
    blocks = [(shot, part) for part in range(2) for shot in range(shots)]
    goes = [pltpu.make_async_copy(fine.at[at], out.at[block], left.at[at]) for at, block in enumerate(blocks)]
    lines = [values[:, strip * across : (strip + 1) * across] for strip in range(strips)]
    wide[...] = exact_dot(jnp.concatenate(lines, axis=0), membership(width, across), 1)
    for at, (shot, part) in enumerate(blocks):
        for strip in range(strips):
            line = strip * 2 * shots + at
            value = jnp.broadcast_to(wide[line : line + 1, :], (QY, width))
            for plane in range(depth):
                rows = slice(strip * QY, (strip + 1) * QY)
                fine[at, plane, rows, :] = smoothed[shot, part, plane, rows, :] + value
        goes[at].start()
    for copy in goes:
        copy.wait()


def lift_kernel(smoothed, coarse, out, fine, wide, left):
    lifted(smoothed, coarse[...], out, fine, wide, left)


def last_kernel(step, smoothed, kept_before, matrix, same, other, out, fine, wide, left, vector, coarse):
    coarse[...] = kept_before[...]

    @pl.when(lax.axis_index("layer") == step)
    def _():
        ordered(vector, same, other, lax.axis_index("row") % 2 == 0)
        full = vector[...]
        coarse[...] = combined(times(full, matrix[0]), times(full, matrix[1]))

    lifted(smoothed, coarse[...], out, fine, wide, left)


def lift(smoothed, kept, step=None, *operands):
    shots, _, depth, height, width = smoothed.shape
    lines, cells = kept.shape
    scratch = [
        pltpu.VMEM((2 * shots, depth, height, width), f32),
        pltpu.VMEM((height // QY * lines, width), f32),
        pltpu.SemaphoreType.DMA((2 * shots,)),
    ]
    kernel = lift_kernel
    if operands:
        columns = operands[1].shape[0]
        kernel = functools.partial(last_kernel, step)
        scratch += [pltpu.VMEM((lines, 2 * columns * cells), bf16), pltpu.VMEM((lines, cells), f32)]
    return pl.pallas_call(
        kernel,
        out_shape=pltpu.HBM(smoothed.shape, f32),
        in_specs=[pl.BlockSpec(memory_space=VMEM)] * (2 + len(operands)),
        out_specs=pl.BlockSpec(memory_space=pltpu.HBM),
        scratch_shapes=scratch,
        compiler_params=limit(6),
        name="lift",
    )(smoothed, kept, *operands)


def pack_planes_kernel(residual, wavenumber, first, last):
    shots, _, depth, height, width = residual.shape
    for out, base in ((first, 0), (last, depth - HALO)):
        for plane in range(HALO):
            for shot in range(shots):
                for part in range(2):
                    out[2 * shot + part, plane] = residual[shot, part, base + plane].astype(bf16)
            out[2 * shots, plane] = wavenumber[base + plane].astype(bf16)


def pack_planes(residual, wavenumber):
    shots, _, _, height, width = residual.shape
    shape = jax.ShapeDtypeStruct((2 * shots + 1, HALO, height, width), bf16)
    return pl.pallas_call(
        pack_planes_kernel, out_shape=(shape, shape), compiler_params=limit(10), name="pack_planes"
    )(residual, wavenumber)


def pack_rows_kernel(residual, wavenumber, below, above, first, last):
    shots, _, depth, height, width = residual.shape
    for out, base in ((first, 0), (last, height - ROWS)):
        rows = slice(base, base + ROWS)
        for field in range(2 * shots + 1):
            for plane in range(HALO):
                out[field, plane] = below[field, plane, rows, :]
                out[field, HALO + depth + plane] = above[field, plane, rows, :]
            for plane in range(depth):
                own = wavenumber[plane, rows, :] if field == 2 * shots else residual[field // 2, field % 2, plane, rows, :]
                out[field, HALO + plane] = own.astype(bf16)


def pack_rows(residual, wavenumber, below, above):
    shots, _, depth, _, width = residual.shape
    shape = jax.ShapeDtypeStruct((2 * shots + 1, depth + 2 * HALO, ROWS, width), bf16)
    return pl.pallas_call(
        pack_rows_kernel, out_shape=(shape, shape), compiler_params=limit(10), name="pack_rows"
    )(residual, wavenumber, below, above)


def both_ways(low_block, high_block, axis):
    size = lax.axis_size(axis)
    up = [(i, i + 1) for i in range(size - 1)]
    return lax.ppermute(high_block, axis, up), lax.ppermute(low_block, axis, [(b, a) for a, b in up])


def every_layer(residual, wavenumber, inverse):
    layers, devices = lax.axis_size("layer"), lax.axis_size("row")
    layer, row = lax.axis_index("layer"), lax.axis_index("row")
    inside = jnp.stack([layer > 0, layer < layers - 1, row > 0, row < devices - 1]).astype(f32)

    rhs, spread = restrict(residual, devices)
    next_rhs = lax.ppermute(rhs, "layer", [(i + 1, i) for i in range(layers - 1)])
    matrix = pltpu.with_memory_space_constraint(inverse[:, 0], pltpu.HBM)
    gathered = lax.cond(
        layer == 0,
        lambda blocks: lax.all_to_all(blocks, "row", 0, 0, tiled=True),
        lambda blocks: blocks,
        spread,
    )
    kept, spread = solve_first(matrix, gathered, next_rhs)

    ends = [[2 * column + end for column in range(devices // 2)] for end in range(2)]

    def gather(step, spread):
        return lax.cond(
            layer == step,
            lambda blocks: lax.all_to_all(blocks, "row", 0, 0, axis_index_groups=ends, tiled=True),
            lambda blocks: blocks,
            spread,
        )

    def swap(step, half):
        found = []
        for flip in (1, 0):
            way = [
                (i * devices + j, (i ^ (step - 1) ^ step) * devices + (j ^ flip))
                for i in range(layers)
                for j in range(devices)
            ]
            found.append(lax.ppermute(half, ("layer", "row"), way))
        return found

    def send(step, half):
        found = []
        for flip in (1, 0):
            way = [((step - 1) * devices + j, step * devices + (j ^ flip)) for j in range(devices)]
            found.append(lax.ppermute(half, ("layer", "row"), way))
        return found

    def solve(step, other, same, kept):
        held = hold(step, matrix)
        return solve_layer(step, held, same, other, next_rhs, kept)

    open_hops = (2, layers // 2)
    for step in range(1, layers - 1):
        half = gather(step - 1, spread)
        if step in open_hops:
            kept, spread = solve(step, *send(step, half), kept)
            continue
        kept, spread = lax.cond(
            (layer == step - 1) | (layer == step),
            lambda half, kept, step=step: tuple(solve(step, *swap(step, half), kept)),
            lambda half, kept: (kept, half),
            half,
            kept,
        )

    def planes_of(first, last, pairs):
        back = [(high, low) for low, high in pairs]
        return lax.ppermute(last, "layer", pairs), lax.ppermute(first, "layer", back)

    first, last = pack_planes(residual, wavenumber)
    pairs = [(i, i + 1) for i in range(layers - 1) if i != 1]
    below, above = planes_of(first, last, pairs)
    late_below, late_above = planes_of(first, last, [(1, 2)])
    below = jnp.where(layer == 2, late_below, below)
    above = jnp.where(layer == 1, late_above, above)
    first, last = pack_rows(residual, wavenumber, below, above)
    row_low, row_high = both_ways(first, last, "row")
    smoothed = smooth(inside, residual, wavenumber, row_low, row_high, below, above)

    step = layers - 1
    half = gather(step - 1, spread)

    def finish(half, smoothed, kept):
        other, same = swap(step, half)
        held = hold(step, matrix)
        return lift(smoothed, kept, step, held, same, other)

    return lax.cond(
        layer >= step - 1, finish, lambda half, smoothed, kept: lift(smoothed, kept), half, smoothed, kept
    )


def solution(mesh):
    return jax.shard_map(
        every_layer,
        mesh=mesh,
        in_specs=(
            P(None, None, "layer", "row", None),
            P("layer", "row", None),
            P(None, "layer", "row", None),
        ),
        out_specs=P(None, None, "layer", "row", None),
        check_vma=False,
    )
```

```python
import functools

import jax
import jax.numpy as jnp
from jax import lax
from jax.experimental import pallas as pl
from jax.experimental.pallas import tpu as pltpu
from jax.sharding import PartitionSpec as P


QY = 16
PX = 4
SWEEPS = 4
HALO = SWEEPS - 1
ROWS = 8
SENT = 4
LANES = 256

damping = 0.8
absorb = 0.5
coupling = 0.45

VMEM = pltpu.VMEM
f32 = jnp.float32
bf16 = jnp.bfloat16


def limit(mebibytes):
    return pltpu.CompilerParams(vmem_limit_bytes=mebibytes << 20)


def membership(fine, coarse):
    row = lax.broadcasted_iota(jnp.int32, (fine, coarse), 0)
    col = lax.broadcasted_iota(jnp.int32, (fine, coarse), 1)
    return jnp.where((row >= col * PX) & (row < col * PX + PX), 1.0, 0.0).astype(bf16)


def exact_dot(values, selection, contract):
    first = values.astype(bf16)
    rest = values - first.astype(f32)
    second = rest.astype(bf16)
    third = (rest - second.astype(f32)).astype(bf16)
    total = None
    for piece in (third, second, first):
        part = lax.dot_general(piece, selection, (((1,), (contract,)), ((), ())), preferred_element_type=f32)
        total = part if total is None else total + part
    return total


def restrict_kernel(residual, rhs, spread):
    shots, _, depth, height, width = residual.shape
    strips, across = height // QY, width // PX
    sums = []
    for strip in range(strips):
        for part in range(2):
            for shot in range(shots):
                total = residual[shot, part, 0, strip * QY : (strip + 1) * QY, :]
                for plane in range(1, depth):
                    total = total + residual[shot, part, plane, strip * QY : (strip + 1) * QY, :]
                sums.append(jnp.sum(total, axis=0, keepdims=True))
    means = exact_dot(jnp.concatenate(sums, axis=0), membership(width, across), 0) * (1.0 / (depth * QY * PX))
    lines = 2 * shots
    for strip in range(strips):
        rhs[:, strip * across : (strip + 1) * across] = means[strip * lines : (strip + 1) * lines, :]
    vector = rhs[...].astype(bf16)
    for device in range(spread.shape[0]):
        spread[device] = vector


def restrict(residual, devices):
    shots, _, _, height, width = residual.shape
    cells = (height // QY) * (width // PX)
    return pl.pallas_call(
        restrict_kernel,
        out_shape=(
            jax.ShapeDtypeStruct((2 * shots, cells), f32),
            jax.ShapeDtypeStruct((devices, 2 * shots, cells), bf16),
        ),
        compiler_params=limit(8),
        name="restrict",
    )(residual)


def hold_kernel(step, matrix, held, arrived):
    @pl.when(lax.axis_index("layer") == step)
    def _():
        copy = pltpu.make_async_copy(matrix, held, arrived)
        copy.start()
        copy.wait()


def hold(step, matrix):
    return pl.pallas_call(
        functools.partial(hold_kernel, step),
        out_shape=pltpu.VMEM(matrix.shape, matrix.dtype),
        in_specs=[pl.BlockSpec(memory_space=pltpu.HBM)],
        out_specs=pl.BlockSpec(memory_space=VMEM),
        scratch_shapes=[pltpu.SemaphoreType.DMA],
        compiler_params=limit(1),
        name="hold",
    )(matrix)


def ordered(vector, same, other, first_end):
    columns, _, cells = same.shape
    for column in range(columns):
        own, far = same[column], other[column]
        at = 2 * column * cells
        vector[:, at : at + cells] = jnp.where(first_end, own, far)
        vector[:, at + cells : at + 2 * cells] = jnp.where(first_end, far, own)


def combined(by_re, by_im):
    shots = by_re.shape[0] // 2
    return jnp.concatenate([by_re[:shots] - by_im[shots:], by_re[shots:] + by_im[:shots]], axis=0)


def hand_on(solved, next_rhs, spread):
    out = (next_rhs[...] + coupling * solved).astype(bf16)
    for column in range(spread.shape[0]):
        spread[column] = out


def times(part, rows):
    return lax.dot_general(part, rows, (((1,), (1,)), ((), ())), preferred_element_type=f32)


def first_kernel(matrix, gathered, next_rhs, kept, spread, held, vector, arrived):
    devices, _, cells = gathered.shape
    pieces = arrived.shape[0]
    across = matrix.shape[2] // pieces
    columns = [slice(piece * across, (piece + 1) * across) for piece in range(pieces)]
    copies = [
        pltpu.make_async_copy(matrix.at[:, :, columns[piece]], held.at[:, :, columns[piece]], arrived.at[piece])
        for piece in range(pieces)
    ]
    for copy in copies:
        copy.start()
    for device in range(devices):
        vector[:, device * cells : (device + 1) * cells] = gathered[device]
    by = [None, None]
    for piece in range(pieces):
        part = vector[:, columns[piece]]
        copies[piece].wait()
        for side in range(2):
            product = times(part, held[side, :, columns[piece]])
            by[side] = product if by[side] is None else by[side] + product
    solved = combined(by[0], by[1])
    kept[...] = solved
    hand_on(solved, next_rhs, spread)


def solve_first(matrix, gathered, next_rhs):
    devices, lines, cells = gathered.shape
    pieces = 6
    return pl.pallas_call(
        first_kernel,
        out_shape=(
            jax.ShapeDtypeStruct((lines, cells), f32),
            jax.ShapeDtypeStruct((devices // 2, lines, cells), bf16),
        ),
        in_specs=[pl.BlockSpec(memory_space=pltpu.HBM)] + [pl.BlockSpec(memory_space=VMEM)] * 2,
        scratch_shapes=[
            pltpu.VMEM(matrix.shape, bf16),
            pltpu.VMEM((lines, devices * cells), bf16),
            pltpu.SemaphoreType.DMA((pieces,)),
        ],
        compiler_params=limit(8),
        cost_estimate=pl.CostEstimate(flops=4 * matrix.size, bytes_accessed=2 * matrix.size, transcendentals=0),
        name="solve_first",
    )(matrix, gathered, next_rhs)


def layer_kernel(step, matrix, same, other, next_rhs, kept_before, kept, spread, vector):
    ordered(vector, same, other, lax.axis_index("row") % 2 == 0)
    full = vector[...]
    solved = combined(times(full, matrix[0]), times(full, matrix[1]))
    kept[...] = jnp.where(lax.axis_index("layer") == step, solved, kept_before[...])
    hand_on(solved, next_rhs, spread)


def solve_layer(step, matrix, same, other, next_rhs, kept):
    columns, lines, cells = same.shape
    return pl.pallas_call(
        functools.partial(layer_kernel, step),
        out_shape=(
            jax.ShapeDtypeStruct((lines, cells), f32),
            jax.ShapeDtypeStruct((columns, lines, cells), bf16),
        ),
        in_specs=[pl.BlockSpec(memory_space=VMEM)] * 5,
        scratch_shapes=[pltpu.VMEM((lines, 2 * columns * cells), bf16)],
        compiler_params=limit(3),
        cost_estimate=pl.CostEstimate(flops=4 * matrix.size, bytes_accessed=2 * matrix.size, transcendentals=0),
        name="solve_layer",
    )(matrix, same, other, next_rhs, kept)


def smooth_kernel(inside, residual, wavenumber, row_low, row_high, deep_low, deep_high, smoothed, gain, source, first, second):
    shots, _, depth, height, width = residual.shape
    top = ROWS
    start = top + ROWS
    total = height + 2 * ROWS
    planes = depth + 2 * HALO
    rest = LANES - width
    sides = (
        (0, HALO, deep_low, inside[0]),
        (HALO + depth, HALO, deep_high, inside[1]),
    )

    def gains(values, factor):
        real_part = 6.0 - values
        imag_part = -absorb * values
        scale = damping * factor / (real_part * real_part + imag_part * imag_part)
        return real_part * scale, -imag_part * scale

    def put_gain(plane, row, values, factor):
        real_part, imag_part = gains(values, factor)
        rows = values.shape[0]
        gain[0, plane, pl.ds(row, rows), 0:width] = real_part
        gain[1, plane, pl.ds(row, rows), 0:width] = imag_part

    blank = jnp.zeros((total, rest), f32)

    def clear(plane, _):
        for part in range(2):
            gain[part, plane, top : top + total, width:LANES] = blank
            source[part, plane, top : top + total, width:LANES] = blank
        return _

    lax.fori_loop(0, planes, clear, 0)

    def own_gain(plane, _):
        for row in range(0, height, 16):
            put_gain(HALO + plane, start + row, wavenumber[plane, row : row + 16, :], 1.0)
        return _

    lax.fori_loop(0, depth, own_gain, 0)
    for base, count, ghost, factor in sides:
        for plane in range(count):
            for row in range(0, height, 16):
                put_gain(base + plane, start + row, ghost[2 * shots, plane, row : row + 16, :].astype(f32), factor)
    for base, count, factor in ((0, HALO, inside[0]), (HALO, depth, 1.0), (HALO + depth, HALO, inside[1])):

        def row_gain(plane, _, factor=factor):
            put_gain(plane, start - SENT, row_low[2 * shots, plane].astype(f32), factor * inside[2])
            put_gain(plane, start + height, row_high[2 * shots, plane].astype(f32), factor * inside[3])
            return _

        lax.fori_loop(base, base + count, row_gain, 0)

    def sweep(old, plane, row, rows, store):
        here = pl.ds(row, rows)
        terms = []
        for part in range(2):
            centre = old[part, plane, here, :]
            beside = old[part, plane - 1, here, :] + old[part, plane + 1, here, :]
            beside = beside + old[part, plane, pl.ds(row - 1, rows), :] + old[part, plane, pl.ds(row + 1, rows), :]
            beside = beside + pltpu.roll(centre, 1, 1) + pltpu.roll(centre, LANES - 1, 1)
            terms.append((centre, source[part, plane, here, :] + beside))
        (centre_re, sum_re), (centre_im, sum_im) = terms
        gain_re, gain_im = gain[0, plane, here, :], gain[1, plane, here, :]
        store(0, (1.0 - damping) * centre_re + (gain_re * sum_re - gain_im * sum_im))
        store(1, (1.0 - damping) * centre_im + (gain_re * sum_im + gain_im * sum_re))

    for shot in range(shots):

        def own_source(plane, _):
            for part in range(2):
                source[part, HALO + plane, start : start + height, 0:width] = residual[shot, part, plane]
            return _

        def row_source(plane, _):
            for part in range(2):
                source[part, plane, start - SENT : start, 0:width] = row_low[2 * shot + part, plane].astype(f32)
                source[part, plane, start + height : start + height + SENT, 0:width] = row_high[
                    2 * shot + part, plane
                ].astype(f32)
            return _

        lax.fori_loop(0, depth, own_source, 0)
        lax.fori_loop(0, planes, row_source, 0)
        for base, count, ghost, _ in sides:
            for plane in range(count):
                for part in range(2):
                    source[part, base + plane, start : start + height, 0:width] = ghost[2 * shot + part, plane].astype(f32)

        def begin(plane, _):
            for row in range(top, top + total, 16):
                here = pl.ds(row, 16)
                gain_re, gain_im = gain[0, plane, here, :], gain[1, plane, here, :]
                source_re, source_im = source[0, plane, here, :], source[1, plane, here, :]
                first[0, plane, here, :] = gain_re * source_re - gain_im * source_im
                first[1, plane, here, :] = gain_re * source_im + gain_im * source_re
            return _

        lax.fori_loop(0, planes, begin, 0)
        old, new = first, second
        for counter in range(1, SWEEPS):
            last = counter == SWEEPS - 1

            def one_plane(plane, _, old=old, new=new, last=last, shot=shot):
                low, high = (start, start + height) if last else (top, top + total)
                for row in range(low, high, 16):

                    def store(part, value, row=row):
                        if last:
                            smoothed[shot, part, plane - HALO, row - start : row - start + 16, :] = value[:, :width]
                        else:
                            new[part, plane, pl.ds(row, 16), :] = value

                    sweep(old, plane, row, 16, store)
                return _

            lax.fori_loop(counter, planes - counter, one_plane, 0)
            old, new = new, old


def smooth(inside, residual, wavenumber, row_low, row_high, deep_low, deep_high):
    shots, _, depth, height, width = residual.shape
    scratch = pltpu.VMEM((2, depth + 2 * HALO, height + 4 * ROWS, LANES), f32)
    return pl.pallas_call(
        smooth_kernel,
        out_shape=jax.ShapeDtypeStruct(residual.shape, f32),
        in_specs=[pl.BlockSpec(memory_space=pltpu.SMEM)] + [pl.BlockSpec(memory_space=VMEM)] * 6,
        scratch_shapes=[scratch] * 4,
        cost_estimate=pl.CostEstimate(flops=300 * residual.size, bytes_accessed=12 * residual.size, transcendentals=0),
        compiler_params=limit(28),
        name="smooth",
    )(inside, residual, wavenumber, row_low, row_high, deep_low, deep_high)


def lifted(smoothed, values, out, fine, wide, left):
    shots, _, depth, height, width = smoothed.shape
    strips, across = height // QY, width // PX
    blocks = [(shot, part) for part in range(2) for shot in range(shots)]
    goes = [pltpu.make_async_copy(fine.at[at], out.at[block], left.at[at]) for at, block in enumerate(blocks)]
    lines = [values[:, strip * across : (strip + 1) * across] for strip in range(strips)]
    wide[...] = exact_dot(jnp.concatenate(lines, axis=0), membership(width, across), 1)
    for at, (shot, part) in enumerate(blocks):
        for strip in range(strips):
            line = strip * 2 * shots + at
            value = jnp.broadcast_to(wide[line : line + 1, :], (QY, width))
            for plane in range(depth):
                rows = slice(strip * QY, (strip + 1) * QY)
                fine[at, plane, rows, :] = smoothed[shot, part, plane, rows, :] + value
        goes[at].start()
    for copy in goes:
        copy.wait()


def lift_kernel(smoothed, coarse, out, fine, wide, left):
    lifted(smoothed, coarse[...], out, fine, wide, left)


def last_kernel(step, smoothed, kept_before, matrix, same, other, out, fine, wide, left, vector, coarse):
    coarse[...] = kept_before[...]

    @pl.when(lax.axis_index("layer") == step)
    def _():
        ordered(vector, same, other, lax.axis_index("row") % 2 == 0)
        full = vector[...]
        coarse[...] = combined(times(full, matrix[0]), times(full, matrix[1]))

    lifted(smoothed, coarse[...], out, fine, wide, left)


def lift(smoothed, kept, step=None, *operands):
    shots, _, depth, height, width = smoothed.shape
    lines, cells = kept.shape
    scratch = [
        pltpu.VMEM((2 * shots, depth, height, width), f32),
        pltpu.VMEM((height // QY * lines, width), f32),
        pltpu.SemaphoreType.DMA((2 * shots,)),
    ]
    kernel = lift_kernel
    if operands:
        columns = operands[1].shape[0]
        kernel = functools.partial(last_kernel, step)
        scratch += [pltpu.VMEM((lines, 2 * columns * cells), bf16), pltpu.VMEM((lines, cells), f32)]
    return pl.pallas_call(
        kernel,
        out_shape=pltpu.HBM(smoothed.shape, f32),
        in_specs=[pl.BlockSpec(memory_space=VMEM)] * (2 + len(operands)),
        out_specs=pl.BlockSpec(memory_space=pltpu.HBM),
        scratch_shapes=scratch,
        compiler_params=limit(6),
        name="lift",
    )(smoothed, kept, *operands)


def pack_planes_kernel(residual, wavenumber, first, last):
    shots, _, depth, height, width = residual.shape
    for out, base in ((first, 0), (last, depth - HALO)):
        for plane in range(HALO):
            for shot in range(shots):
                for part in range(2):
                    out[2 * shot + part, plane] = residual[shot, part, base + plane].astype(bf16)
            out[2 * shots, plane] = wavenumber[base + plane].astype(bf16)


def pack_planes(residual, wavenumber):
    shots, _, _, height, width = residual.shape
    shape = jax.ShapeDtypeStruct((2 * shots + 1, HALO, height, width), bf16)
    return pl.pallas_call(
        pack_planes_kernel, out_shape=(shape, shape), compiler_params=limit(10), name="pack_planes"
    )(residual, wavenumber)


def pack_rows_kernel(residual, wavenumber, below, above, first, last):
    shots, _, depth, height, width = residual.shape
    for out, base in ((first, 0), (last, height - SENT)):
        rows = slice(base, base + SENT)
        for field in range(2 * shots + 1):
            for plane in range(HALO):
                out[field, plane] = below[field, plane, rows, :]
                out[field, HALO + depth + plane] = above[field, plane, rows, :]
            for plane in range(depth):
                own = wavenumber[plane, rows, :] if field == 2 * shots else residual[field // 2, field % 2, plane, rows, :]
                out[field, HALO + plane] = own.astype(bf16)


def pack_rows(residual, wavenumber, below, above):
    shots, _, depth, _, width = residual.shape
    shape = jax.ShapeDtypeStruct((2 * shots + 1, depth + 2 * HALO, SENT, width), bf16)
    return pl.pallas_call(
        pack_rows_kernel, out_shape=(shape, shape), compiler_params=limit(10), name="pack_rows"
    )(residual, wavenumber, below, above)


def both_ways(low_block, high_block, axis):
    size = lax.axis_size(axis)
    up = [(i, i + 1) for i in range(size - 1)]
    return lax.ppermute(high_block, axis, up), lax.ppermute(low_block, axis, [(b, a) for a, b in up])


def every_layer(residual, wavenumber, inverse):
    layers, devices = lax.axis_size("layer"), lax.axis_size("row")
    layer, row = lax.axis_index("layer"), lax.axis_index("row")
    inside = jnp.stack([layer > 0, layer < layers - 1, row > 0, row < devices - 1]).astype(f32)

    rhs, spread = restrict(residual, devices)
    next_rhs = lax.ppermute(rhs, "layer", [(i + 1, i) for i in range(layers - 1)])
    matrix = pltpu.with_memory_space_constraint(inverse[:, 0], pltpu.HBM)
    gathered = lax.cond(
        layer == 0,
        lambda blocks: lax.all_to_all(blocks, "row", 0, 0, tiled=True),
        lambda blocks: blocks,
        spread,
    )
    kept, spread = solve_first(matrix, gathered, next_rhs)

    ends = [[2 * column + end for column in range(devices // 2)] for end in range(2)]

    def gather(step, spread):
        return lax.cond(
            layer == step,
            lambda blocks: lax.all_to_all(blocks, "row", 0, 0, axis_index_groups=ends, tiled=True),
            lambda blocks: blocks,
            spread,
        )

    def swap(step, half):
        found = []
        for flip in (1, 0):
            way = [
                (i * devices + j, (i ^ (step - 1) ^ step) * devices + (j ^ flip))
                for i in range(layers)
                for j in range(devices)
            ]
            found.append(lax.ppermute(half, ("layer", "row"), way))
        return found

    def send(step, half):
        found = []
        for flip in (1, 0):
            way = [((step - 1) * devices + j, step * devices + (j ^ flip)) for j in range(devices)]
            found.append(lax.ppermute(half, ("layer", "row"), way))
        return found

    def solve(step, other, same, kept):
        held = hold(step, matrix)
        return solve_layer(step, held, same, other, next_rhs, kept)

    open_hops = (2, layers // 2)
    for step in range(1, layers - 1):
        half = gather(step - 1, spread)
        if step in open_hops:
            kept, spread = solve(step, *send(step, half), kept)
            continue
        kept, spread = lax.cond(
            (layer == step - 1) | (layer == step),
            lambda half, kept, step=step: tuple(solve(step, *swap(step, half), kept)),
            lambda half, kept: (kept, half),
            half,
            kept,
        )

    def planes_of(first, last, pairs):
        back = [(high, low) for low, high in pairs]
        return lax.ppermute(last, "layer", pairs), lax.ppermute(first, "layer", back)

    first, last = pack_planes(residual, wavenumber)
    pairs = [(i, i + 1) for i in range(layers - 1) if i != 1]
    below, above = planes_of(first, last, pairs)
    late_below, late_above = planes_of(first, last, [(1, 2)])
    below = jnp.where(layer == 2, late_below, below)
    above = jnp.where(layer == 1, late_above, above)
    first, last = pack_rows(residual, wavenumber, below, above)
    row_low, row_high = both_ways(first, last, "row")
    smoothed = smooth(inside, residual, wavenumber, row_low, row_high, below, above)

    step = layers - 1
    half = gather(step - 1, spread)

    def finish(half, smoothed, kept):
        other, same = swap(step, half)
        held = hold(step, matrix)
        return lift(smoothed, kept, step, held, same, other)

    return lax.cond(
        layer >= step - 1, finish, lambda half, smoothed, kept: lift(smoothed, kept), half, smoothed, kept
    )


def solution(mesh):
    return jax.shard_map(
        every_layer,
        mesh=mesh,
        in_specs=(
            P(None, None, "layer", "row", None),
            P("layer", "row", None),
            P(None, "layer", "row", None),
        ),
        out_specs=P(None, None, "layer", "row", None),
        check_vma=False,
    )
```

```python
import functools

import jax
import jax.numpy as jnp
from jax import lax
from jax.experimental import pallas as pl
from jax.experimental.pallas import tpu as pltpu
from jax.sharding import PartitionSpec as P


QY = 16
PX = 4
SWEEPS = 4
HALO = SWEEPS - 1
ROWS = 8
SENT = 4
LANES = 256

damping = 0.8
absorb = 0.5
coupling = 0.45

VMEM = pltpu.VMEM
f32 = jnp.float32
bf16 = jnp.bfloat16


def limit(mebibytes):
    return pltpu.CompilerParams(vmem_limit_bytes=mebibytes << 20)


def membership(fine, coarse):
    row = lax.broadcasted_iota(jnp.int32, (fine, coarse), 0)
    col = lax.broadcasted_iota(jnp.int32, (fine, coarse), 1)
    return jnp.where((row >= col * PX) & (row < col * PX + PX), 1.0, 0.0).astype(bf16)


def exact_dot(values, selection, contract):
    first = values.astype(bf16)
    rest = values - first.astype(f32)
    second = rest.astype(bf16)
    third = (rest - second.astype(f32)).astype(bf16)
    total = None
    for piece in (third, second, first):
        part = lax.dot_general(piece, selection, (((1,), (contract,)), ((), ())), preferred_element_type=f32)
        total = part if total is None else total + part
    return total


def restrict_kernel(residual, rhs, spread):
    shots, _, depth, height, width = residual.shape
    strips, across = height // QY, width // PX
    sums = []
    for strip in range(strips):
        for part in range(2):
            for shot in range(shots):
                total = residual[shot, part, 0, strip * QY : (strip + 1) * QY, :]
                for plane in range(1, depth):
                    total = total + residual[shot, part, plane, strip * QY : (strip + 1) * QY, :]
                sums.append(jnp.sum(total, axis=0, keepdims=True))
    means = exact_dot(jnp.concatenate(sums, axis=0), membership(width, across), 0) * (1.0 / (depth * QY * PX))
    lines = 2 * shots
    for strip in range(strips):
        rhs[:, strip * across : (strip + 1) * across] = means[strip * lines : (strip + 1) * lines, :]
    vector = rhs[...].astype(bf16)
    for device in range(spread.shape[0]):
        spread[device] = vector


def restrict(residual, devices):
    shots, _, _, height, width = residual.shape
    cells = (height // QY) * (width // PX)
    return pl.pallas_call(
        restrict_kernel,
        out_shape=(
            jax.ShapeDtypeStruct((2 * shots, cells), f32),
            jax.ShapeDtypeStruct((devices, 2 * shots, cells), bf16),
        ),
        compiler_params=limit(8),
        name="restrict",
    )(residual)


def hold_kernel(step, matrix, held, arrived):
    @pl.when(lax.axis_index("layer") == step)
    def _():
        copy = pltpu.make_async_copy(matrix, held, arrived)
        copy.start()
        copy.wait()


def hold(step, matrix):
    return pl.pallas_call(
        functools.partial(hold_kernel, step),
        out_shape=pltpu.VMEM(matrix.shape, matrix.dtype),
        in_specs=[pl.BlockSpec(memory_space=pltpu.HBM)],
        out_specs=pl.BlockSpec(memory_space=VMEM),
        scratch_shapes=[pltpu.SemaphoreType.DMA],
        compiler_params=limit(1),
        name="hold",
    )(matrix)


def ordered(vector, pairs):
    first_end = lax.axis_index("row") % 2 == 0
    for column, (own, far) in enumerate(pairs):
        cells = own.shape[-1]
        at = 2 * column * cells
        vector[:, at : at + cells] = jnp.where(first_end, own, far)
        vector[:, at + cells : at + 2 * cells] = jnp.where(first_end, far, own)


def halves(both):
    lines = both.shape[1] // 2
    return [(both[column, :lines], both[column, lines:]) for column in range(both.shape[0])]


def combined(by_re, by_im):
    shots = by_re.shape[0] // 2
    return jnp.concatenate([by_re[:shots] - by_im[shots:], by_re[shots:] + by_im[:shots]], axis=0)


def handed_on(solved, next_rhs):
    return (next_rhs[...] + coupling * solved).astype(bf16)


def times(part, rows):
    return lax.dot_general(part, rows, (((1,), (1,)), ((), ())), preferred_element_type=f32)


def first_kernel(matrix, gathered, next_rhs, kept, block, held, vector, arrived):
    devices, _, cells = gathered.shape
    pieces = arrived.shape[0]
    across = matrix.shape[2] // pieces
    columns = [slice(piece * across, (piece + 1) * across) for piece in range(pieces)]

    @pl.when(lax.axis_index("layer") == 0)
    def _():
        copies = [
            pltpu.make_async_copy(matrix.at[:, :, columns[piece]], held.at[:, :, columns[piece]], arrived.at[piece])
            for piece in range(pieces)
        ]
        for copy in copies:
            copy.start()
        for device in range(devices):
            vector[:, device * cells : (device + 1) * cells] = gathered[device]
        by = [None, None]
        for piece in range(pieces):
            part = vector[:, columns[piece]]
            copies[piece].wait()
            for side in range(2):
                product = times(part, held[side, :, columns[piece]])
                by[side] = product if by[side] is None else by[side] + product
        solved = combined(by[0], by[1])
        kept[...] = solved
        block[...] = handed_on(solved, next_rhs)


def solve_first(matrix, gathered, next_rhs):
    devices, lines, cells = gathered.shape
    pieces = 6
    return pl.pallas_call(
        first_kernel,
        out_shape=(
            jax.ShapeDtypeStruct((lines, cells), f32),
            jax.ShapeDtypeStruct((lines, cells), bf16),
        ),
        in_specs=[pl.BlockSpec(memory_space=pltpu.HBM)] + [pl.BlockSpec(memory_space=VMEM)] * 2,
        scratch_shapes=[
            pltpu.VMEM(matrix.shape, bf16),
            pltpu.VMEM((lines, devices * cells), bf16),
            pltpu.SemaphoreType.DMA((pieces,)),
        ],
        compiler_params=limit(8),
        cost_estimate=pl.CostEstimate(flops=4 * matrix.size, bytes_accessed=2 * matrix.size, transcendentals=0),
        name="solve_first",
    )(matrix, gathered, next_rhs)


def pair_up_kernel(near, far, spread):
    lines = near.shape[0]
    for column in range(spread.shape[0]):
        spread[column, :lines] = near[...]
        spread[column, lines:] = far[...]


def pair_up(near, far, columns):
    lines, cells = near.shape
    return pl.pallas_call(
        pair_up_kernel,
        out_shape=jax.ShapeDtypeStruct((columns, 2 * lines, cells), bf16),
        compiler_params=limit(2),
        name="pair_up",
    )(near, far)


def odd_kernel(matrix, both, next_rhs, product, spread, vector):
    ordered(vector, halves(both))
    full = vector[...]
    solved = combined(times(full, matrix[0]), times(full, matrix[1]))
    product[...] = solved
    block = handed_on(solved, next_rhs)
    for column in range(spread.shape[0]):
        spread[column] = block


def even_kernel(matrix, same, other, next_rhs, product, block, vector):
    ordered(vector, [(same[column], other[column]) for column in range(same.shape[0])])
    full = vector[...]
    solved = combined(times(full, matrix[0]), times(full, matrix[1]))
    product[...] = solved
    block[...] = handed_on(solved, next_rhs)


def solve_layer(step, matrix, blocks, next_rhs):
    lines, cells = next_rhs.shape
    columns = blocks[0].shape[0]
    out = (columns, lines, cells) if step % 2 else (lines, cells)
    return pl.pallas_call(
        odd_kernel if step % 2 else even_kernel,
        out_shape=(jax.ShapeDtypeStruct((lines, cells), f32), jax.ShapeDtypeStruct(out, bf16)),
        in_specs=[pl.BlockSpec(memory_space=VMEM)] * (2 + len(blocks)),
        scratch_shapes=[pltpu.VMEM((lines, 2 * columns * cells), bf16)],
        compiler_params=limit(3),
        cost_estimate=pl.CostEstimate(flops=4 * matrix.size, bytes_accessed=2 * matrix.size, transcendentals=0),
        name="solve_layer",
    )(matrix, *blocks, next_rhs)


def smooth_kernel(inside, residual, wavenumber, row_low, row_high, deep_low, deep_high, smoothed, gain, source, first, second):
    shots, _, depth, height, width = residual.shape
    top = ROWS
    start = top + ROWS
    total = height + 2 * ROWS
    planes = depth + 2 * HALO
    rest = LANES - width
    sides = (
        (0, HALO, deep_low, inside[0]),
        (HALO + depth, HALO, deep_high, inside[1]),
    )

    def gains(values, factor):
        real_part = 6.0 - values
        imag_part = -absorb * values
        scale = damping * factor / (real_part * real_part + imag_part * imag_part)
        return real_part * scale, -imag_part * scale

    def put_gain(plane, row, values, factor):
        real_part, imag_part = gains(values, factor)
        rows = values.shape[0]
        gain[0, plane, pl.ds(row, rows), 0:width] = real_part
        gain[1, plane, pl.ds(row, rows), 0:width] = imag_part

    blank = jnp.zeros((total, rest), f32)

    def clear(plane, _):
        for part in range(2):
            gain[part, plane, top : top + total, width:LANES] = blank
            source[part, plane, top : top + total, width:LANES] = blank
        return _

    lax.fori_loop(0, planes, clear, 0)

    def own_gain(plane, _):
        for row in range(0, height, 16):
            put_gain(HALO + plane, start + row, wavenumber[plane, row : row + 16, :], 1.0)
        return _

    lax.fori_loop(0, depth, own_gain, 0)
    for base, count, ghost, factor in sides:
        for plane in range(count):
            for row in range(0, height, 16):
                put_gain(base + plane, start + row, ghost[2 * shots, plane, row : row + 16, :].astype(f32), factor)
    for base, count, factor in ((0, HALO, inside[0]), (HALO, depth, 1.0), (HALO + depth, HALO, inside[1])):

        def row_gain(plane, _, factor=factor):
            put_gain(plane, start - SENT, row_low[2 * shots, plane].astype(f32), factor * inside[2])
            put_gain(plane, start + height, row_high[2 * shots, plane].astype(f32), factor * inside[3])
            return _

        lax.fori_loop(base, base + count, row_gain, 0)

    def sweep(old, plane, row, rows, store):
        here = pl.ds(row, rows)
        terms = []
        for part in range(2):
            centre = old[part, plane, here, :]
            beside = old[part, plane - 1, here, :] + old[part, plane + 1, here, :]
            beside = beside + old[part, plane, pl.ds(row - 1, rows), :] + old[part, plane, pl.ds(row + 1, rows), :]
            beside = beside + pltpu.roll(centre, 1, 1) + pltpu.roll(centre, LANES - 1, 1)
            terms.append((centre, source[part, plane, here, :] + beside))
        (centre_re, sum_re), (centre_im, sum_im) = terms
        gain_re, gain_im = gain[0, plane, here, :], gain[1, plane, here, :]
        store(0, (1.0 - damping) * centre_re + (gain_re * sum_re - gain_im * sum_im))
        store(1, (1.0 - damping) * centre_im + (gain_re * sum_im + gain_im * sum_re))

    for shot in range(shots):

        def own_source(plane, _):
            for part in range(2):
                source[part, HALO + plane, start : start + height, 0:width] = residual[shot, part, plane]
            return _

        def row_source(plane, _):
            for part in range(2):
                source[part, plane, start - SENT : start, 0:width] = row_low[2 * shot + part, plane].astype(f32)
                source[part, plane, start + height : start + height + SENT, 0:width] = row_high[
                    2 * shot + part, plane
                ].astype(f32)
            return _

        lax.fori_loop(0, depth, own_source, 0)
        lax.fori_loop(0, planes, row_source, 0)
        for base, count, ghost, _ in sides:
            for plane in range(count):
                for part in range(2):
                    source[part, base + plane, start : start + height, 0:width] = ghost[2 * shot + part, plane].astype(f32)

        def begin(plane, _):
            for row in range(top, top + total, 16):
                here = pl.ds(row, 16)
                gain_re, gain_im = gain[0, plane, here, :], gain[1, plane, here, :]
                source_re, source_im = source[0, plane, here, :], source[1, plane, here, :]
                first[0, plane, here, :] = gain_re * source_re - gain_im * source_im
                first[1, plane, here, :] = gain_re * source_im + gain_im * source_re
            return _

        lax.fori_loop(0, planes, begin, 0)
        old, new = first, second
        for counter in range(1, SWEEPS):
            last = counter == SWEEPS - 1

            def one_plane(plane, _, old=old, new=new, last=last, shot=shot):
                low, high = (start, start + height) if last else (top, top + total)
                for row in range(low, high, 16):

                    def store(part, value, row=row):
                        if last:
                            smoothed[shot, part, plane - HALO, row - start : row - start + 16, :] = value[:, :width]
                        else:
                            new[part, plane, pl.ds(row, 16), :] = value

                    sweep(old, plane, row, 16, store)
                return _

            lax.fori_loop(counter, planes - counter, one_plane, 0)
            old, new = new, old


def smooth(inside, residual, wavenumber, row_low, row_high, deep_low, deep_high):
    shots, _, depth, height, width = residual.shape
    scratch = pltpu.VMEM((2, depth + 2 * HALO, height + 4 * ROWS, LANES), f32)
    return pl.pallas_call(
        smooth_kernel,
        out_shape=jax.ShapeDtypeStruct(residual.shape, f32),
        in_specs=[pl.BlockSpec(memory_space=pltpu.SMEM)] + [pl.BlockSpec(memory_space=VMEM)] * 6,
        scratch_shapes=[scratch] * 4,
        cost_estimate=pl.CostEstimate(flops=300 * residual.size, bytes_accessed=12 * residual.size, transcendentals=0),
        compiler_params=limit(28),
        name="smooth",
    )(inside, residual, wavenumber, row_low, row_high, deep_low, deep_high)


def lifted(smoothed, values, out, fine, wide, left):
    shots, _, depth, height, width = smoothed.shape
    strips, across = height // QY, width // PX
    blocks = [(shot, part) for part in range(2) for shot in range(shots)]
    goes = [pltpu.make_async_copy(fine.at[at], out.at[block], left.at[at]) for at, block in enumerate(blocks)]
    lines = [values[:, strip * across : (strip + 1) * across] for strip in range(strips)]
    wide[...] = exact_dot(jnp.concatenate(lines, axis=0), membership(width, across), 1)
    for at, (shot, part) in enumerate(blocks):
        for strip in range(strips):
            line = strip * 2 * shots + at
            value = jnp.broadcast_to(wide[line : line + 1, :], (QY, width))
            for plane in range(depth):
                rows = slice(strip * QY, (strip + 1) * QY)
                fine[at, plane, rows, :] = smoothed[shot, part, plane, rows, :] + value
        goes[at].start()
    for copy in goes:
        copy.wait()


def lift_kernel(smoothed, coarse, out, fine, wide, left):
    lifted(smoothed, coarse[...], out, fine, wide, left)


def last_kernel(step, smoothed, kept_before, matrix, both, out, fine, wide, left, vector, coarse):
    coarse[...] = kept_before[...]

    @pl.when(lax.axis_index("layer") == step)
    def _():
        ordered(vector, halves(both))
        full = vector[...]
        coarse[...] = combined(times(full, matrix[0]), times(full, matrix[1]))

    lifted(smoothed, coarse[...], out, fine, wide, left)


def lift(smoothed, kept, step=None, *operands):
    shots, _, depth, height, width = smoothed.shape
    lines, cells = kept.shape
    scratch = [
        pltpu.VMEM((2 * shots, depth, height, width), f32),
        pltpu.VMEM((height // QY * lines, width), f32),
        pltpu.SemaphoreType.DMA((2 * shots,)),
    ]
    kernel = lift_kernel
    if operands:
        columns = operands[1].shape[0]
        kernel = functools.partial(last_kernel, step)
        scratch += [pltpu.VMEM((lines, 2 * columns * cells), bf16), pltpu.VMEM((lines, cells), f32)]
    return pl.pallas_call(
        kernel,
        out_shape=pltpu.HBM(smoothed.shape, f32),
        in_specs=[pl.BlockSpec(memory_space=VMEM)] * (2 + len(operands)),
        out_specs=pl.BlockSpec(memory_space=pltpu.HBM),
        scratch_shapes=scratch,
        compiler_params=limit(6),
        name="lift",
    )(smoothed, kept, *operands)


def pack_planes_kernel(residual, wavenumber, first, last):
    shots, _, depth, height, width = residual.shape
    for out, base in ((first, 0), (last, depth - HALO)):
        for plane in range(HALO):
            for shot in range(shots):
                for part in range(2):
                    out[2 * shot + part, plane] = residual[shot, part, base + plane].astype(bf16)
            out[2 * shots, plane] = wavenumber[base + plane].astype(bf16)


def pack_planes(residual, wavenumber):
    shots, _, _, height, width = residual.shape
    shape = jax.ShapeDtypeStruct((2 * shots + 1, HALO, height, width), bf16)
    return pl.pallas_call(
        pack_planes_kernel, out_shape=(shape, shape), compiler_params=limit(10), name="pack_planes"
    )(residual, wavenumber)


def pack_rows_kernel(residual, wavenumber, below, above, first, last):
    shots, _, depth, height, width = residual.shape
    for out, base in ((first, 0), (last, height - SENT)):
        rows = slice(base, base + SENT)
        for field in range(2 * shots + 1):
            for plane in range(HALO):
                out[field, plane] = below[field, plane, rows, :]
                out[field, HALO + depth + plane] = above[field, plane, rows, :]
            for plane in range(depth):
                own = wavenumber[plane, rows, :] if field == 2 * shots else residual[field // 2, field % 2, plane, rows, :]
                out[field, HALO + plane] = own.astype(bf16)


def pack_rows(residual, wavenumber, below, above):
    shots, _, depth, _, width = residual.shape
    shape = jax.ShapeDtypeStruct((2 * shots + 1, depth + 2 * HALO, SENT, width), bf16)
    return pl.pallas_call(
        pack_rows_kernel, out_shape=(shape, shape), compiler_params=limit(10), name="pack_rows"
    )(residual, wavenumber, below, above)


def both_ways(low_block, high_block, axis):
    size = lax.axis_size(axis)
    up = [(i, i + 1) for i in range(size - 1)]
    return lax.ppermute(high_block, axis, up), lax.ppermute(low_block, axis, [(b, a) for a, b in up])


def every_layer(residual, wavenumber, inverse):
    layers, devices = lax.axis_size("layer"), lax.axis_size("row")
    layer, row = lax.axis_index("layer"), lax.axis_index("row")
    inside = jnp.stack([layer > 0, layer < layers - 1, row > 0, row < devices - 1]).astype(f32)

    rhs, spread = restrict(residual, devices)
    next_rhs = lax.ppermute(rhs, "layer", [(i + 1, i) for i in range(layers - 1)])
    matrix = pltpu.with_memory_space_constraint(inverse[:, 0], pltpu.HBM)
    gathered = lax.cond(
        layer == 0,
        lambda blocks: lax.all_to_all(blocks, "row", 0, 0, tiled=True),
        lambda blocks: blocks,
        spread,
    )
    kept, block = solve_first(matrix, gathered, next_rhs)

    columns = devices // 2
    ends = [[2 * column + end for column in range(columns)] for end in range(2)]

    def gather(blocks):
        return lax.all_to_all(blocks, "row", 0, 0, axis_index_groups=ends, tiled=True)

    def hop(step, sent, way):
        found = []
        for flip in (1, 0):
            found.append(lax.ppermute(sent, ("layer", "row"), way(step, flip)))
        return found[1], found[0]

    def swapped(step, flip):
        return [
            (i * devices + j, (i ^ (step - 1) ^ step) * devices + (j ^ flip))
            for i in range(layers)
            for j in range(devices)
        ]

    def straight(step, flip):
        return [((step - 1) * devices + j, step * devices + (j ^ flip)) for j in range(devices)]

    def held(step):
        return hold(step, matrix)

    def solve(step, own, blocks):
        return tuple(solve_layer(step, own, blocks, next_rhs))

    def to_odd(step, block):
        near, far = hop(step, block, swapped)
        return gather(pair_up(near, far, columns))

    def odd_step(step, kept, block):
        own = held(step)
        return solve(step, own, [to_odd(step, block)])

    def even_step(step, kept, half, block):
        own = held(step)
        return solve(step, own, hop(step, half, swapped))

    open_hops = (2, layers // 2)
    for step in range(1, layers - 1):
        takes_part = (layer == step - 1) | (layer == step)
        if step % 2:
            product, spread = lax.cond(
                takes_part,
                functools.partial(odd_step, step),
                lambda kept, block: (kept, jnp.broadcast_to(block[None], (columns, *block.shape))),
                kept,
                block,
            )
        else:
            half = lax.cond(layer == step - 1, gather, lambda blocks: blocks, spread)
            if step in open_hops:
                product, block = solve(step, held(step), hop(step, half, straight))
            else:
                product, block = lax.cond(
                    takes_part,
                    functools.partial(even_step, step),
                    lambda kept, half, block: (kept, block),
                    kept,
                    half,
                    block,
                )
        kept = jnp.where(layer == step, product, kept)

    def planes_of(first, last, pairs):
        back = [(high, low) for low, high in pairs]
        return lax.ppermute(last, "layer", pairs), lax.ppermute(first, "layer", back)

    first, last = pack_planes(residual, wavenumber)
    pairs = [(i, i + 1) for i in range(layers - 1) if i != 1]
    below, above = planes_of(first, last, pairs)
    late_below, late_above = planes_of(first, last, [(1, 2)])
    below = jnp.where(layer == 2, late_below, below)
    above = jnp.where(layer == 1, late_above, above)
    first, last = pack_rows(residual, wavenumber, below, above)
    row_low, row_high = both_ways(first, last, "row")
    smoothed = smooth(inside, residual, wavenumber, row_low, row_high, below, above)

    step = layers - 1

    def finish(block, smoothed, kept):
        own = held(step)
        both = to_odd(step, block)
        return lift(smoothed, kept, step, own, both)

    return lax.cond(
        layer >= step - 1, finish, lambda block, smoothed, kept: lift(smoothed, kept), block, smoothed, kept
    )


def solution(mesh):
    return jax.shard_map(
        every_layer,
        mesh=mesh,
        in_specs=(
            P(None, None, "layer", "row", None),
            P("layer", "row", None),
            P(None, "layer", "row", None),
        ),
        out_specs=P(None, None, "layer", "row", None),
        check_vma=False,
    )
```

```python
import functools

import jax
import jax.numpy as jnp
from jax import lax
from jax.experimental import pallas as pl
from jax.experimental.pallas import tpu as pltpu
from jax.sharding import PartitionSpec as P


QY = 16
PX = 4
SWEEPS = 4
HALO = SWEEPS - 1
ROWS = 8
SENT = 4
LANES = 256

damping = 0.8
absorb = 0.5
coupling = 0.45

VMEM = pltpu.VMEM
f32 = jnp.float32
bf16 = jnp.bfloat16


def limit(mebibytes):
    return pltpu.CompilerParams(vmem_limit_bytes=mebibytes << 20)


def membership(fine, coarse):
    row = lax.broadcasted_iota(jnp.int32, (fine, coarse), 0)
    col = lax.broadcasted_iota(jnp.int32, (fine, coarse), 1)
    return jnp.where((row >= col * PX) & (row < col * PX + PX), 1.0, 0.0).astype(bf16)


def exact_dot(values, selection, contract):
    first = values.astype(bf16)
    rest = values - first.astype(f32)
    second = rest.astype(bf16)
    third = (rest - second.astype(f32)).astype(bf16)
    total = None
    for piece in (third, second, first):
        part = lax.dot_general(piece, selection, (((1,), (contract,)), ((), ())), preferred_element_type=f32)
        total = part if total is None else total + part
    return total


def restrict_kernel(residual, rhs, spread, brick, arrived):
    shots, _, depth, height, width = residual.shape
    strips, across = height // QY, width // PX
    lines = 2 * shots
    blocks = [(shot, part) for part in range(2) for shot in range(shots)]
    copies = [
        pltpu.make_async_copy(residual.at[block], brick.at[at], arrived.at[at]) for at, block in enumerate(blocks)
    ]
    for copy in copies:
        copy.start()
    sums = [None] * (strips * lines)
    for at in range(lines):
        copies[at].wait()
        for strip in range(strips):
            total = brick[at, 0, strip * QY : (strip + 1) * QY, :]
            for plane in range(1, depth):
                total = total + brick[at, plane, strip * QY : (strip + 1) * QY, :]
            sums[strip * lines + at] = jnp.sum(total, axis=0, keepdims=True)
    means = exact_dot(jnp.concatenate(sums, axis=0), membership(width, across), 0) * (1.0 / (depth * QY * PX))
    for strip in range(strips):
        rhs[:, strip * across : (strip + 1) * across] = means[strip * lines : (strip + 1) * lines, :]
    vector = rhs[...].astype(bf16)
    for device in range(spread.shape[0]):
        spread[device] = vector


def restrict(residual, devices):
    shots, _, depth, height, width = residual.shape
    cells = (height // QY) * (width // PX)
    return pl.pallas_call(
        restrict_kernel,
        out_shape=(
            jax.ShapeDtypeStruct((2 * shots, cells), f32),
            jax.ShapeDtypeStruct((devices, 2 * shots, cells), bf16),
        ),
        in_specs=[pl.BlockSpec(memory_space=pltpu.HBM)],
        scratch_shapes=[
            pltpu.VMEM((2 * shots, depth, height, width), f32),
            pltpu.SemaphoreType.DMA((2 * shots,)),
        ],
        compiler_params=limit(8),
        name="restrict",
    )(pltpu.with_memory_space_constraint(residual, pltpu.HBM))


def hold_kernel(step, matrix, held, arrived):
    @pl.when(lax.axis_index("layer") == step)
    def _():
        copy = pltpu.make_async_copy(matrix, held, arrived)
        copy.start()
        copy.wait()


def hold(step, matrix):
    return pl.pallas_call(
        functools.partial(hold_kernel, step),
        out_shape=pltpu.VMEM(matrix.shape, matrix.dtype),
        in_specs=[pl.BlockSpec(memory_space=pltpu.HBM)],
        out_specs=pl.BlockSpec(memory_space=VMEM),
        scratch_shapes=[pltpu.SemaphoreType.DMA],
        compiler_params=limit(1),
        name="hold",
    )(matrix)


def ordered(vector, pairs):
    first_end = lax.axis_index("row") % 2 == 0
    for column, (own, far) in enumerate(pairs):
        cells = own.shape[-1]
        at = 2 * column * cells
        vector[:, at : at + cells] = jnp.where(first_end, own, far)
        vector[:, at + cells : at + 2 * cells] = jnp.where(first_end, far, own)


def halves(both):
    lines = both.shape[1] // 2
    return [(both[column, :lines], both[column, lines:]) for column in range(both.shape[0])]


def combined(by_re, by_im):
    shots = by_re.shape[0] // 2
    return jnp.concatenate([by_re[:shots] - by_im[shots:], by_re[shots:] + by_im[:shots]], axis=0)


def handed_on(solved, next_rhs):
    return (next_rhs[...] + coupling * solved).astype(bf16)


def times(part, rows):
    return lax.dot_general(part, rows, (((1,), (1,)), ((), ())), preferred_element_type=f32)


def first_kernel(matrix, gathered, next_rhs, kept, block, held, vector, arrived):
    devices, _, cells = gathered.shape
    pieces = arrived.shape[0]
    across = matrix.shape[2] // pieces
    columns = [slice(piece * across, (piece + 1) * across) for piece in range(pieces)]

    @pl.when(lax.axis_index("layer") == 0)
    def _():
        copies = [
            pltpu.make_async_copy(matrix.at[:, :, columns[piece]], held.at[:, :, columns[piece]], arrived.at[piece])
            for piece in range(pieces)
        ]
        for copy in copies:
            copy.start()
        for device in range(devices):
            vector[:, device * cells : (device + 1) * cells] = gathered[device]
        by = [None, None]
        for piece in range(pieces):
            part = vector[:, columns[piece]]
            copies[piece].wait()
            for side in range(2):
                product = times(part, held[side, :, columns[piece]])
                by[side] = product if by[side] is None else by[side] + product
        solved = combined(by[0], by[1])
        kept[...] = solved
        block[...] = handed_on(solved, next_rhs)


def solve_first(matrix, gathered, next_rhs):
    devices, lines, cells = gathered.shape
    pieces = 6
    return pl.pallas_call(
        first_kernel,
        out_shape=(
            jax.ShapeDtypeStruct((lines, cells), f32),
            jax.ShapeDtypeStruct((lines, cells), bf16),
        ),
        in_specs=[pl.BlockSpec(memory_space=pltpu.HBM)] + [pl.BlockSpec(memory_space=VMEM)] * 2,
        scratch_shapes=[
            pltpu.VMEM(matrix.shape, bf16),
            pltpu.VMEM((lines, devices * cells), bf16),
            pltpu.SemaphoreType.DMA((pieces,)),
        ],
        compiler_params=limit(8),
        cost_estimate=pl.CostEstimate(flops=4 * matrix.size, bytes_accessed=2 * matrix.size, transcendentals=0),
        name="solve_first",
    )(matrix, gathered, next_rhs)


def pair_up_kernel(near, far, spread):
    lines = near.shape[0]
    for column in range(spread.shape[0]):
        spread[column, :lines] = near[...]
        spread[column, lines:] = far[...]


def pair_up(near, far, columns):
    lines, cells = near.shape
    return pl.pallas_call(
        pair_up_kernel,
        out_shape=jax.ShapeDtypeStruct((columns, 2 * lines, cells), bf16),
        compiler_params=limit(2),
        name="pair_up",
    )(near, far)


def odd_kernel(matrix, both, next_rhs, product, spread, vector):
    ordered(vector, halves(both))
    full = vector[...]
    solved = combined(times(full, matrix[0]), times(full, matrix[1]))
    product[...] = solved
    block = handed_on(solved, next_rhs)
    for column in range(spread.shape[0]):
        spread[column] = block


def even_kernel(matrix, same, other, next_rhs, product, block, vector):
    ordered(vector, [(same[column], other[column]) for column in range(same.shape[0])])
    full = vector[...]
    solved = combined(times(full, matrix[0]), times(full, matrix[1]))
    product[...] = solved
    block[...] = handed_on(solved, next_rhs)


def solve_layer(step, matrix, blocks, next_rhs):
    lines, cells = next_rhs.shape
    columns = blocks[0].shape[0]
    out = (columns, lines, cells) if step % 2 else (lines, cells)
    return pl.pallas_call(
        odd_kernel if step % 2 else even_kernel,
        out_shape=(jax.ShapeDtypeStruct((lines, cells), f32), jax.ShapeDtypeStruct(out, bf16)),
        in_specs=[pl.BlockSpec(memory_space=VMEM)] * (2 + len(blocks)),
        scratch_shapes=[pltpu.VMEM((lines, 2 * columns * cells), bf16)],
        compiler_params=limit(3),
        cost_estimate=pl.CostEstimate(flops=4 * matrix.size, bytes_accessed=2 * matrix.size, transcendentals=0),
        name="solve_layer",
    )(matrix, *blocks, next_rhs)


def smooth_kernel(inside, residual, wavenumber, row_low, row_high, deep_low, deep_high, smoothed, gain, source, first, second):
    shots, _, depth, height, width = residual.shape
    top = ROWS
    start = top + ROWS
    total = height + 2 * ROWS
    planes = depth + 2 * HALO
    rest = LANES - width
    sides = (
        (0, HALO, deep_low, inside[0]),
        (HALO + depth, HALO, deep_high, inside[1]),
    )

    def gains(values, factor):
        real_part = 6.0 - values
        imag_part = -absorb * values
        scale = damping * factor / (real_part * real_part + imag_part * imag_part)
        return real_part * scale, -imag_part * scale

    def put_gain(plane, row, values, factor):
        real_part, imag_part = gains(values, factor)
        rows = values.shape[0]
        gain[0, plane, pl.ds(row, rows), 0:width] = real_part
        gain[1, plane, pl.ds(row, rows), 0:width] = imag_part

    blank = jnp.zeros((total, rest), f32)

    def clear(plane, _):
        for part in range(2):
            gain[part, plane, top : top + total, width:LANES] = blank
            source[part, plane, top : top + total, width:LANES] = blank
        return _

    lax.fori_loop(0, planes, clear, 0)

    def own_gain(plane, _):
        for row in range(0, height, 16):
            put_gain(HALO + plane, start + row, wavenumber[plane, row : row + 16, :], 1.0)
        return _

    lax.fori_loop(0, depth, own_gain, 0)
    for base, count, ghost, factor in sides:
        for plane in range(count):
            for row in range(0, height, 16):
                put_gain(base + plane, start + row, ghost[2 * shots, plane, row : row + 16, :].astype(f32), factor)
    for base, count, factor in ((0, HALO, inside[0]), (HALO, depth, 1.0), (HALO + depth, HALO, inside[1])):

        def row_gain(plane, _, factor=factor):
            put_gain(plane, start - SENT, row_low[2 * shots, plane].astype(f32), factor * inside[2])
            put_gain(plane, start + height, row_high[2 * shots, plane].astype(f32), factor * inside[3])
            return _

        lax.fori_loop(base, base + count, row_gain, 0)

    def sweep(old, plane, row, rows, store):
        here = pl.ds(row, rows)
        terms = []
        for part in range(2):
            centre = old[part, plane, here, :]
            beside = old[part, plane - 1, here, :] + old[part, plane + 1, here, :]
            beside = beside + old[part, plane, pl.ds(row - 1, rows), :] + old[part, plane, pl.ds(row + 1, rows), :]
            beside = beside + pltpu.roll(centre, 1, 1) + pltpu.roll(centre, LANES - 1, 1)
            terms.append((centre, source[part, plane, here, :] + beside))
        (centre_re, sum_re), (centre_im, sum_im) = terms
        gain_re, gain_im = gain[0, plane, here, :], gain[1, plane, here, :]
        store(0, (1.0 - damping) * centre_re + (gain_re * sum_re - gain_im * sum_im))
        store(1, (1.0 - damping) * centre_im + (gain_re * sum_im + gain_im * sum_re))

    for shot in range(shots):

        def own_source(plane, _):
            for part in range(2):
                source[part, HALO + plane, start : start + height, 0:width] = residual[shot, part, plane]
            return _

        def row_source(plane, _):
            for part in range(2):
                source[part, plane, start - SENT : start, 0:width] = row_low[2 * shot + part, plane].astype(f32)
                source[part, plane, start + height : start + height + SENT, 0:width] = row_high[
                    2 * shot + part, plane
                ].astype(f32)
            return _

        lax.fori_loop(0, depth, own_source, 0)
        lax.fori_loop(0, planes, row_source, 0)
        for base, count, ghost, _ in sides:
            for plane in range(count):
                for part in range(2):
                    source[part, base + plane, start : start + height, 0:width] = ghost[2 * shot + part, plane].astype(f32)

        def begin(plane, _):
            for row in range(top, top + total, 16):
                here = pl.ds(row, 16)
                gain_re, gain_im = gain[0, plane, here, :], gain[1, plane, here, :]
                source_re, source_im = source[0, plane, here, :], source[1, plane, here, :]
                first[0, plane, here, :] = gain_re * source_re - gain_im * source_im
                first[1, plane, here, :] = gain_re * source_im + gain_im * source_re
            return _

        lax.fori_loop(0, planes, begin, 0)
        old, new = first, second
        for counter in range(1, SWEEPS):
            last = counter == SWEEPS - 1

            def one_plane(plane, _, old=old, new=new, last=last, shot=shot):
                low, high = (start, start + height) if last else (top, top + total)
                for row in range(low, high, 16):

                    def store(part, value, row=row):
                        if last:
                            smoothed[shot, part, plane - HALO, row - start : row - start + 16, :] = value[:, :width]
                        else:
                            new[part, plane, pl.ds(row, 16), :] = value

                    sweep(old, plane, row, 16, store)
                return _

            lax.fori_loop(counter, planes - counter, one_plane, 0)
            old, new = new, old


def smooth(inside, residual, wavenumber, row_low, row_high, deep_low, deep_high):
    shots, _, depth, height, width = residual.shape
    scratch = pltpu.VMEM((2, depth + 2 * HALO, height + 4 * ROWS, LANES), f32)
    return pl.pallas_call(
        smooth_kernel,
        out_shape=jax.ShapeDtypeStruct(residual.shape, f32),
        in_specs=[pl.BlockSpec(memory_space=pltpu.SMEM)] + [pl.BlockSpec(memory_space=VMEM)] * 6,
        scratch_shapes=[scratch] * 4,
        cost_estimate=pl.CostEstimate(flops=300 * residual.size, bytes_accessed=12 * residual.size, transcendentals=0),
        compiler_params=limit(28),
        name="smooth",
    )(inside, residual, wavenumber, row_low, row_high, deep_low, deep_high)


def lifted(smoothed, values, out, fine, wide, left):
    shots, _, depth, height, width = smoothed.shape
    strips, across = height // QY, width // PX
    blocks = [(shot, part) for part in range(2) for shot in range(shots)]
    goes = [pltpu.make_async_copy(fine.at[at], out.at[block], left.at[at]) for at, block in enumerate(blocks)]
    lines = [values[:, strip * across : (strip + 1) * across] for strip in range(strips)]
    wide[...] = exact_dot(jnp.concatenate(lines, axis=0), membership(width, across), 1)
    for at, (shot, part) in enumerate(blocks):
        for strip in range(strips):
            line = strip * 2 * shots + at
            value = jnp.broadcast_to(wide[line : line + 1, :], (QY, width))
            for plane in range(depth):
                rows = slice(strip * QY, (strip + 1) * QY)
                fine[at, plane, rows, :] = smoothed[shot, part, plane, rows, :] + value
        goes[at].start()
    for copy in goes:
        copy.wait()


def lift_kernel(smoothed, coarse, out, fine, wide, left):
    lifted(smoothed, coarse[...], out, fine, wide, left)


def last_kernel(step, smoothed, kept, matrix, both, out, fine, wide, left, vector):
    ordered(vector, halves(both))
    full = vector[...]
    solved = combined(times(full, matrix[0]), times(full, matrix[1]))
    lifted(smoothed, jnp.where(lax.axis_index("layer") == step, solved, kept[...]), out, fine, wide, left)


def lift(smoothed, kept, step=None, *operands):
    shots, _, depth, height, width = smoothed.shape
    lines, cells = kept.shape
    scratch = [
        pltpu.VMEM((2 * shots, depth, height, width), f32),
        pltpu.VMEM((height // QY * lines, width), f32),
        pltpu.SemaphoreType.DMA((2 * shots,)),
    ]
    kernel = lift_kernel
    if operands:
        columns = operands[1].shape[0]
        kernel = functools.partial(last_kernel, step)
        scratch += [pltpu.VMEM((lines, 2 * columns * cells), bf16)]
    return pl.pallas_call(
        kernel,
        out_shape=pltpu.HBM(smoothed.shape, f32),
        in_specs=[pl.BlockSpec(memory_space=VMEM)] * (2 + len(operands)),
        out_specs=pl.BlockSpec(memory_space=pltpu.HBM),
        scratch_shapes=scratch,
        compiler_params=limit(6),
        name="lift",
    )(smoothed, kept, *operands)


def pack_planes_kernel(residual, wavenumber, first, last):
    shots, _, depth, height, width = residual.shape
    for out, base in ((first, 0), (last, depth - HALO)):
        for plane in range(HALO):
            for shot in range(shots):
                for part in range(2):
                    out[2 * shot + part, plane] = residual[shot, part, base + plane].astype(bf16)
            out[2 * shots, plane] = wavenumber[base + plane].astype(bf16)


def pack_planes(residual, wavenumber):
    shots, _, _, height, width = residual.shape
    shape = jax.ShapeDtypeStruct((2 * shots + 1, HALO, height, width), bf16)
    return pl.pallas_call(
        pack_planes_kernel, out_shape=(shape, shape), compiler_params=limit(10), name="pack_planes"
    )(residual, wavenumber)


def pack_rows_kernel(residual, wavenumber, below, above, first, last):
    shots, _, depth, height, width = residual.shape
    for out, base in ((first, 0), (last, height - SENT)):
        rows = slice(base, base + SENT)
        for field in range(2 * shots + 1):
            for plane in range(HALO):
                out[field, plane] = below[field, plane, rows, :]
                out[field, HALO + depth + plane] = above[field, plane, rows, :]
            for plane in range(depth):
                own = wavenumber[plane, rows, :] if field == 2 * shots else residual[field // 2, field % 2, plane, rows, :]
                out[field, HALO + plane] = own.astype(bf16)


def pack_rows(residual, wavenumber, below, above):
    shots, _, depth, _, width = residual.shape
    shape = jax.ShapeDtypeStruct((2 * shots + 1, depth + 2 * HALO, SENT, width), bf16)
    return pl.pallas_call(
        pack_rows_kernel, out_shape=(shape, shape), compiler_params=limit(10), name="pack_rows"
    )(residual, wavenumber, below, above)


def both_ways(low_block, high_block, axis):
    size = lax.axis_size(axis)
    up = [(i, i + 1) for i in range(size - 1)]
    return lax.ppermute(high_block, axis, up), lax.ppermute(low_block, axis, [(b, a) for a, b in up])


def every_layer(residual, wavenumber, inverse):
    layers, devices = lax.axis_size("layer"), lax.axis_size("row")
    layer, row = lax.axis_index("layer"), lax.axis_index("row")
    inside = jnp.stack([layer > 0, layer < layers - 1, row > 0, row < devices - 1]).astype(f32)

    rhs, spread = restrict(residual, devices)
    next_rhs = lax.ppermute(rhs, "layer", [(i + 1, i) for i in range(layers - 1)])
    matrix = pltpu.with_memory_space_constraint(inverse[:, 0], pltpu.HBM)
    gathered = lax.cond(
        layer == 0,
        lambda blocks: lax.all_to_all(blocks, "row", 0, 0, tiled=True),
        lambda blocks: blocks,
        spread,
    )
    kept, block = solve_first(matrix, gathered, next_rhs)

    columns = devices // 2
    ends = [[2 * column + end for column in range(columns)] for end in range(2)]

    def gather(blocks):
        return lax.all_to_all(blocks, "row", 0, 0, axis_index_groups=ends, tiled=True)

    def hop(step, sent, way):
        found = []
        for flip in (1, 0):
            found.append(lax.ppermute(sent, ("layer", "row"), way(step, flip)))
        return found[1], found[0]

    def swapped(step, flip):
        return [
            (i * devices + j, (i ^ (step - 1) ^ step) * devices + (j ^ flip))
            for i in range(layers)
            for j in range(devices)
        ]

    def straight(step, flip):
        return [((step - 1) * devices + j, step * devices + (j ^ flip)) for j in range(devices)]

    def held(step):
        return hold(step, matrix)

    def solve(step, own, blocks):
        return tuple(solve_layer(step, own, blocks, next_rhs))

    def to_odd(step, block):
        near, far = hop(step, block, swapped)
        return gather(pair_up(near, far, columns))

    def odd_step(step, kept, block):
        own = held(step)
        return solve(step, own, [to_odd(step, block)])

    def even_step(step, kept, half, block):
        own = held(step)
        return solve(step, own, hop(step, half, swapped))

    open_hops = (2, layers // 2)
    for step in range(1, layers - 1):
        takes_part = (layer == step - 1) | (layer == step)
        if step % 2:
            product, spread = lax.cond(
                takes_part,
                functools.partial(odd_step, step),
                lambda kept, block: (kept, jnp.broadcast_to(block[None], (columns, *block.shape))),
                kept,
                block,
            )
        else:
            half = lax.cond(layer == step - 1, gather, lambda blocks: blocks, spread)
            if step in open_hops:
                product, block = solve(step, held(step), hop(step, half, straight))
            else:
                product, block = lax.cond(
                    takes_part,
                    functools.partial(even_step, step),
                    lambda kept, half, block: (kept, block),
                    kept,
                    half,
                    block,
                )
        kept = jnp.where(layer == step, product, kept)

    def planes_of(first, last, pairs):
        back = [(high, low) for low, high in pairs]
        return lax.ppermute(last, "layer", pairs), lax.ppermute(first, "layer", back)

    first, last = pack_planes(residual, wavenumber)
    pairs = [(i, i + 1) for i in range(layers - 1) if i != 1]
    below, above = planes_of(first, last, pairs)
    late_below, late_above = planes_of(first, last, [(1, 2)])
    below = jnp.where(layer == 2, late_below, below)
    above = jnp.where(layer == 1, late_above, above)
    first, last = pack_rows(residual, wavenumber, below, above)
    row_low, row_high = both_ways(first, last, "row")
    smoothed = smooth(inside, residual, wavenumber, row_low, row_high, below, above)

    step = layers - 1

    def finish(block, smoothed, kept):
        own = held(step)
        both = to_odd(step, block)
        return lift(smoothed, kept, step, own, both)

    return lax.cond(
        layer >= step - 1, finish, lambda block, smoothed, kept: lift(smoothed, kept), block, smoothed, kept
    )


def solution(mesh):
    return jax.shard_map(
        every_layer,
        mesh=mesh,
        in_specs=(
            P(None, None, "layer", "row", None),
            P("layer", "row", None),
            P(None, "layer", "row", None),
        ),
        out_specs=P(None, None, "layer", "row", None),
        check_vma=False,
    )
```

```python
import functools

import jax
import jax.numpy as jnp
from jax import lax
from jax.experimental import pallas as pl
from jax.experimental.pallas import tpu as pltpu
from jax.sharding import PartitionSpec as P


QY = 16
PX = 4
SWEEPS = 4
HALO = SWEEPS - 1
ROWS = 8
SENT = 4
LANES = 256

damping = 0.8
absorb = 0.5
coupling = 0.45

VMEM = pltpu.VMEM
f32 = jnp.float32
bf16 = jnp.bfloat16


def limit(mebibytes):
    return pltpu.CompilerParams(vmem_limit_bytes=mebibytes << 20)


def membership(fine, coarse):
    row = lax.broadcasted_iota(jnp.int32, (fine, coarse), 0)
    col = lax.broadcasted_iota(jnp.int32, (fine, coarse), 1)
    return jnp.where((row >= col * PX) & (row < col * PX + PX), 1.0, 0.0).astype(bf16)


def exact_dot(values, selection, contract):
    first = values.astype(bf16)
    rest = values - first.astype(f32)
    second = rest.astype(bf16)
    third = (rest - second.astype(f32)).astype(bf16)
    total = None
    for piece in (third, second, first):
        part = lax.dot_general(piece, selection, (((1,), (contract,)), ((), ())), preferred_element_type=f32)
        total = part if total is None else total + part
    return total


def restrict_kernel(residual, rhs, spread):
    shots, _, depth, height, width = residual.shape
    strips, across = height // QY, width // PX
    sums = []
    for strip in range(strips):
        for part in range(2):
            for shot in range(shots):
                total = residual[shot, part, 0, strip * QY : (strip + 1) * QY, :]
                for plane in range(1, depth):
                    total = total + residual[shot, part, plane, strip * QY : (strip + 1) * QY, :]
                sums.append(jnp.sum(total, axis=0, keepdims=True))
    means = exact_dot(jnp.concatenate(sums, axis=0), membership(width, across), 0) * (1.0 / (depth * QY * PX))
    lines = 2 * shots
    for strip in range(strips):
        rhs[:, strip * across : (strip + 1) * across] = means[strip * lines : (strip + 1) * lines, :]
    vector = rhs[...].astype(bf16)
    for device in range(spread.shape[0]):
        spread[device] = vector


def restrict(residual, devices):
    shots, _, _, height, width = residual.shape
    cells = (height // QY) * (width // PX)
    return pl.pallas_call(
        restrict_kernel,
        out_shape=(
            jax.ShapeDtypeStruct((2 * shots, cells), f32),
            jax.ShapeDtypeStruct((devices, 2 * shots, cells), bf16),
        ),
        compiler_params=limit(8),
        name="restrict",
    )(residual)


def hold_kernel(step, matrix, held, arrived):
    @pl.when(lax.axis_index("layer") == step)
    def _():
        copy = pltpu.make_async_copy(matrix, held, arrived)
        copy.start()
        copy.wait()


def hold(step, matrix):
    return pl.pallas_call(
        functools.partial(hold_kernel, step),
        out_shape=pltpu.VMEM(matrix.shape, matrix.dtype),
        in_specs=[pl.BlockSpec(memory_space=pltpu.HBM)],
        out_specs=pl.BlockSpec(memory_space=VMEM),
        scratch_shapes=[pltpu.SemaphoreType.DMA],
        compiler_params=limit(1),
        name="hold",
    )(matrix)


def ordered(vector, pairs):
    first_end = lax.axis_index("row") % 2 == 0
    for column, (own, far) in enumerate(pairs):
        cells = own.shape[-1]
        at = 2 * column * cells
        vector[:, at : at + cells] = jnp.where(first_end, own, far)
        vector[:, at + cells : at + 2 * cells] = jnp.where(first_end, far, own)


def halves(both):
    lines = both.shape[1] // 2
    return [(both[column, :lines], both[column, lines:]) for column in range(both.shape[0])]


def combined(by_re, by_im):
    shots = by_re.shape[0] // 2
    return jnp.concatenate([by_re[:shots] - by_im[shots:], by_re[shots:] + by_im[:shots]], axis=0)


def handed_on(solved, next_rhs):
    return (next_rhs[...] + coupling * solved).astype(bf16)


def times(part, rows):
    return lax.dot_general(part, rows, (((1,), (1,)), ((), ())), preferred_element_type=f32)


def first_kernel(matrix, gathered, next_rhs, kept, block, held, vector, arrived):
    devices, _, cells = gathered.shape
    pieces = arrived.shape[0]
    across = matrix.shape[2] // pieces
    columns = [slice(piece * across, (piece + 1) * across) for piece in range(pieces)]

    @pl.when(lax.axis_index("layer") == 0)
    def _():
        copies = [
            pltpu.make_async_copy(matrix.at[:, :, columns[piece]], held.at[:, :, columns[piece]], arrived.at[piece])
            for piece in range(pieces)
        ]
        for copy in copies:
            copy.start()
        for device in range(devices):
            vector[:, device * cells : (device + 1) * cells] = gathered[device]
        by = [None, None]
        for piece in range(pieces):
            part = vector[:, columns[piece]]
            copies[piece].wait()
            for side in range(2):
                product = times(part, held[side, :, columns[piece]])
                by[side] = product if by[side] is None else by[side] + product
        solved = combined(by[0], by[1])
        kept[...] = solved
        block[...] = handed_on(solved, next_rhs)


def solve_first(matrix, gathered, next_rhs):
    devices, lines, cells = gathered.shape
    pieces = 6
    return pl.pallas_call(
        first_kernel,
        out_shape=(
            jax.ShapeDtypeStruct((lines, cells), f32),
            jax.ShapeDtypeStruct((lines, cells), bf16),
        ),
        in_specs=[pl.BlockSpec(memory_space=pltpu.HBM)] + [pl.BlockSpec(memory_space=VMEM)] * 2,
        scratch_shapes=[
            pltpu.VMEM(matrix.shape, bf16),
            pltpu.VMEM((lines, devices * cells), bf16),
            pltpu.SemaphoreType.DMA((pieces,)),
        ],
        compiler_params=limit(8),
        cost_estimate=pl.CostEstimate(flops=4 * matrix.size, bytes_accessed=2 * matrix.size, transcendentals=0),
        name="solve_first",
    )(matrix, gathered, next_rhs)


def pair_up_kernel(near, far, spread):
    lines = near.shape[0]
    for column in range(spread.shape[0]):
        spread[column, :lines] = near[...]
        spread[column, lines:] = far[...]


def pair_up(near, far, columns):
    lines, cells = near.shape
    return pl.pallas_call(
        pair_up_kernel,
        out_shape=jax.ShapeDtypeStruct((columns, 2 * lines, cells), bf16),
        compiler_params=limit(2),
        name="pair_up",
    )(near, far)


def odd_kernel(matrix, both, next_rhs, product, spread, vector):
    ordered(vector, halves(both))
    full = vector[...]
    solved = combined(times(full, matrix[0]), times(full, matrix[1]))
    product[...] = solved
    block = handed_on(solved, next_rhs)
    for column in range(spread.shape[0]):
        spread[column] = block


def even_kernel(matrix, same, other, next_rhs, product, block, vector):
    ordered(vector, [(same[column], other[column]) for column in range(same.shape[0])])
    full = vector[...]
    solved = combined(times(full, matrix[0]), times(full, matrix[1]))
    product[...] = solved
    block[...] = handed_on(solved, next_rhs)


def solve_layer(step, matrix, blocks, next_rhs):
    lines, cells = next_rhs.shape
    columns = blocks[0].shape[0]
    out = (columns, lines, cells) if step % 2 else (lines, cells)
    return pl.pallas_call(
        odd_kernel if step % 2 else even_kernel,
        out_shape=(jax.ShapeDtypeStruct((lines, cells), f32), jax.ShapeDtypeStruct(out, bf16)),
        in_specs=[pl.BlockSpec(memory_space=VMEM)] * (2 + len(blocks)),
        scratch_shapes=[pltpu.VMEM((lines, 2 * columns * cells), bf16)],
        compiler_params=limit(3),
        cost_estimate=pl.CostEstimate(flops=4 * matrix.size, bytes_accessed=2 * matrix.size, transcendentals=0),
        name="solve_layer",
    )(matrix, *blocks, next_rhs)


def smooth_kernel(inside, residual, wavenumber, row_low, row_high, deep_low, deep_high, smoothed, gain, source, first, second):
    shots, _, depth, height, width = residual.shape
    top = ROWS
    start = top + ROWS
    total = height + 2 * ROWS
    planes = depth + 2 * HALO
    rest = LANES - width
    sides = (
        (0, HALO, deep_low, inside[0]),
        (HALO + depth, HALO, deep_high, inside[1]),
    )

    def gains(values, factor):
        real_part = 6.0 - values
        imag_part = -absorb * values
        scale = damping * factor / (real_part * real_part + imag_part * imag_part)
        return real_part * scale, -imag_part * scale

    def put_gain(plane, row, values, factor):
        real_part, imag_part = gains(values, factor)
        rows = values.shape[0]
        gain[0, plane, pl.ds(row, rows), 0:width] = real_part
        gain[1, plane, pl.ds(row, rows), 0:width] = imag_part

    blank = jnp.zeros((total, rest), f32)

    def clear(plane, _):
        for part in range(2):
            gain[part, plane, top : top + total, width:LANES] = blank
            source[part, plane, top : top + total, width:LANES] = blank
        return _

    lax.fori_loop(0, planes, clear, 0)

    def own_gain(plane, _):
        for row in range(0, height, 16):
            put_gain(HALO + plane, start + row, wavenumber[plane, row : row + 16, :], 1.0)
        return _

    lax.fori_loop(0, depth, own_gain, 0)
    for base, count, ghost, factor in sides:
        for plane in range(count):
            for row in range(0, height, 16):
                put_gain(base + plane, start + row, ghost[2 * shots, plane, row : row + 16, :].astype(f32), factor)
    for base, count, factor in ((0, HALO, inside[0]), (HALO, depth, 1.0), (HALO + depth, HALO, inside[1])):

        def row_gain(plane, _, factor=factor):
            put_gain(plane, start - SENT, row_low[2 * shots, plane].astype(f32), factor * inside[2])
            put_gain(plane, start + height, row_high[2 * shots, plane].astype(f32), factor * inside[3])
            return _

        lax.fori_loop(base, base + count, row_gain, 0)

    def sweep(old, plane, row, rows, store):
        here = pl.ds(row, rows)
        terms = []
        for part in range(2):
            centre = old[part, plane, here, :]
            beside = old[part, plane - 1, here, :] + old[part, plane + 1, here, :]
            beside = beside + old[part, plane, pl.ds(row - 1, rows), :] + old[part, plane, pl.ds(row + 1, rows), :]
            beside = beside + pltpu.roll(centre, 1, 1) + pltpu.roll(centre, LANES - 1, 1)
            terms.append((centre, source[part, plane, here, :] + beside))
        (centre_re, sum_re), (centre_im, sum_im) = terms
        gain_re, gain_im = gain[0, plane, here, :], gain[1, plane, here, :]
        store(0, (1.0 - damping) * centre_re + (gain_re * sum_re - gain_im * sum_im))
        store(1, (1.0 - damping) * centre_im + (gain_re * sum_im + gain_im * sum_re))

    for shot in range(shots):

        def own_source(plane, _):
            for part in range(2):
                source[part, HALO + plane, start : start + height, 0:width] = residual[shot, part, plane]
            return _

        def row_source(plane, _):
            for part in range(2):
                source[part, plane, start - SENT : start, 0:width] = row_low[2 * shot + part, plane].astype(f32)
                source[part, plane, start + height : start + height + SENT, 0:width] = row_high[
                    2 * shot + part, plane
                ].astype(f32)
            return _

        lax.fori_loop(0, depth, own_source, 0)
        lax.fori_loop(0, planes, row_source, 0)
        for base, count, ghost, _ in sides:
            for plane in range(count):
                for part in range(2):
                    source[part, base + plane, start : start + height, 0:width] = ghost[2 * shot + part, plane].astype(f32)

        def begin(plane, _):
            for row in range(top, top + total, 16):
                here = pl.ds(row, 16)
                gain_re, gain_im = gain[0, plane, here, :], gain[1, plane, here, :]
                source_re, source_im = source[0, plane, here, :], source[1, plane, here, :]
                first[0, plane, here, :] = gain_re * source_re - gain_im * source_im
                first[1, plane, here, :] = gain_re * source_im + gain_im * source_re
            return _

        lax.fori_loop(0, planes, begin, 0)
        old, new = first, second
        for counter in range(1, SWEEPS):
            last = counter == SWEEPS - 1

            def one_plane(plane, _, old=old, new=new, last=last, shot=shot):
                low, high = (start, start + height) if last else (top, top + total)
                for row in range(low, high, 16):

                    def store(part, value, row=row):
                        if last:
                            smoothed[shot, part, plane - HALO, row - start : row - start + 16, :] = value[:, :width]
                        else:
                            new[part, plane, pl.ds(row, 16), :] = value

                    sweep(old, plane, row, 16, store)
                return _

            lax.fori_loop(counter, planes - counter, one_plane, 0)
            old, new = new, old


def smooth(inside, residual, wavenumber, row_low, row_high, deep_low, deep_high):
    shots, _, depth, height, width = residual.shape
    scratch = pltpu.VMEM((2, depth + 2 * HALO, height + 4 * ROWS, LANES), f32)
    return pl.pallas_call(
        smooth_kernel,
        out_shape=jax.ShapeDtypeStruct(residual.shape, f32),
        in_specs=[pl.BlockSpec(memory_space=pltpu.SMEM)] + [pl.BlockSpec(memory_space=VMEM)] * 6,
        scratch_shapes=[scratch] * 4,
        cost_estimate=pl.CostEstimate(flops=300 * residual.size, bytes_accessed=12 * residual.size, transcendentals=0),
        compiler_params=limit(28),
        name="smooth",
    )(inside, residual, wavenumber, row_low, row_high, deep_low, deep_high)


def lifted(smoothed, values, out, fine, wide, left):
    shots, _, depth, height, width = smoothed.shape
    strips, across = height // QY, width // PX
    blocks = [(shot, part) for part in range(2) for shot in range(shots)]
    goes = [pltpu.make_async_copy(fine.at[at], out.at[block], left.at[at]) for at, block in enumerate(blocks)]
    lines = [values[:, strip * across : (strip + 1) * across] for strip in range(strips)]
    wide[...] = exact_dot(jnp.concatenate(lines, axis=0), membership(width, across), 1)
    for at, (shot, part) in enumerate(blocks):
        for strip in range(strips):
            line = strip * 2 * shots + at
            value = jnp.broadcast_to(wide[line : line + 1, :], (QY, width))
            for plane in range(depth):
                rows = slice(strip * QY, (strip + 1) * QY)
                fine[at, plane, rows, :] = smoothed[shot, part, plane, rows, :] + value
        goes[at].start()
    for copy in goes:
        copy.wait()


def lift_kernel(smoothed, coarse, out, fine, wide, left):
    lifted(smoothed, coarse[...], out, fine, wide, left)


def last_kernel(step, smoothed, kept_before, matrix, both, out, fine, wide, left, vector, coarse):
    coarse[...] = kept_before[...]

    @pl.when(lax.axis_index("layer") == step)
    def _():
        ordered(vector, halves(both))
        full = vector[...]
        coarse[...] = combined(times(full, matrix[0]), times(full, matrix[1]))

    lifted(smoothed, coarse[...], out, fine, wide, left)


def lift(smoothed, kept, step=None, *operands):
    shots, _, depth, height, width = smoothed.shape
    lines, cells = kept.shape
    scratch = [
        pltpu.VMEM((2 * shots, depth, height, width), f32),
        pltpu.VMEM((height // QY * lines, width), f32),
        pltpu.SemaphoreType.DMA((2 * shots,)),
    ]
    kernel = lift_kernel
    if operands:
        columns = operands[1].shape[0]
        kernel = functools.partial(last_kernel, step)
        scratch += [pltpu.VMEM((lines, 2 * columns * cells), bf16), pltpu.VMEM((lines, cells), f32)]
    return pl.pallas_call(
        kernel,
        out_shape=pltpu.HBM(smoothed.shape, f32),
        in_specs=[pl.BlockSpec(memory_space=VMEM)] * (2 + len(operands)),
        out_specs=pl.BlockSpec(memory_space=pltpu.HBM),
        scratch_shapes=scratch,
        compiler_params=limit(6),
        name="lift",
    )(smoothed, kept, *operands)


def pack_planes_kernel(residual, wavenumber, first, last):
    shots, _, depth, height, width = residual.shape
    for out, base in ((first, 0), (last, depth - HALO)):
        for plane in range(HALO):
            for shot in range(shots):
                for part in range(2):
                    out[2 * shot + part, plane] = residual[shot, part, base + plane].astype(bf16)
            out[2 * shots, plane] = wavenumber[base + plane].astype(bf16)


def pack_planes(residual, wavenumber):
    shots, _, _, height, width = residual.shape
    shape = jax.ShapeDtypeStruct((2 * shots + 1, HALO, height, width), bf16)
    return pl.pallas_call(
        pack_planes_kernel, out_shape=(shape, shape), compiler_params=limit(10), name="pack_planes"
    )(residual, wavenumber)


def pack_rows_kernel(residual, wavenumber, below, above, first, last):
    shots, _, depth, height, width = residual.shape
    for out, base in ((first, 0), (last, height - SENT)):
        rows = slice(base, base + SENT)
        for field in range(2 * shots + 1):
            for plane in range(HALO):
                out[field, plane] = below[field, plane, rows, :]
                out[field, HALO + depth + plane] = above[field, plane, rows, :]
            for plane in range(depth):
                own = wavenumber[plane, rows, :] if field == 2 * shots else residual[field // 2, field % 2, plane, rows, :]
                out[field, HALO + plane] = own.astype(bf16)


def pack_rows(residual, wavenumber, below, above):
    shots, _, depth, _, width = residual.shape
    shape = jax.ShapeDtypeStruct((2 * shots + 1, depth + 2 * HALO, SENT, width), bf16)
    return pl.pallas_call(
        pack_rows_kernel, out_shape=(shape, shape), compiler_params=limit(10), name="pack_rows"
    )(residual, wavenumber, below, above)


def both_ways(low_block, high_block, axis):
    size = lax.axis_size(axis)
    up = [(i, i + 1) for i in range(size - 1)]
    return lax.ppermute(high_block, axis, up), lax.ppermute(low_block, axis, [(b, a) for a, b in up])


def every_layer(residual, wavenumber, inverse):
    layers, devices = lax.axis_size("layer"), lax.axis_size("row")
    layer, row = lax.axis_index("layer"), lax.axis_index("row")
    inside = jnp.stack([layer > 0, layer < layers - 1, row > 0, row < devices - 1]).astype(f32)

    rhs, spread = restrict(residual, devices)
    flipped = lax.ppermute(rhs, "layer", [(i, i ^ 1) for i in range(layers)])
    matrix = pltpu.with_memory_space_constraint(inverse[:, 0], pltpu.HBM)
    gathered = lax.cond(
        layer == 0,
        lambda blocks: lax.all_to_all(blocks, "row", 0, 0, tiled=True),
        lambda blocks: blocks,
        spread,
    )
    above_rhs = lax.cond(
        layer == 0,
        lambda rhs: rhs,
        lambda rhs: lax.ppermute(rhs, "layer", [(i + 1, i) for i in range(1, layers - 1, 2)]),
        rhs,
    )
    next_rhs = jnp.where((layer & 1) == 0, flipped, above_rhs)
    kept, block = solve_first(matrix, gathered, next_rhs)

    columns = devices // 2
    ends = [[2 * column + end for column in range(columns)] for end in range(2)]

    def gather(blocks):
        return lax.all_to_all(blocks, "row", 0, 0, axis_index_groups=ends, tiled=True)

    def hop(step, sent, way):
        found = []
        for flip in (1, 0):
            found.append(lax.ppermute(sent, ("layer", "row"), way(step, flip)))
        return found[1], found[0]

    def swapped(step, flip):
        return [
            (i * devices + j, (i ^ (step - 1) ^ step) * devices + (j ^ flip))
            for i in range(layers)
            for j in range(devices)
        ]

    def straight(step, flip):
        return [((step - 1) * devices + j, step * devices + (j ^ flip)) for j in range(devices)]

    def held(step):
        return hold(step, matrix)

    def solve(step, own, blocks):
        return tuple(solve_layer(step, own, blocks, next_rhs))

    def to_odd(step, block):
        near, far = hop(step, block, swapped)
        return gather(pair_up(near, far, columns))

    def odd_step(step, kept, block):
        own = held(step)
        return solve(step, own, [to_odd(step, block)])

    def even_step(step, kept, half, block):
        own = held(step)
        return solve(step, own, hop(step, half, swapped))

    open_hops = (2, layers // 2)
    for step in range(1, layers - 1):
        takes_part = (layer == step - 1) | (layer == step)
        if step % 2:
            product, spread = lax.cond(
                takes_part,
                functools.partial(odd_step, step),
                lambda kept, block: (kept, jnp.broadcast_to(block[None], (columns, *block.shape))),
                kept,
                block,
            )
        else:
            half = lax.cond(layer == step - 1, gather, lambda blocks: blocks, spread)
            if step in open_hops:
                product, block = solve(step, held(step), hop(step, half, straight))
            else:
                product, block = lax.cond(
                    takes_part,
                    functools.partial(even_step, step),
                    lambda kept, half, block: (kept, block),
                    kept,
                    half,
                    block,
                )
        kept = jnp.where(layer == step, product, kept)

    def planes_of(first, last, pairs):
        back = [(high, low) for low, high in pairs]
        return lax.ppermute(last, "layer", pairs), lax.ppermute(first, "layer", back)

    first, last = pack_planes(residual, wavenumber)
    pairs = [(i, i + 1) for i in range(layers - 1) if i != 1]
    below, above = planes_of(first, last, pairs)
    late_below, late_above = planes_of(first, last, [(1, 2)])
    below = jnp.where(layer == 2, late_below, below)
    above = jnp.where(layer == 1, late_above, above)
    first, last = pack_rows(residual, wavenumber, below, above)
    row_low, row_high = both_ways(first, last, "row")
    smoothed = smooth(inside, residual, wavenumber, row_low, row_high, below, above)

    step = layers - 1

    def finish(block, smoothed, kept):
        own = held(step)
        both = to_odd(step, block)
        return lift(smoothed, kept, step, own, both)

    return lax.cond(
        layer >= step - 1, finish, lambda block, smoothed, kept: lift(smoothed, kept), block, smoothed, kept
    )


def solution(mesh):
    return jax.shard_map(
        every_layer,
        mesh=mesh,
        in_specs=(
            P(None, None, "layer", "row", None),
            P("layer", "row", None),
            P(None, "layer", "row", None),
        ),
        out_specs=P(None, None, "layer", "row", None),
        check_vma=False,
    )
```
